512 devices in a mesh: ctx: 64 (over y, z), tp: 8 (over x, core).
Axes of the slice: x: 4, y: 8, z: 8, core: 2. Of those that a mesh axis runs over, the one named last changes fastest.
Arguments:
- inputs: bfloat16 [8192, 4096], P('ctx', 'tp'), may hold values from -6 to 6
- gate_in: bfloat16 [8192, 4096], P('ctx', 'tp'), may hold values from -6 to 6
- b_proj: bfloat16 [8192, 128], P('ctx'), may hold values from -0.5 to 0.5
- c_proj: bfloat16 [8192, 128], P('ctx'), may hold values from -0.5 to 0.5
- log_decay: float32 [32, 8192], P('tp', 'ctx'), may hold values from -0.75 to 0
- w_out: bfloat16 [4096, 4096], P('tp'), may hold values from -0.09375 to 0.09375
- cotangent: bfloat16 [8192, 4096], P(('ctx', 'tp')), may hold values from -6 to 6
Outputs:
- layer_out: bfloat16 [8192, 4096], P(('ctx', 'tp'))
- grad_inputs: bfloat16 [8192, 4096], P('ctx', 'tp')
- grad_gate: bfloat16 [8192, 4096], P('ctx', 'tp')
- grad_b: float32 [8192, 128], P(('ctx', 'tp'))
- grad_c: float32 [8192, 128], P(('ctx', 'tp'))
- grad_decay: float32 [32, 8192], P('tp', 'ctx')
The draws below stay inside these ranges and needn't reach their ends.
All inputs are finite; a program needn't handle non-finite values.
Results may differ from the reference program's by a relative error of at most 0.017.
Values may be sent and summed in bfloat16 or wider, within the bound.
No kernel may reach another device: no remote copies, remote signals or barrier semaphores. Data moves between devices by JAX's collectives and lax.ppermute only.
A program may use at most 128 MiB of HBM per device.

```python
import jax
import jax.numpy as jnp
from jax import lax

D = 4096
P_SIZE = 128
NSTATE = 128
BLOCK = 128
TOK_DEV = 128
HEAD_TOTAL = 32
TOKEN_POSITIONS = 8192
N_TP = 8


def draw_log_decay(key, part):
    random_split_keys = jax.random.split(key, 7)
    ranking = jax.random.permutation(random_split_keys[0], HEAD_TOTAL)
    fast_count = HEAD_TOTAL // 2
    is_fast = ranking < fast_count
    fast_rate = jnp.exp(jax.random.uniform(random_split_keys[1], (HEAD_TOTAL,), jnp.float32, jnp.log(1.0 / 50.0), jnp.log(1.0 / 30.0)))
    slow_rate = jax.random.uniform(random_split_keys[2], (HEAD_TOTAL,), jnp.float32, 0.5, 1.0) * (0.5 / TOKEN_POSITIONS)
    baseline_rate = jnp.where(is_fast, fast_rate, slow_rate)
    block_count = TOKEN_POSITIONS // TOK_DEV
    block_multiplier = jnp.repeat(jax.random.uniform(random_split_keys[3], (HEAD_TOTAL, block_count), jnp.float32, 0.5, 1.0), TOK_DEV, axis=1)
    token_multiplier = jax.random.uniform(random_split_keys[4], (HEAD_TOTAL, TOKEN_POSITIONS), jnp.float32, 0.5, 1.5)
    spike_locations = jax.random.randint(random_split_keys[5], (2,), 0, TOKEN_POSITIONS)
    spike_flags = jnp.any(jnp.arange(TOKEN_POSITIONS)[None, :] == spike_locations[:, None], axis=0)
    spike_loss_value = jax.random.uniform(random_split_keys[6], (HEAD_TOTAL, TOKEN_POSITIONS), jnp.float32, 0.2, 0.5)
    return -baseline_rate[:, None] * block_multiplier * token_multiplier + jnp.where(spike_flags[None, :], jnp.log1p(-spike_loss_value), 0.0)


def shard_levels(own_key, shape, cuts, least, largest):
    def one(dim, parts):
        heights = jax.random.uniform(jax.random.fold_in(jax.random.fold_in(own_key, 6), dim), (parts,), jnp.float32, least / len(cuts), largest / len(cuts))
        return jnp.repeat(jnp.exp(heights), shape[dim] // parts).reshape((-1,) + (1,) * (len(shape) - dim - 1))

    loudness = one(*cuts[0])
    for cut in cuts[1:]:
        loudness = loudness * one(*cut)
    return loudness


def scatter_about(stream_key, dims, width, bound, shards=(), kind=jnp.bfloat16):
    gain = shard_levels(stream_key, dims, shards, -0.22, 0.18) if shards else 1.0
    values = jax.random.normal(stream_key, dims, jnp.float32) * width * gain
    return jnp.minimum(jnp.maximum(values, -bound), bound).astype(kind)


def setup_inputs(seed: int = 0) -> dict:
    arg_keys = jax.random.split(jax.random.key(seed), 8)
    return {
        "inputs": scatter_about(arg_keys[0], (TOKEN_POSITIONS, HEAD_TOTAL * P_SIZE), 1.0, 6.0, ((0, 64), (1, 8))),
        "gate_in": scatter_about(arg_keys[1], (TOKEN_POSITIONS, HEAD_TOTAL * P_SIZE), 1.0, 6.0, ((0, 64), (1, 8))),
        "b_proj": scatter_about(arg_keys[2], (TOKEN_POSITIONS, NSTATE), 0.08, 0.5, ((0, 64),)),
        "c_proj": scatter_about(arg_keys[3], (TOKEN_POSITIONS, NSTATE), 0.08, 0.5, ((0, 64),)),
        "log_decay": draw_log_decay(jax.random.fold_in(arg_keys[7], 71), 0),
        "w_out": scatter_about(arg_keys[5], (HEAD_TOTAL * P_SIZE, D), (HEAD_TOTAL * P_SIZE) ** -0.5, 0.09375, ((0, 8),)),
        "cotangent": scatter_about(arg_keys[6], (TOKEN_POSITIONS, D), 1.0, 6.0, ((0, 512),)),
    }


def block_pieces(x_block, b_block, c_block, d_block):
    length = d_block.shape[0]
    cumulative = jnp.cumsum(d_block, axis=0)
    final_sum = cumulative[-1]
    tail_weight = jnp.exp(final_sum[None, :] - cumulative)
    column_cum = cumulative.T
    differ = column_cum[:, :, None] - column_cum[:, None, :]
    position = jnp.arange(length)
    causal = position[:, None] >= position[None, :]
    decay_mat = jnp.where(causal[None], jnp.exp(jnp.minimum(differ, 0.0)), 0.0)
    scores = jnp.dot(c_block, b_block.T, preferred_element_type=jnp.float32)
    mixing_b = (scores[None] * decay_mat).astype(jnp.bfloat16)
    y_intra = jnp.einsum('hqk,khp->qhp', mixing_b.astype(jnp.float32), x_block.astype(jnp.float32))
    weighted = (x_block.astype(jnp.float32) * tail_weight[:, :, None]).astype(jnp.bfloat16)
    block_state = jnp.einsum('qhp,qn->hpn', weighted.astype(jnp.float32), b_block.astype(jnp.float32))
    return cumulative, tail_weight, decay_mat, scores, mixing_b, y_intra, weighted, block_state, jnp.exp(final_sum)


def reference(inputs, gate_in, b_proj, c_proj, log_decay, w_out, cotangent):
    total_len, feature_width = inputs.shape
    head_count = log_decay.shape[0]
    head_dim = feature_width // head_count
    nblocks = total_len // BLOCK
    x_blocks = inputs.reshape(nblocks, BLOCK, head_count, head_dim)
    z_blocks = gate_in.reshape(nblocks, BLOCK, head_count, head_dim)
    b_blocks = b_proj.reshape(nblocks, BLOCK, -1)
    c_blocks = c_proj.reshape(nblocks, BLOCK, -1)
    d_blocks = log_decay.reshape(head_count, nblocks, BLOCK).transpose(1, 2, 0)

    def first_pass(packed):
        pieces = block_pieces(*packed)
        return pieces[7], pieces[8]

    block_state, block_decay = lax.map(first_pass, (x_blocks, b_blocks, c_blocks, d_blocks))
    zero_state = jnp.zeros(block_state.shape[1:], jnp.float32)

    def chain_step(running, packed):
        decay_step, term_block = packed
        return decay_step[:, None, None] * running + term_block, running

    unused, state_in = lax.scan(chain_step, zero_state, (block_decay, block_state))

    def second_pass(packed):
        x_block, b_block, c_block, d_block, z_block, s_block = packed
        pieces = block_pieces(x_block, b_block, c_block, d_block)
        state_b = s_block.astype(jnp.bfloat16)
        y_inter = jnp.einsum('qn,hpn->qhp', c_block.astype(jnp.float32), state_b.astype(jnp.float32)) * jnp.exp(pieces[0])[:, :, None]
        y_full = pieces[5] + y_inter
        gated_out = (y_full * jax.nn.silu(z_block.astype(jnp.float32))).astype(jnp.bfloat16)
        return gated_out.reshape(BLOCK, feature_width)

    gated_out = lax.map(second_pass, (x_blocks, b_blocks, c_blocks, d_blocks, z_blocks, state_in)).reshape(total_len, feature_width)
    group_cols = feature_width // N_TP

    def add_group(running_sum, group_index):
        columns = lax.dynamic_slice_in_dim(gated_out, group_index * group_cols, group_cols, 1)
        weight_rows = lax.dynamic_slice_in_dim(w_out, group_index * group_cols, group_cols, 0)
        partial_sum = jnp.dot(columns, weight_rows, preferred_element_type=jnp.float32).astype(jnp.bfloat16)
        partial_sum = lax.optimization_barrier(partial_sum)
        return running_sum + partial_sum.astype(jnp.float32), None

    summed, unused = lax.scan(add_group, jnp.zeros((total_len, w_out.shape[1]), jnp.float32), jnp.arange(N_TP, dtype=jnp.int32))
    layer_out = summed.astype(jnp.bfloat16)
    dgated = jnp.dot(cotangent, w_out.T, preferred_element_type=jnp.float32).reshape(nblocks, BLOCK, head_count, head_dim)

    def adjoint_source(packed):
        c_block, d_block, z_block, g_block = packed
        cumulative = jnp.cumsum(d_block, axis=0)
        grad_y = g_block * jax.nn.silu(z_block.astype(jnp.float32))
        grad_w = (grad_y * jnp.exp(cumulative)[:, :, None]).astype(jnp.bfloat16)
        return jnp.einsum('qhp,qn->hpn', grad_w.astype(jnp.float32), c_block.astype(jnp.float32))

    injected = lax.map(adjoint_source, (c_blocks, d_blocks, z_blocks, dgated))
    unused, adjoint_next = lax.scan(chain_step, zero_state, (block_decay, injected), reverse=True)

    def third_pass(packed):
        x_block, b_block, c_block, d_block, z_block, g_block, s_block, r_block = packed
        cumulative, tail_weight, decay_mat, scores, mixing_b, y_intra, weighted, unused_state, block_dec = block_pieces(x_block, b_block, c_block, d_block)
        state_b = s_block.astype(jnp.bfloat16)
        adjoint_b = r_block.astype(jnp.bfloat16)
        y_inter = jnp.einsum('qn,hpn->qhp', c_block.astype(jnp.float32), state_b.astype(jnp.float32)) * jnp.exp(cumulative)[:, :, None]
        y_full = y_intra + y_inter
        gate_float = z_block.astype(jnp.float32)
        sigmoid_z = jax.nn.sigmoid(gate_float)
        grad_gate = (g_block * y_full * (sigmoid_z + gate_float * sigmoid_z * (1.0 - sigmoid_z))).astype(jnp.bfloat16)
        grad_y = g_block * gate_float * sigmoid_z
        grad_y_b = grad_y.astype(jnp.bfloat16)
        grad_w = (grad_y * jnp.exp(cumulative)[:, :, None]).astype(jnp.bfloat16)
        pair_dots = jnp.einsum('qhp,khp->hqk', grad_y_b.astype(jnp.float32), x_block.astype(jnp.float32))
        dmix = pair_dots * decay_mat
        dmix_b = dmix.astype(jnp.bfloat16).astype(jnp.float32)
        state_dx = jnp.einsum('kn,hpn->khp', b_block.astype(jnp.float32), adjoint_b.astype(jnp.float32)) * tail_weight[:, :, None]
        grad_inputs = (jnp.einsum('hqk,qhp->khp', mixing_b.astype(jnp.float32), grad_y_b.astype(jnp.float32)) + state_dx).astype(jnp.bfloat16)
        grad_b = jnp.einsum('hqk,qn->kn', dmix_b, c_block.astype(jnp.float32)) + jnp.einsum('khp,hpn->kn', weighted.astype(jnp.float32), adjoint_b.astype(jnp.float32))
        grad_c = jnp.einsum('hqk,kn->qn', dmix_b, b_block.astype(jnp.float32)) + jnp.einsum('qhp,hpn->qn', grad_w.astype(jnp.float32), state_b.astype(jnp.float32))
        cross_terms = dmix * scores[None]
        decay_flow = (jnp.sum(cross_terms, 2) - jnp.sum(cross_terms, 1)).T
        outflow = jnp.sum(x_block.astype(jnp.float32) * state_dx, 2)
        decay_flow = decay_flow + jnp.sum(grad_y * y_inter, 2) - outflow
        closing = jnp.sum(outflow, 0) + block_dec * jnp.sum(r_block * s_block, (1, 2))
        decay_flow = decay_flow.at[-1].add(closing)
        grad_decay = jnp.flip(jnp.cumsum(jnp.flip(decay_flow, 0), 0), 0)
        return grad_inputs.reshape(BLOCK, feature_width), grad_gate.reshape(BLOCK, feature_width), grad_b, grad_c, grad_decay.T

    results = lax.map(third_pass, (x_blocks, b_blocks, c_blocks, d_blocks, z_blocks, dgated, state_in, adjoint_next))
    grad_inputs = results[0].reshape(total_len, feature_width)
    grad_gate = results[1].reshape(total_len, feature_width)
    grad_b = results[2].reshape(total_len, -1)
    grad_c = results[3].reshape(total_len, -1)
    grad_decay = results[4].transpose(1, 0, 2).reshape(head_count, total_len)
    return layer_out, grad_inputs, grad_gate, grad_b, grad_c, grad_decay
```

```python
import functools

import jax
import jax.numpy as jnp
from jax import lax
from jax.experimental import pallas as pl
from jax.experimental.pallas import tpu as pltpu
from jax.sharding import PartitionSpec as P

BF = jnp.bfloat16
F32 = jnp.float32
NT = (((1,), (1,)), ((), ()))
VMEM_LIMIT = 48 * 1024 * 1024


def mm(a, b):
    return jnp.dot(a, b, preferred_element_type=F32)


def mm_nt(a, b):
    return lax.dot_general(a, b, NT, preferred_element_type=F32)


def flip(a):
    return jnp.transpose(a.astype(F32)).astype(BF)


def split(a):
    hi = a.astype(BF)
    rest = a - hi.astype(F32)
    mid = rest.astype(BF)
    return hi, mid, (rest - mid.astype(F32)).astype(BF)


def sum_by(a, ones):
    hi, mid, lo = split(a)
    return mm(hi, ones) + (mm(mid, ones) + mm(lo, ones))


def grid_of(size):
    return (
        lax.broadcasted_iota(jnp.int32, (size, size), 0),
        lax.broadcasted_iota(jnp.int32, (size, size), 1),
    )


def pre_kernel(heads, x_ref, gate_ref, b_ref, c_ref, ld_ref,
               st_ref, dec_ref, mask_ref, mixt_ref, scores_ref, yi_ref, ec_ref, tail_ref,
               wx_ref, silu_ref, slope_ref):
    size = x_ref.shape[0]
    width = x_ref.shape[1] // heads
    row, col = grid_of(size)
    ld = jnp.concatenate([ld_ref[...], jnp.zeros((8 - heads, size), F32)], axis=0)
    cum = sum_by(ld, (row <= col).astype(BF))
    scores = mm_nt(c_ref[...], b_ref[...])
    scores_ref[...] = scores
    b_t = flip(b_ref[...])
    for h in range(heads):
        at = slice(h * width, (h + 1) * width)
        across = jnp.broadcast_to(cum[h:h + 1, :], (size, size))
        down = jnp.transpose(across)
        mask = jnp.where(row >= col, jnp.exp(jnp.minimum(down - across, 0.0)), 0.0)
        mask_ref[h] = mask
        mixing = scores * mask
        mixt_ref[h] = jnp.transpose(mixing).astype(BF)
        x = x_ref[:, at]
        yi_ref[:, at] = mm(mixing.astype(BF), x)
        last = cum[h:h + 1, size - 1:size]
        ec_ref[:, at] = jnp.exp(down)
        tail = jnp.exp(last - down)
        tail_ref[:, at] = tail
        wx = (x.astype(F32) * tail).astype(BF)
        wx_ref[:, at] = wx
        st_ref[:, at] = mm(b_t, wx)
        decay = jnp.broadcast_to(jnp.exp(last), (8, size))
        hi = decay.astype(BF).astype(F32)
        lo = decay - hi
        dec_ref[h] = jnp.where(lax.broadcasted_iota(jnp.int32, (8, size), 0) < 4, hi, lo)
    v = gate_ref[...].astype(F32)
    g = 1.0 / (1.0 + jnp.exp(-v))
    silu_ref[...] = v * g
    slope_ref[...] = g + v * g * (1.0 - g)


def mid_kernel(heads, piece, near_ref, far_ref, w_ref, c_ref, silu_ref, ec_ref, st_ref, dec_ref,
               msg_ref, dg_ref):
    size = st_ref.shape[0]
    width = st_ref.shape[1] // heads
    me = lax.axis_index("tp")
    core = me % 2
    chip = me // 2
    w = w_ref[...]
    near = mm_nt(near_ref[...], w)
    far = mm_nt(far_ref[...], w)
    chips = near_ref.shape[0] // piece
    for s in range(chips):
        rows = slice(s * piece, (s + 1) * piece)
        src = 2 * ((chip + chips - s) % chips)
        dg_ref[pl.ds(pl.multiple_of(piece * (src + core), piece), piece), :] = near[rows, :]
        dg_ref[pl.ds(pl.multiple_of(piece * (src + 1 - core), piece), piece), :] = far[rows, :]
    gw = (dg_ref[...] * silu_ref[...] * ec_ref[...]).astype(BF)
    inj = mm(flip(c_ref[...]), gw)
    for a in range(size // 8):
        for h in range(heads):
            j = a * heads + h
            at = slice(h * width, (h + 1) * width)
            both = jnp.concatenate([st_ref[8 * a:8 * a + 8, at], inj[8 * a:8 * a + 8, at]], axis=0)
            msg_ref[j, 0:16, :] = both.astype(BF)
            msg_ref[j, 16:24, :] = dec_ref[h].astype(BF)


def scan_kernel(msg_ref, out_ref, dec_ref, state_ref):
    count = msg_ref.shape[0]
    state = jnp.zeros((8, msg_ref.shape[2]), F32)
    for k in range(count):
        pair = msg_ref[k, 16:24, :].astype(F32)
        decay = pair + pltpu.roll(pair, 4, 0)
        dec_ref[k] = decay
        state_ref[k] = state
        state = decay * state + msg_ref[k, 0:8, :].astype(F32)
    adjoint = jnp.zeros((8, msg_ref.shape[2]), F32)
    for k in reversed(range(count)):
        out_ref[k] = jnp.concatenate([state_ref[k], adjoint], axis=0).astype(BF)
        adjoint = dec_ref[k] * adjoint + msg_ref[k, 8:16, :].astype(F32)


def fin_kernel(heads, back_ref, x_ref, b_ref, c_ref, w_ref, dg_ref, silu_ref, slope_ref, mask_ref,
               mixt_ref, scores_ref, yi_ref, ec_ref, tail_ref, wx_ref, dec_ref,
               part_ref, gi_ref, gg_ref, gd_ref, state_ref, adj_ref):
    size, full = x_ref.shape
    width = full // heads
    for a in range(size // 8):
        for h in range(heads):
            both = back_ref[a * heads + h].astype(F32)
            state_ref[8 * a:8 * a + 8, h * width:(h + 1) * width] = both[0:8]
            adj_ref[8 * a:8 * a + 8, h * width:(h + 1) * width] = both[8:16]
    state = state_ref[...]
    adj = adj_ref[...]
    state_b = state.astype(BF)
    adj_b = adj.astype(BF)
    x = x_ref[...]
    b = b_ref[...]
    c = c_ref[...]
    silu = silu_ref[...]
    dg = dg_ref[...]
    ec = ec_ref[...]
    y_inter = mm(c, state_b) * ec
    y = yi_ref[...] + y_inter
    gated = (y * silu).astype(BF)
    out_width = w_ref.shape[1]
    step = 512
    for o in range(0, out_width, step):
        part_ref[:, o:o + step] = mm(gated, w_ref[:, o:o + step]).astype(BF)
    gg_ref[...] = (dg * y * slope_ref[...]).astype(BF)
    gy = dg * silu
    gy_b = gy.astype(BF)
    gw = (gy * ec).astype(BF)
    sdx = mm(b, adj_b) * tail_ref[...]
    through = x.astype(F32) * sdx
    entering = gy * y_inter
    scores = scores_ref[...]
    row, col = grid_of(size)
    sub = lax.broadcasted_iota(jnp.int32, (8, size), 0)
    dmix_sum = jnp.zeros((size, size), F32)
    columns = jnp.zeros((size, size), F32)
    lines = jnp.zeros((8, size), F32)
    closing = jnp.zeros((8, size), F32)
    product = adj * state
    for h in range(heads):
        at = slice(h * width, (h + 1) * width)
        dmix = mm_nt(gy_b[:, at], x[:, at]) * mask_ref[h]
        dmix_sum = dmix_sum + dmix
        cross = dmix * scores
        gi_ref[:, at] = (mm(mixt_ref[h], gy_b[:, at]) + sdx[:, at]).astype(BF)
        down = jnp.sum(cross + entering[:, at] - through[:, at], axis=1, keepdims=True)
        columns = jnp.where(col == h, down, columns)
        lines = jnp.where(sub == h, jnp.sum(cross, axis=0, keepdims=True), lines)
        decay = jnp.max(dec_ref[h][0:1, 0:1] + dec_ref[h][4:5, 0:1], axis=1, keepdims=True)
        end = jnp.sum(jnp.sum(through[:, at], axis=0, keepdims=True), axis=1, keepdims=True)
        dots = jnp.sum(jnp.sum(product[:, at], axis=0, keepdims=True), axis=1, keepdims=True)
        closing = jnp.where(sub == h, end + decay * dots, closing)
    flow = jnp.transpose(columns)[0:8, :] - lines
    total = sum_by(flow, (row >= col).astype(BF)) + closing
    gd_ref[...] = total[0:heads, :]
    dmix_b = dmix_sum.astype(BF)
    n = b.shape[1]
    part_ref[:, out_width:out_width + n] = (
        mm(jnp.transpose(dmix_sum).astype(BF), c) + mm_nt(wx_ref[...], adj_b)
    ).astype(BF)
    part_ref[:, out_width + n:out_width + 2 * n] = (mm(dmix_b, b) + mm_nt(gw, state_b)).astype(BF)


def call(kernel, outs, scratch=()):
    return pl.pallas_call(
        kernel,
        out_shape=tuple(jax.ShapeDtypeStruct(s, d) for s, d in outs),
        scratch_shapes=list(scratch),
        compiler_params=pltpu.CompilerParams(vmem_limit_bytes=VMEM_LIMIT),
    )


def local(inputs, gate_in, b_proj, c_proj, log_decay, w_out, cotangent):
    size, full = inputs.shape
    heads = log_decay.shape[0]
    n = b_proj.shape[1]
    tp = lax.axis_size("tp")
    chips = tp // 2
    workers = lax.axis_size("ctx")
    piece, out_width = cotangent.shape

    def turn(s):
        return [(2 * i + k, 2 * ((i + s) % chips) + k) for i in range(chips) for k in range(2)]

    pieces = [cotangent] + [lax.ppermute(cotangent, "tp", turn(s)) for s in range(1, chips)]
    near = jnp.concatenate(pieces, axis=0)
    far = lax.ppermute(near, "tp", [(i, i ^ 1) for i in range(tp)])

    wide = ((size, full), F32)
    square = (heads, size, size)
    st, dec, mask, mixt, scores, yi, ec, tail, wx, silu, slope = call(
        functools.partial(pre_kernel, heads),
        [((n, full), F32), ((heads, 8, size), F32), (square, F32), (square, BF), ((size, size), F32),
         wide, wide, wide, ((size, full), BF), wide, wide],
    )(inputs, gate_in, b_proj, c_proj, log_decay)
    msg, dg = call(
        functools.partial(mid_kernel, heads, piece),
        [((workers, 24, size), BF), wide],
    )(near, far, w_out, c_proj, silu, ec, st, dec)
    msg = lax.all_to_all(msg, "ctx", 0, 0, tiled=True)
    (back,) = call(
        scan_kernel,
        [((workers, 16, size), BF)],
        [pltpu.VMEM((workers, 8, size), F32), pltpu.VMEM((workers, 8, size), F32)],
    )(msg)
    back = lax.all_to_all(back, "ctx", 0, 0, tiled=True)
    part, grad_inputs, grad_gate, grad_decay = call(
        functools.partial(fin_kernel, heads),
        [((size, out_width + 2 * n), BF), ((size, full), BF), ((size, full), BF), ((heads, size), F32)],
        [pltpu.VMEM((n, full), F32), pltpu.VMEM((n, full), F32)],
    )(back, inputs, b_proj, c_proj, w_out, dg, silu, slope, mask, mixt, scores, yi, ec, tail, wx, dec)
    part = lax.all_to_all(part.reshape(tp, size // tp, out_width + 2 * n), "tp", 0, 0, tiled=True)
    total = jnp.sum(part.astype(F32), axis=0)
    layer_out = total[:, :out_width].astype(BF)
    grad_b = total[:, out_width:out_width + n]
    grad_c = total[:, out_width + n:]
    return (layer_out, grad_inputs, grad_gate, grad_b, grad_c, grad_decay)


def solution(mesh):
    in_specs = (
        P("ctx", "tp"),
        P("ctx", "tp"),
        P("ctx", None),
        P("ctx", None),
        P("tp", "ctx"),
        P("tp", None),
        P(("ctx", "tp"), None),
    )
    out_specs = (
        P(("ctx", "tp"), None),
        P("ctx", "tp"),
        P("ctx", "tp"),
        P(("ctx", "tp"), None),
        P(("ctx", "tp"), None),
        P("tp", "ctx"),
    )
    return jax.shard_map(local, mesh=mesh, in_specs=in_specs, out_specs=out_specs, check_vma=False)
```

```python
import functools

import jax
import jax.numpy as jnp
from jax import lax
from jax.experimental import pallas as pl
from jax.experimental.pallas import tpu as pltpu
from jax.sharding import PartitionSpec as P

BF = jnp.bfloat16
F32 = jnp.float32
NT = (((1,), (1,)), ((), ()))
VMEM_LIMIT = 48 * 1024 * 1024


def mm(a, b):
    return jnp.dot(a, b, preferred_element_type=F32)


def mm_nt(a, b):
    return lax.dot_general(a, b, NT, preferred_element_type=F32)


def flip(a):
    return jnp.transpose(a.astype(F32)).astype(BF)


def split(a):
    hi = a.astype(BF)
    rest = a - hi.astype(F32)
    mid = rest.astype(BF)
    return hi, mid, (rest - mid.astype(F32)).astype(BF)


def sum_by(a, ones):
    hi, mid, lo = split(a)
    return mm(hi, ones) + (mm(mid, ones) + mm(lo, ones))


def grid_of(size):
    return (
        lax.broadcasted_iota(jnp.int32, (size, size), 0),
        lax.broadcasted_iota(jnp.int32, (size, size), 1),
    )


def fetch(pairs, sems):
    copies = [pltpu.make_async_copy(src, dst, sems.at[i]) for i, (src, dst) in enumerate(pairs)]
    for copy in copies:
        copy.start()
    return copies


def pre_kernel(heads, x_hbm, gate_hbm, b_hbm, c_hbm, ld_hbm,
               st_ref, dec_ref, mask_ref, mixt_ref, scores_ref, yi_ref, ec_ref, tail_ref,
               wx_ref, silu_ref, slope_ref, x_ref, b_ref, c_ref, gate_ref, ld_ref, sems):
    copies = fetch(
        ((ld_hbm, ld_ref), (b_hbm, b_ref), (c_hbm, c_ref), (x_hbm, x_ref), (gate_hbm, gate_ref)), sems
    )
    size = x_ref.shape[0]
    width = x_ref.shape[1] // heads
    row, col = grid_of(size)
    copies[0].wait()
    ld = jnp.concatenate([ld_ref[...], jnp.zeros((8 - heads, size), F32)], axis=0)
    cum = sum_by(ld, (row <= col).astype(BF))
    copies[1].wait()
    copies[2].wait()
    scores = mm_nt(c_ref[...], b_ref[...])
    scores_ref[...] = scores
    b_t = flip(b_ref[...])
    copies[3].wait()
    for h in range(heads):
        at = slice(h * width, (h + 1) * width)
        across = jnp.broadcast_to(cum[h:h + 1, :], (size, size))
        down = jnp.transpose(across)
        mask = jnp.where(row >= col, jnp.exp(jnp.minimum(down - across, 0.0)), 0.0)
        mask_ref[h] = mask
        mixing = scores * mask
        mixt_ref[h] = jnp.transpose(mixing).astype(BF)
        x = x_ref[:, at]
        yi_ref[:, at] = mm(mixing.astype(BF), x)
        last = cum[h:h + 1, size - 1:size]
        ec_ref[:, at] = jnp.exp(down)
        tail = jnp.exp(last - down)
        tail_ref[:, at] = tail
        wx = (x.astype(F32) * tail).astype(BF)
        wx_ref[:, at] = wx
        st_ref[:, at] = mm(b_t, wx)
        decay = jnp.broadcast_to(jnp.exp(last), (8, size))
        hi = decay.astype(BF).astype(F32)
        lo = decay - hi
        dec_ref[h] = jnp.where(lax.broadcasted_iota(jnp.int32, (8, size), 0) < 4, hi, lo)
    copies[4].wait()
    v = gate_ref[...].astype(F32)
    g = 1.0 / (1.0 + jnp.exp(-v))
    silu_ref[...] = v * g
    slope_ref[...] = g + v * g * (1.0 - g)


def mid_kernel(heads, near_ref, far_ref, w_hbm, c_hbm, silu_ref, ec_ref, st_ref, dec_ref,
               msg_ref, dg_ref, w_ref, cot_ref, c_ref, sems):
    chips, piece = near_ref.shape[:2]
    size, full = st_ref.shape
    width = full // heads
    copies = fetch(
        [(w_hbm.at[pl.ds(h * width, width), :], w_ref.at[pl.ds(h * width, width), :])
         for h in range(heads)] + [(c_hbm, c_ref)], sems
    )
    core = lax.axis_index("tp") % 2
    for s in range(chips):
        at = pl.multiple_of(piece * (2 * s + core), piece)
        cot_ref[pl.ds(at, piece), :] = near_ref[s]
        at = pl.multiple_of(piece * (2 * s + 1 - core), piece)
        cot_ref[pl.ds(at, piece), :] = far_ref[s]
    copies[heads].wait()
    c_t = flip(c_ref[...])
    for h in range(heads):
        at = slice(h * width, (h + 1) * width)
        copies[h].wait()
        dg = mm_nt(cot_ref[...], w_ref[at, :])
        dg_ref[:, at] = dg
        gw = (dg * silu_ref[:, at] * ec_ref[:, at]).astype(BF)
        inj = mm(c_t, gw)
        pair = dec_ref[h].astype(BF)
        for a in range(size // 8):
            j = a * heads + h
            both = jnp.concatenate([st_ref[8 * a:8 * a + 8, at], inj[8 * a:8 * a + 8, :]], axis=0)
            msg_ref[j, 0:16, :] = both.astype(BF)
            msg_ref[j, 16:24, :] = pair


def scan_kernel(msg_ref, out_ref, dec_ref, state_ref):
    count = msg_ref.shape[0]
    state = jnp.zeros((8, msg_ref.shape[2]), F32)
    for k in range(count):
        pair = msg_ref[k, 16:24, :].astype(F32)
        decay = pair + pltpu.roll(pair, 4, 0)
        dec_ref[k] = decay
        state_ref[k] = state
        state = decay * state + msg_ref[k, 0:8, :].astype(F32)
    adjoint = jnp.zeros((8, msg_ref.shape[2]), F32)
    for k in reversed(range(count)):
        out_ref[k] = jnp.concatenate([state_ref[k], adjoint], axis=0).astype(BF)
        adjoint = dec_ref[k] * adjoint + msg_ref[k, 8:16, :].astype(F32)


def fin_kernel(heads, piece, back_ref, x_hbm, b_hbm, c_hbm, w_hbm, dg_ref, silu_ref, slope_ref, mask_ref,
               mixt_ref, scores_ref, yi_ref, ec_ref, tail_ref, wx_ref, dec_ref,
               mine_ref, theirs_ref, gi_ref, gg_ref, gd_ref,
               state_ref, adj_ref, gated_ref, terms_ref, x_ref, b_ref, c_ref, w_ref, sems):
    size, full = x_ref.shape
    width = full // heads
    copies = fetch(
        [(b_hbm, b_ref), (c_hbm, c_ref), (x_hbm, x_ref)]
        + [(w_hbm.at[pl.ds(h * width, width), :], w_ref.at[pl.ds(h * width, width), :])
           for h in range(heads)], sems
    )
    for a in range(size // 8):
        for h in range(heads):
            both = back_ref[a * heads + h].astype(F32)
            state_ref[8 * a:8 * a + 8, h * width:(h + 1) * width] = both[0:8]
            adj_ref[8 * a:8 * a + 8, h * width:(h + 1) * width] = both[8:16]
    state = state_ref[...]
    adj = adj_ref[...]
    state_b = state.astype(BF)
    adj_b = adj.astype(BF)
    copies[0].wait()
    copies[1].wait()
    b = b_ref[...]
    c = c_ref[...]
    silu = silu_ref[...]
    dg = dg_ref[...]
    ec = ec_ref[...]
    y_inter = mm(c, state_b) * ec
    y = yi_ref[...] + y_inter
    gated = (y * silu).astype(BF)
    core = lax.axis_index("tp") % 2
    places = []
    for i in range(size // piece // 2):
        for k in range(2):
            away = jnp.where(core == k, 0, 1)
            places.append((slice(piece * (2 * i + k), piece * (2 * i + k + 1)),
                           pl.ds(pl.multiple_of(size // 2 * (1 - away) + piece * i, piece), piece)))
    for src, dst in places:
        gated_ref[dst, :] = gated[src, :]
    gg_ref[...] = (dg * y * slope_ref[...]).astype(BF)
    gy = dg * silu
    gy_b = gy.astype(BF)
    gw = (gy * ec).astype(BF)
    sdx = mm(b, adj_b) * tail_ref[...]
    copies[2].wait()
    x = x_ref[...]
    through = x.astype(F32) * sdx
    entering = gy * y_inter
    scores = scores_ref[...]
    row, col = grid_of(size)
    sub = lax.broadcasted_iota(jnp.int32, (8, size), 0)
    dmix_sum = jnp.zeros((size, size), F32)
    columns = jnp.zeros((size, size), F32)
    lines = jnp.zeros((8, size), F32)
    closing = jnp.zeros((8, size), F32)
    product = adj * state
    for h in range(heads):
        at = slice(h * width, (h + 1) * width)
        dmix = mm_nt(gy_b[:, at], x[:, at]) * mask_ref[h]
        dmix_sum = dmix_sum + dmix
        cross = dmix * scores
        gi_ref[:, at] = (mm(mixt_ref[h], gy_b[:, at]) + sdx[:, at]).astype(BF)
        down = jnp.sum(cross + entering[:, at] - through[:, at], axis=1, keepdims=True)
        columns = jnp.where(col == h, down, columns)
        lines = jnp.where(sub == h, jnp.sum(cross, axis=0, keepdims=True), lines)
        decay = dec_ref[h] + pltpu.roll(dec_ref[h], 4, 0)
        end = jnp.sum(jnp.sum(through[:, at], axis=0, keepdims=True), axis=1, keepdims=True)
        dots = jnp.sum(jnp.sum(product[:, at], axis=0, keepdims=True), axis=1, keepdims=True)
        closing = jnp.where(sub == h, end + decay * dots, closing)
    flow = jnp.transpose(columns)[0:8, :] - lines
    total = sum_by(flow, (row >= col).astype(BF)) + closing
    gd_ref[...] = total[0:heads, :]
    n = b.shape[1]
    grad_b = mm(jnp.transpose(dmix_sum).astype(BF), c) + mm_nt(wx_ref[...], adj_b)
    grad_c = mm(dmix_sum.astype(BF), b) + mm_nt(gw, state_b)
    half = size // 2
    out_width = w_ref.shape[1]
    for src, dst in places:
        terms_ref[dst, 0:n] = grad_b[src, :]
        terms_ref[dst, n:2 * n] = grad_c[src, :]
    theirs_ref[:, out_width:out_width + 2 * n] = terms_ref[0:half, :].astype(BF)
    mine_ref[:, out_width:out_width + 2 * n] = terms_ref[half:size, :].astype(BF)
    for h in range(heads):
        copies[3 + h].wait()
    step = 512
    gated = gated_ref[...]
    for o in range(0, out_width, step):
        part = mm(gated, w_ref[:, o:o + step]).astype(BF)
        theirs_ref[:, o:o + step] = part[0:half, :]
        mine_ref[:, o:o + step] = part[half:size, :]


def end_kernel(part_ref, out_ref, gb_ref, gc_ref):
    out_width = out_ref.shape[1]
    n = gb_ref.shape[1]
    total = part_ref[0].astype(F32)
    for i in range(1, part_ref.shape[0]):
        total = total + part_ref[i].astype(F32)
    out_ref[...] = total[:, 0:out_width].astype(BF)
    gb_ref[...] = total[:, out_width:out_width + n]
    gc_ref[...] = total[:, out_width + n:out_width + 2 * n]


def call(kernel, outs, count, remote=(), scratch=()):
    return pl.pallas_call(
        kernel,
        out_shape=tuple(jax.ShapeDtypeStruct(s, d) for s, d in outs),
        in_specs=[
            pl.BlockSpec(memory_space=pltpu.HBM if i in remote else pltpu.VMEM)
            for i in range(count)
        ],
        scratch_shapes=list(scratch),
        compiler_params=pltpu.CompilerParams(vmem_limit_bytes=VMEM_LIMIT),
    )


def local(inputs, gate_in, b_proj, c_proj, log_decay, w_out, cotangent):
    size, full = inputs.shape
    heads = log_decay.shape[0]
    n = b_proj.shape[1]
    tp = lax.axis_size("tp")
    chips = tp // 2
    workers = lax.axis_size("ctx")
    piece, out_width = cotangent.shape
    wide = ((size, full), F32)
    wide_b = ((size, full), BF)
    square = (heads, size, size)
    small = pltpu.VMEM((size, n), BF)
    weights = pltpu.VMEM((full, out_width), BF)
    lanes = pltpu.VMEM((size, full), F32)
    rows = pltpu.VMEM((size, full), BF)
    across = [[2 * i + k for i in range(chips)] for k in range(2)]
    swap = [(i, i ^ 1) for i in range(tp)]

    near = lax.all_to_all(
        jnp.broadcast_to(cotangent[None], (chips, piece, out_width)),
        "tp", 0, 0, tiled=True, axis_index_groups=across,
    )
    far = lax.ppermute(near, "tp", swap)
    st, dec, mask, mixt, scores, yi, ec, tail, wx, silu, slope = call(
        functools.partial(pre_kernel, heads),
        [((n, full), F32), ((heads, 8, size), F32), (square, F32), (square, BF), ((size, size), F32),
         wide, wide, wide, wide_b, wide, wide],
        5, range(5),
        [rows, small, small, rows, pltpu.VMEM((heads, size), F32), pltpu.SemaphoreType.DMA((5,))],
    )(inputs, gate_in, b_proj, c_proj, log_decay)
    msg, dg = call(
        functools.partial(mid_kernel, heads),
        [((workers, 24, size), BF), wide],
        8, (2, 3),
        [weights, pltpu.VMEM((size, out_width), BF), small, pltpu.SemaphoreType.DMA((heads + 1,))],
    )(near, far, w_out, c_proj, silu, ec, st, dec)
    msg = lax.all_to_all(msg, "ctx", 0, 0, tiled=True)
    (back,) = call(
        scan_kernel, [((workers, 16, size), BF)], 1, (),
        [pltpu.VMEM((workers, 8, size), F32), pltpu.VMEM((workers, 8, size), F32)],
    )(msg)
    back = lax.all_to_all(back, "ctx", 0, 0, tiled=True)
    half = ((size // 2, out_width + 2 * n), BF)
    mine, theirs, grad_inputs, grad_gate, grad_decay = call(
        functools.partial(fin_kernel, heads, piece),
        [half, half, wide_b, wide_b, ((heads, size), F32)],
        16, range(1, 5),
        [lanes, lanes, rows, pltpu.VMEM((size, 2 * n), F32), rows, small, small, weights,
         pltpu.SemaphoreType.DMA((heads + 3,))],
    )(back, inputs, b_proj, c_proj, w_out, dg, silu, slope, mask, mixt, scores, yi, ec, tail, wx, dec)
    part = (mine.astype(F32) + lax.ppermute(theirs, "tp", swap).astype(F32)).astype(BF)
    part = lax.all_to_all(
        part.reshape(chips, piece, out_width + 2 * n),
        "tp", 0, 0, tiled=True, axis_index_groups=across,
    )
    layer_out, grad_b, grad_c = call(
        end_kernel, [((piece, out_width), BF), ((piece, n), F32), ((piece, n), F32)], 1
    )(part)
    return (layer_out, grad_inputs, grad_gate, grad_b, grad_c, grad_decay)


def solution(mesh):
    in_specs = (
        P("ctx", "tp"),
        P("ctx", "tp"),
        P("ctx", None),
        P("ctx", None),
        P("tp", "ctx"),
        P("tp", None),
        P(("ctx", "tp"), None),
    )
    out_specs = (
        P(("ctx", "tp"), None),
        P("ctx", "tp"),
        P("ctx", "tp"),
        P(("ctx", "tp"), None),
        P(("ctx", "tp"), None),
        P("tp", "ctx"),
    )
    return jax.shard_map(local, mesh=mesh, in_specs=in_specs, out_specs=out_specs, check_vma=False)
```

```python
import functools

import jax
import jax.numpy as jnp
from jax import lax
from jax.experimental import pallas as pl
from jax.experimental.pallas import tpu as pltpu
from jax.sharding import PartitionSpec as P

BF = jnp.bfloat16
F32 = jnp.float32
NT = (((1,), (1,)), ((), ()))
VMEM_LIMIT = 48 * 1024 * 1024
ROWS = 18


def mm(a, b):
    return jnp.dot(a, b, preferred_element_type=F32)


def mm_nt(a, b):
    return lax.dot_general(a, b, NT, preferred_element_type=F32)


def flip(a):
    return jnp.transpose(a.astype(F32)).astype(BF)


def split(a):
    hi = a.astype(BF)
    rest = a - hi.astype(F32)
    mid = rest.astype(BF)
    return hi, mid, (rest - mid.astype(F32)).astype(BF)


def sum_by(a, ones):
    hi, mid, lo = split(a)
    return mm(hi, ones) + (mm(mid, ones) + mm(lo, ones))


def grid_of(size):
    return (
        lax.broadcasted_iota(jnp.int32, (size, size), 0),
        lax.broadcasted_iota(jnp.int32, (size, size), 1),
    )


def fetch(pairs, sems):
    copies = [pltpu.make_async_copy(src, dst, sems.at[i]) for i, (src, dst) in enumerate(pairs)]
    for copy in copies:
        copy.start()
    return copies


def pre_kernel(heads, x_hbm, gate_hbm, b_hbm, c_hbm, ld_hbm,
               st_ref, dec_ref, mask_ref, mixt_ref, scores_ref, yi_ref, ec_ref, tail_ref,
               wx_ref, silu_ref, slope_ref, x_ref, b_ref, c_ref, gate_ref, ld_ref, sems):
    copies = fetch(
        ((ld_hbm, ld_ref), (b_hbm, b_ref), (c_hbm, c_ref), (x_hbm, x_ref), (gate_hbm, gate_ref)), sems
    )
    size = x_ref.shape[0]
    width = x_ref.shape[1] // heads
    row, col = grid_of(size)
    copies[0].wait()
    ld = jnp.concatenate([ld_ref[...], jnp.zeros((8 - heads, size), F32)], axis=0)
    cum = sum_by(ld, (row <= col).astype(BF))
    copies[1].wait()
    copies[2].wait()
    scores = mm_nt(c_ref[...], b_ref[...])
    scores_ref[...] = scores
    b_t = flip(b_ref[...])
    copies[3].wait()
    for h in range(heads):
        at = slice(h * width, (h + 1) * width)
        across = jnp.broadcast_to(cum[h:h + 1, :], (size, size))
        down = jnp.transpose(across)
        mask = jnp.where(row >= col, jnp.exp(jnp.minimum(down - across, 0.0)), 0.0)
        mask_ref[h] = mask
        mixing = scores * mask
        mixt_ref[h] = jnp.transpose(mixing).astype(BF)
        x = x_ref[:, at]
        yi_ref[:, at] = mm(mixing.astype(BF), x)
        last = cum[h:h + 1, size - 1:size]
        ec_ref[:, at] = jnp.exp(down)
        tail = jnp.exp(last - down)
        tail_ref[:, at] = tail
        wx = (x.astype(F32) * tail).astype(BF)
        wx_ref[:, at] = wx
        st_ref[:, at] = mm(b_t, wx)
        dec_ref[h] = jnp.broadcast_to(jnp.exp(last), (8, size))
    copies[4].wait()
    v = gate_ref[...].astype(F32)
    g = 1.0 / (1.0 + jnp.exp(-v))
    silu_ref[...] = v * g
    slope_ref[...] = g + v * g * (1.0 - g)


def mid_kernel(heads, near_ref, far_ref, w_hbm, c_hbm, silu_ref, ec_ref, st_ref, dec_ref,
               msg_ref, dg_ref, w_ref, cot_ref, c_ref, sems):
    chips, piece = near_ref.shape[:2]
    size, full = st_ref.shape
    width = full // heads
    copies = fetch(
        [(w_hbm.at[pl.ds(h * width, width), :], w_ref.at[pl.ds(h * width, width), :])
         for h in range(heads)] + [(c_hbm, c_ref)], sems
    )
    core = lax.axis_index("tp") % 2
    for s in range(chips):
        at = pl.multiple_of(piece * (2 * s + core), piece)
        cot_ref[pl.ds(at, piece), :] = near_ref[s]
        at = pl.multiple_of(piece * (2 * s + 1 - core), piece)
        cot_ref[pl.ds(at, piece), :] = far_ref[s]
    copies[heads].wait()
    c_t = flip(c_ref[...])
    sub = lax.broadcasted_iota(jnp.int32, (2, size), 0)
    for h in range(heads):
        at = slice(h * width, (h + 1) * width)
        if h % 2 == 0:
            copies[h].wait()
            copies[h + 1].wait()
        dg = jnp.transpose(mm_nt(w_ref[at, :], cot_ref[...]))
        dg_ref[:, at] = dg
        gw = (dg * silu_ref[:, at] * ec_ref[:, at]).astype(BF)
        inj = mm(c_t, gw)
        decay = dec_ref[h][0:2, :]
        hi = decay.astype(BF).astype(F32)
        pair = jnp.where(sub == 0, hi, decay - hi).astype(BF)
        for a in range(size // 8):
            j = ROWS * (a * heads + h)
            both = jnp.concatenate([st_ref[8 * a:8 * a + 8, at], inj[8 * a:8 * a + 8, :]], axis=0)
            msg_ref[j:j + 16, :] = both.astype(BF)
            msg_ref[j + 16:j + 18, :] = pair


def scan_kernel(msg_ref, out_ref, dec_ref, state_ref):
    count = out_ref.shape[0]
    lanes = out_ref.shape[2]
    state = jnp.zeros((8, lanes), F32)
    for k in range(count):
        at = ROWS * k
        pair = msg_ref[at + 16:at + 18, :].astype(F32)
        decay = jnp.broadcast_to(jnp.sum(pair, axis=0, keepdims=True), (8, lanes))
        dec_ref[k] = decay
        state_ref[k] = state
        state = decay * state + msg_ref[at:at + 8, :].astype(F32)
    adjoint = jnp.zeros((8, lanes), F32)
    for k in reversed(range(count)):
        at = ROWS * k
        out_ref[k] = jnp.concatenate([state_ref[k], adjoint], axis=0).astype(BF)
        adjoint = dec_ref[k] * adjoint + msg_ref[at + 8:at + 16, :].astype(F32)


def fin_kernel(heads, piece, back_ref, x_hbm, b_hbm, c_hbm, w_hbm, dg_ref, silu_ref, slope_ref, mask_ref,
               mixt_ref, scores_ref, yi_ref, ec_ref, tail_ref, wx_ref, dec_ref,
               mine_ref, theirs_ref, gi_ref, gg_ref, gd_ref,
               state_ref, adj_ref, gated_ref, terms_ref, x_ref, b_ref, c_ref, w_ref, sems):
    size, full = x_ref.shape
    width = full // heads
    copies = fetch(
        [(b_hbm, b_ref), (c_hbm, c_ref), (x_hbm, x_ref)]
        + [(w_hbm.at[pl.ds(h * width, width), :], w_ref.at[pl.ds(h * width, width), :])
           for h in range(heads)], sems
    )
    for a in range(size // 8):
        for h in range(heads):
            both = back_ref[a * heads + h].astype(F32)
            state_ref[8 * a:8 * a + 8, h * width:(h + 1) * width] = both[0:8]
            adj_ref[8 * a:8 * a + 8, h * width:(h + 1) * width] = both[8:16]
    state = state_ref[...]
    adj = adj_ref[...]
    state_b = state.astype(BF)
    adj_b = adj.astype(BF)
    copies[0].wait()
    copies[1].wait()
    b = b_ref[...]
    c = c_ref[...]
    silu = silu_ref[...]
    dg = dg_ref[...]
    ec = ec_ref[...]
    y_inter = mm(c, state_b) * ec
    y = yi_ref[...] + y_inter
    gated = (y * silu).astype(BF)
    core = lax.axis_index("tp") % 2
    places = []
    for i in range(size // piece // 2):
        for k in range(2):
            away = jnp.where(core == k, 0, 1)
            places.append((slice(piece * (2 * i + k), piece * (2 * i + k + 1)),
                           pl.ds(pl.multiple_of(size // 2 * (1 - away) + piece * i, piece), piece)))
    for src, dst in places:
        gated_ref[dst, :] = gated[src, :]
    gg_ref[...] = (dg * y * slope_ref[...]).astype(BF)
    gy = dg * silu
    gy_b = gy.astype(BF)
    gw = (gy * ec).astype(BF)
    sdx = mm(b, adj_b) * tail_ref[...]
    copies[2].wait()
    x = x_ref[...]
    through = x.astype(F32) * sdx
    entering = gy * y_inter
    scores = scores_ref[...]
    row, col = grid_of(size)
    sub = lax.broadcasted_iota(jnp.int32, (8, size), 0)
    dmix_sum = jnp.zeros((size, size), F32)
    columns = jnp.zeros((size, size), F32)
    lines = jnp.zeros((8, size), F32)
    closing = jnp.zeros((8, size), F32)
    product = adj * state
    for h in range(heads):
        at = slice(h * width, (h + 1) * width)
        dmix = mm_nt(gy_b[:, at], x[:, at]) * mask_ref[h]
        dmix_sum = dmix_sum + dmix
        cross = dmix * scores
        gi_ref[:, at] = (mm(mixt_ref[h], gy_b[:, at]) + sdx[:, at]).astype(BF)
        down = jnp.sum(cross + entering[:, at] - through[:, at], axis=1, keepdims=True)
        columns = jnp.where(col == h, down, columns)
        lines = jnp.where(sub == h, jnp.sum(cross, axis=0, keepdims=True), lines)
        end = jnp.sum(jnp.sum(through[:, at], axis=0, keepdims=True), axis=1, keepdims=True)
        dots = jnp.sum(jnp.sum(product[:, at], axis=0, keepdims=True), axis=1, keepdims=True)
        closing = jnp.where(sub == h, end + dec_ref[h] * dots, closing)
    flow = jnp.transpose(columns)[0:8, :] - lines
    total = sum_by(flow, (row >= col).astype(BF)) + closing
    gd_ref[...] = total[0:heads, :]
    n = b.shape[1]
    grad_b = mm(jnp.transpose(dmix_sum).astype(BF), c) + mm_nt(wx_ref[...], adj_b)
    grad_c = mm(dmix_sum.astype(BF), b) + mm_nt(gw, state_b)
    half = size // 2
    out_width = w_ref.shape[1]
    for src, dst in places:
        terms_ref[dst, 0:n] = grad_b[src, :]
        terms_ref[dst, n:2 * n] = grad_c[src, :]
    theirs_ref[:, out_width:out_width + 2 * n] = terms_ref[0:half, :].astype(BF)
    mine_ref[:, out_width:out_width + 2 * n] = terms_ref[half:size, :].astype(BF)
    for h in range(heads):
        copies[3 + h].wait()
    step = 512
    gated = gated_ref[...]
    for o in range(0, out_width, step):
        part = mm(gated, w_ref[:, o:o + step]).astype(BF)
        theirs_ref[:, o:o + step] = part[0:half, :]
        mine_ref[:, o:o + step] = part[half:size, :]


def end_kernel(part_ref, out_ref, gb_ref, gc_ref):
    out_width = out_ref.shape[1]
    n = gb_ref.shape[1]
    total = part_ref[0].astype(F32)
    for i in range(1, part_ref.shape[0]):
        total = total + part_ref[i].astype(F32)
    out_ref[...] = total[:, 0:out_width].astype(BF)
    gb_ref[...] = total[:, out_width:out_width + n]
    gc_ref[...] = total[:, out_width + n:out_width + 2 * n]


def call(kernel, outs, count, remote=(), scratch=()):
    return pl.pallas_call(
        kernel,
        out_shape=tuple(jax.ShapeDtypeStruct(s, d) for s, d in outs),
        in_specs=[
            pl.BlockSpec(memory_space=pltpu.HBM if i in remote else pltpu.VMEM)
            for i in range(count)
        ],
        scratch_shapes=list(scratch),
        compiler_params=pltpu.CompilerParams(vmem_limit_bytes=VMEM_LIMIT),
    )


def local(inputs, gate_in, b_proj, c_proj, log_decay, w_out, cotangent):
    size, full = inputs.shape
    heads = log_decay.shape[0]
    n = b_proj.shape[1]
    tp = lax.axis_size("tp")
    chips = tp // 2
    workers = lax.axis_size("ctx")
    piece, out_width = cotangent.shape
    wide = ((size, full), F32)
    wide_b = ((size, full), BF)
    square = (heads, size, size)
    small = pltpu.VMEM((size, n), BF)
    weights = pltpu.VMEM((full, out_width), BF)
    lanes = pltpu.VMEM((size, full), F32)
    rows = pltpu.VMEM((size, full), BF)
    across = [[2 * i + k for i in range(chips)] for k in range(2)]
    swap = [(i, i ^ 1) for i in range(tp)]

    near = lax.all_to_all(
        jnp.broadcast_to(cotangent[None], (chips, piece, out_width)),
        "tp", 0, 0, tiled=True, axis_index_groups=across,
    )
    far = lax.ppermute(near, "tp", swap)
    st, dec, mask, mixt, scores, yi, ec, tail, wx, silu, slope = call(
        functools.partial(pre_kernel, heads),
        [((n, full), F32), ((heads, 8, size), F32), (square, F32), (square, BF), ((size, size), F32),
         wide, wide, wide, wide_b, wide, wide],
        5, range(5),
        [rows, small, small, rows, pltpu.VMEM((heads, size), F32), pltpu.SemaphoreType.DMA((5,))],
    )(inputs, gate_in, b_proj, c_proj, log_decay)
    msg, dg = call(
        functools.partial(mid_kernel, heads),
        [((workers * ROWS, size), BF), wide],
        8, (2, 3),
        [weights, pltpu.VMEM((size, out_width), BF), small, pltpu.SemaphoreType.DMA((heads + 1,))],
    )(near, far, w_out, c_proj, silu, ec, st, dec)
    msg = lax.all_to_all(msg.reshape(workers, ROWS // 2, 2, size), "ctx", 0, 0, tiled=True)
    msg = msg.reshape(workers * ROWS, size)
    (back,) = call(
        scan_kernel, [((workers, 16, size), BF)], 1, (),
        [pltpu.VMEM((workers, 8, size), F32), pltpu.VMEM((workers, 8, size), F32)],
    )(msg)
    back = lax.all_to_all(back, "ctx", 0, 0, tiled=True)
    half = ((size // 2, out_width + 2 * n), BF)
    mine, theirs, grad_inputs, grad_gate, grad_decay = call(
        functools.partial(fin_kernel, heads, piece),
        [half, half, wide_b, wide_b, ((heads, size), F32)],
        16, range(1, 5),
        [lanes, lanes, rows, pltpu.VMEM((size, 2 * n), F32), rows, small, small, weights,
         pltpu.SemaphoreType.DMA((heads + 3,))],
    )(back, inputs, b_proj, c_proj, w_out, dg, silu, slope, mask, mixt, scores, yi, ec, tail, wx, dec)
    part = (mine.astype(F32) + lax.ppermute(theirs, "tp", swap).astype(F32)).astype(BF)
    part = lax.all_to_all(
        part.reshape(chips, piece, out_width + 2 * n),
        "tp", 0, 0, tiled=True, axis_index_groups=across,
    )
    layer_out, grad_b, grad_c = call(
        end_kernel, [((piece, out_width), BF), ((piece, n), F32), ((piece, n), F32)], 1
    )(part)
    return (layer_out, grad_inputs, grad_gate, grad_b, grad_c, grad_decay)


def solution(mesh):
    in_specs = (
        P("ctx", "tp"),
        P("ctx", "tp"),
        P("ctx", None),
        P("ctx", None),
        P("tp", "ctx"),
        P("tp", None),
        P(("ctx", "tp"), None),
    )
    out_specs = (
        P(("ctx", "tp"), None),
        P("ctx", "tp"),
        P("ctx", "tp"),
        P(("ctx", "tp"), None),
        P(("ctx", "tp"), None),
        P("tp", "ctx"),
    )
    return jax.shard_map(local, mesh=mesh, in_specs=in_specs, out_specs=out_specs, check_vma=False)
```

```python
import functools

import jax
import jax.numpy as jnp
from jax import lax
from jax.experimental import pallas as pl
from jax.experimental.pallas import tpu as pltpu
from jax.sharding import PartitionSpec as P

BF = jnp.bfloat16
F32 = jnp.float32
NT = (((1,), (1,)), ((), ()))
VMEM_LIMIT = 48 * 1024 * 1024
ROWS = 18
CHUNKS = 8


def mm(a, b):
    return jnp.dot(a, b, preferred_element_type=F32)


def mm_nt(a, b):
    return lax.dot_general(a, b, NT, preferred_element_type=F32)


def flip(a):
    return jnp.transpose(a.astype(F32)).astype(BF)


def split(a):
    hi = a.astype(BF)
    rest = a - hi.astype(F32)
    mid = rest.astype(BF)
    return hi, mid, (rest - mid.astype(F32)).astype(BF)


def sum_by(a, ones):
    hi, mid, lo = split(a)
    return mm(hi, ones) + (mm(mid, ones) + mm(lo, ones))


def grid_of(size):
    return (
        lax.broadcasted_iota(jnp.int32, (size, size), 0),
        lax.broadcasted_iota(jnp.int32, (size, size), 1),
    )


def fetch(pairs, sems):
    copies = [pltpu.make_async_copy(src, dst, sems.at[i]) for i, (src, dst) in enumerate(pairs)]
    for copy in copies:
        copy.start()
    return copies


def strips(src, dst):
    step = dst.shape[1] // CHUNKS
    cuts = [pl.ds(i * step, step) for i in range(CHUNKS)]
    return [(src.at[:, cut], dst.at[:, cut]) for cut in cuts]


def pre_kernel(heads, x_hbm, gate_hbm, b_hbm, c_hbm, ld_hbm,
               st_ref, dec_ref, mask_ref, mixt_ref, scores_ref, yi_ref, ec_ref, tail_ref,
               wx_ref, silu_ref, slope_ref, x_ref, b_ref, c_ref, gate_ref, ld_ref, sems):
    copies = fetch(
        ((ld_hbm, ld_ref), (b_hbm, b_ref), (c_hbm, c_ref), (x_hbm, x_ref), (gate_hbm, gate_ref)), sems
    )
    size = x_ref.shape[0]
    width = x_ref.shape[1] // heads
    row, col = grid_of(size)
    copies[0].wait()
    ld = jnp.concatenate([ld_ref[...], jnp.zeros((8 - heads, size), F32)], axis=0)
    cum = sum_by(ld, (row <= col).astype(BF))
    copies[1].wait()
    copies[2].wait()
    scores = mm_nt(c_ref[...], b_ref[...])
    scores_ref[...] = scores
    b_t = flip(b_ref[...])
    copies[3].wait()
    for h in range(heads):
        at = slice(h * width, (h + 1) * width)
        across = jnp.broadcast_to(cum[h:h + 1, :], (size, size))
        down = jnp.transpose(across)
        mask = jnp.where(row >= col, jnp.exp(jnp.minimum(down - across, 0.0)), 0.0)
        mask_ref[h] = mask
        mixing = scores * mask
        mixt_ref[h] = jnp.transpose(mixing).astype(BF)
        x = x_ref[:, at]
        yi_ref[:, at] = mm(mixing.astype(BF), x)
        last = cum[h:h + 1, size - 1:size]
        ec_ref[:, at] = jnp.exp(down)
        tail = jnp.exp(last - down)
        tail_ref[:, at] = tail
        wx = (x.astype(F32) * tail).astype(BF)
        wx_ref[:, at] = wx
        st_ref[:, at] = mm(b_t, wx)
        dec_ref[h] = jnp.broadcast_to(jnp.exp(last), (8, size))
    copies[4].wait()
    v = gate_ref[...].astype(F32)
    g = 1.0 / (1.0 + jnp.exp(-v))
    silu_ref[...] = v * g
    slope_ref[...] = g + v * g * (1.0 - g)


def mid_kernel(heads, near_ref, far_ref, w_hbm, c_hbm, silu_ref, ec_ref, st_ref, dec_ref,
               msg_ref, dg_ref, w_ref, cot_ref, c_ref, sems):
    chips, piece = near_ref.shape[:2]
    size, full = st_ref.shape
    width = full // heads
    chunk = w_ref.shape[1] // CHUNKS
    copies = fetch(strips(w_hbm, w_ref) + [(c_hbm, c_ref)], sems)
    core = lax.axis_index("tp") % 2
    for s in range(chips):
        at = pl.multiple_of(piece * (2 * s + core), piece)
        cot_ref[pl.ds(at, piece), :] = near_ref[s]
        at = pl.multiple_of(piece * (2 * s + 1 - core), piece)
        cot_ref[pl.ds(at, piece), :] = far_ref[s]
    copies[CHUNKS].wait()
    c_t = flip(c_ref[...])
    total = None
    for i in range(CHUNKS):
        copies[i].wait()
        part = slice(i * chunk, (i + 1) * chunk)
        term = mm_nt(cot_ref[:, part], w_ref[:, part])
        total = term if total is None else total + term
    dg_ref[...] = total
    sub = lax.broadcasted_iota(jnp.int32, (2, size), 0)
    for h in range(heads):
        at = slice(h * width, (h + 1) * width)
        gw = (total[:, at] * silu_ref[:, at] * ec_ref[:, at]).astype(BF)
        inj = mm(c_t, gw)
        decay = dec_ref[h][0:2, :]
        hi = decay.astype(BF).astype(F32)
        pair = jnp.where(sub == 0, hi, decay - hi).astype(BF)
        for a in range(size // 8):
            j = ROWS * (a * heads + h)
            both = jnp.concatenate([st_ref[8 * a:8 * a + 8, at], inj[8 * a:8 * a + 8, :]], axis=0)
            msg_ref[j:j + 16, :] = both.astype(BF)
            msg_ref[j + 16:j + 18, :] = pair


def scan_kernel(msg_ref, out_ref, dec_ref, state_ref):
    count = out_ref.shape[0]
    lanes = out_ref.shape[2]
    state = jnp.zeros((8, lanes), F32)
    for k in range(count):
        at = ROWS * k
        pair = msg_ref[at + 16:at + 18, :].astype(F32)
        decay = jnp.broadcast_to(jnp.sum(pair, axis=0, keepdims=True), (8, lanes))
        dec_ref[k] = decay
        state_ref[k] = state
        state = decay * state + msg_ref[at:at + 8, :].astype(F32)
    adjoint = jnp.zeros((8, lanes), F32)
    for k in reversed(range(count)):
        at = ROWS * k
        out_ref[k] = jnp.concatenate([state_ref[k], adjoint], axis=0).astype(BF)
        adjoint = dec_ref[k] * adjoint + msg_ref[at + 8:at + 16, :].astype(F32)


def fin_kernel(heads, piece, back_ref, x_hbm, b_hbm, c_hbm, w_hbm, dg_ref, silu_ref, slope_ref, mask_ref,
               mixt_ref, scores_ref, yi_ref, ec_ref, tail_ref, wx_ref, dec_ref,
               mine_ref, theirs_ref, gi_ref, gg_ref, gd_ref,
               state_ref, adj_ref, gated_ref, terms_ref, x_ref, b_ref, c_ref, w_ref, sems):
    size, full = x_ref.shape
    width = full // heads
    copies = fetch(
        [(b_hbm, b_ref), (c_hbm, c_ref), (x_hbm, x_ref)] + strips(w_hbm, w_ref), sems
    )
    for a in range(size // 8):
        for h in range(heads):
            both = back_ref[a * heads + h].astype(F32)
            state_ref[8 * a:8 * a + 8, h * width:(h + 1) * width] = both[0:8]
            adj_ref[8 * a:8 * a + 8, h * width:(h + 1) * width] = both[8:16]
    state = state_ref[...]
    adj = adj_ref[...]
    state_b = state.astype(BF)
    adj_b = adj.astype(BF)
    copies[0].wait()
    copies[1].wait()
    b = b_ref[...]
    c = c_ref[...]
    silu = silu_ref[...]
    dg = dg_ref[...]
    ec = ec_ref[...]
    y_inter = mm(c, state_b) * ec
    y = yi_ref[...] + y_inter
    gated = (y * silu).astype(BF)
    core = lax.axis_index("tp") % 2
    places = []
    for i in range(size // piece // 2):
        for k in range(2):
            away = jnp.where(core == k, 0, 1)
            places.append((slice(piece * (2 * i + k), piece * (2 * i + k + 1)),
                           pl.ds(pl.multiple_of(size // 2 * (1 - away) + piece * i, piece), piece)))
    for src, dst in places:
        gated_ref[dst, :] = gated[src, :]
    gg_ref[...] = (dg * y * slope_ref[...]).astype(BF)
    gy = dg * silu
    gy_b = gy.astype(BF)
    gw = (gy * ec).astype(BF)
    sdx = mm(b, adj_b) * tail_ref[...]
    copies[2].wait()
    x = x_ref[...]
    through = x.astype(F32) * sdx
    entering = gy * y_inter
    scores = scores_ref[...]
    row, col = grid_of(size)
    sub = lax.broadcasted_iota(jnp.int32, (8, size), 0)
    dmix_sum = jnp.zeros((size, size), F32)
    columns = jnp.zeros((size, size), F32)
    lines = jnp.zeros((8, size), F32)
    closing = jnp.zeros((8, size), F32)
    product = adj * state
    for h in range(heads):
        at = slice(h * width, (h + 1) * width)
        dmix = mm_nt(gy_b[:, at], x[:, at]) * mask_ref[h]
        dmix_sum = dmix_sum + dmix
        cross = dmix * scores
        gi_ref[:, at] = (mm(mixt_ref[h], gy_b[:, at]) + sdx[:, at]).astype(BF)
        down = jnp.sum(cross + entering[:, at] - through[:, at], axis=1, keepdims=True)
        columns = jnp.where(col == h, down, columns)
        lines = jnp.where(sub == h, jnp.sum(cross, axis=0, keepdims=True), lines)
        end = jnp.sum(jnp.sum(through[:, at], axis=0, keepdims=True), axis=1, keepdims=True)
        dots = jnp.sum(jnp.sum(product[:, at], axis=0, keepdims=True), axis=1, keepdims=True)
        closing = jnp.where(sub == h, end + dec_ref[h] * dots, closing)
    flow = jnp.transpose(columns)[0:8, :] - lines
    total = sum_by(flow, (row >= col).astype(BF)) + closing
    gd_ref[...] = total[0:heads, :]
    n = b.shape[1]
    grad_b = mm(jnp.transpose(dmix_sum).astype(BF), c) + mm_nt(wx_ref[...], adj_b)
    grad_c = mm(dmix_sum.astype(BF), b) + mm_nt(gw, state_b)
    half = size // 2
    out_width = w_ref.shape[1]
    for src, dst in places:
        terms_ref[dst, 0:n] = grad_b[src, :]
        terms_ref[dst, n:2 * n] = grad_c[src, :]
    theirs_ref[:, out_width:out_width + 2 * n] = terms_ref[0:half, :].astype(BF)
    mine_ref[:, out_width:out_width + 2 * n] = terms_ref[half:size, :].astype(BF)
    step = out_width // CHUNKS
    gated = gated_ref[...]
    for i in range(CHUNKS):
        copies[3 + i].wait()
        o = i * step
        part = mm(gated, w_ref[:, o:o + step]).astype(BF)
        theirs_ref[:, o:o + step] = part[0:half, :]
        mine_ref[:, o:o + step] = part[half:size, :]


def end_kernel(part_ref, out_ref, gb_ref, gc_ref):
    out_width = out_ref.shape[1]
    n = gb_ref.shape[1]
    total = part_ref[0].astype(F32)
    for i in range(1, part_ref.shape[0]):
        total = total + part_ref[i].astype(F32)
    out_ref[...] = total[:, 0:out_width].astype(BF)
    gb_ref[...] = total[:, out_width:out_width + n]
    gc_ref[...] = total[:, out_width + n:out_width + 2 * n]


def call(kernel, outs, count, remote=(), scratch=()):
    return pl.pallas_call(
        kernel,
        out_shape=tuple(jax.ShapeDtypeStruct(s, d) for s, d in outs),
        in_specs=[
            pl.BlockSpec(memory_space=pltpu.HBM if i in remote else pltpu.VMEM)
            for i in range(count)
        ],
        scratch_shapes=list(scratch),
        compiler_params=pltpu.CompilerParams(vmem_limit_bytes=VMEM_LIMIT),
    )


def local(inputs, gate_in, b_proj, c_proj, log_decay, w_out, cotangent):
    size, full = inputs.shape
    heads = log_decay.shape[0]
    n = b_proj.shape[1]
    tp = lax.axis_size("tp")
    chips = tp // 2
    workers = lax.axis_size("ctx")
    piece, out_width = cotangent.shape
    wide = ((size, full), F32)
    wide_b = ((size, full), BF)
    square = (heads, size, size)
    small = pltpu.VMEM((size, n), BF)
    weights = pltpu.VMEM((full, out_width), BF)
    lanes = pltpu.VMEM((size, full), F32)
    rows = pltpu.VMEM((size, full), BF)
    across = [[2 * i + k for i in range(chips)] for k in range(2)]
    swap = [(i, i ^ 1) for i in range(tp)]

    near = lax.all_to_all(
        jnp.broadcast_to(cotangent[None], (chips, piece, out_width)),
        "tp", 0, 0, tiled=True, axis_index_groups=across,
    )
    far = lax.ppermute(near, "tp", swap)
    st, dec, mask, mixt, scores, yi, ec, tail, wx, silu, slope = call(
        functools.partial(pre_kernel, heads),
        [((n, full), F32), ((heads, 8, size), F32), (square, F32), (square, BF), ((size, size), F32),
         wide, wide, wide, wide_b, wide, wide],
        5, range(5),
        [rows, small, small, rows, pltpu.VMEM((heads, size), F32), pltpu.SemaphoreType.DMA((5,))],
    )(inputs, gate_in, b_proj, c_proj, log_decay)
    msg, dg = call(
        functools.partial(mid_kernel, heads),
        [((workers * ROWS, size), BF), wide],
        8, (2, 3),
        [weights, pltpu.VMEM((size, out_width), BF), small, pltpu.SemaphoreType.DMA((CHUNKS + 1,))],
    )(near, far, w_out, c_proj, silu, ec, st, dec)
    msg = lax.all_to_all(msg.reshape(workers, ROWS // 2, 2, size), "ctx", 0, 0, tiled=True)
    msg = msg.reshape(workers * ROWS, size)
    (back,) = call(
        scan_kernel, [((workers, 16, size), BF)], 1, (),
        [pltpu.VMEM((workers, 8, size), F32), pltpu.VMEM((workers, 8, size), F32)],
    )(msg)
    back = lax.all_to_all(back, "ctx", 0, 0, tiled=True)
    half = ((size // 2, out_width + 2 * n), BF)
    mine, theirs, grad_inputs, grad_gate, grad_decay = call(
        functools.partial(fin_kernel, heads, piece),
        [half, half, wide_b, wide_b, ((heads, size), F32)],
        16, range(1, 5),
        [lanes, lanes, rows, pltpu.VMEM((size, 2 * n), F32), rows, small, small, weights,
         pltpu.SemaphoreType.DMA((CHUNKS + 3,))],
    )(back, inputs, b_proj, c_proj, w_out, dg, silu, slope, mask, mixt, scores, yi, ec, tail, wx, dec)
    part = (mine.astype(F32) + lax.ppermute(theirs, "tp", swap).astype(F32)).astype(BF)
    part = lax.all_to_all(
        part.reshape(chips, piece, out_width + 2 * n),
        "tp", 0, 0, tiled=True, axis_index_groups=across,
    )
    layer_out, grad_b, grad_c = call(
        end_kernel, [((piece, out_width), BF), ((piece, n), F32), ((piece, n), F32)], 1
    )(part)
    return (layer_out, grad_inputs, grad_gate, grad_b, grad_c, grad_decay)


def solution(mesh):
    in_specs = (
        P("ctx", "tp"),
        P("ctx", "tp"),
        P("ctx", None),
        P("ctx", None),
        P("tp", "ctx"),
        P("tp", None),
        P(("ctx", "tp"), None),
    )
    out_specs = (
        P(("ctx", "tp"), None),
        P("ctx", "tp"),
        P("ctx", "tp"),
        P(("ctx", "tp"), None),
        P(("ctx", "tp"), None),
        P("tp", "ctx"),
    )
    return jax.shard_map(local, mesh=mesh, in_specs=in_specs, out_specs=out_specs, check_vma=False)
```

```python
import functools

import jax
import jax.numpy as jnp
from jax import lax
from jax.experimental import pallas as pl
from jax.experimental.pallas import tpu as pltpu
from jax.sharding import PartitionSpec as P

BF = jnp.bfloat16
F32 = jnp.float32
NT = (((1,), (1,)), ((), ()))
VMEM_LIMIT = 48 * 1024 * 1024
ROWS = 18
CHUNKS = 8
KEPT = 4


def mm(a, b):
    return jnp.dot(a, b, preferred_element_type=F32)


def mm_nt(a, b):
    return lax.dot_general(a, b, NT, preferred_element_type=F32)


def flip(a):
    return jnp.transpose(a.astype(F32)).astype(BF)


def split(a):
    hi = a.astype(BF)
    rest = a - hi.astype(F32)
    mid = rest.astype(BF)
    return hi, mid, (rest - mid.astype(F32)).astype(BF)


def sum_by(a, ones):
    hi, mid, lo = split(a)
    return mm(hi, ones) + (mm(mid, ones) + mm(lo, ones))


def grid_of(size):
    return (
        lax.broadcasted_iota(jnp.int32, (size, size), 0),
        lax.broadcasted_iota(jnp.int32, (size, size), 1),
    )


def fetch(pairs, sems):
    copies = [pltpu.make_async_copy(src, dst, sems.at[i]) for i, (src, dst) in enumerate(pairs)]
    for copy in copies:
        copy.start()
    return copies


def strips(src, dst, first, last):
    step = src.shape[1] // CHUNKS
    return [
        (src.at[:, pl.ds(i * step, step)], dst.at[:, pl.ds((i - first) * step, step)])
        for i in range(first, last)
    ]


def downward(cum_ref, h):
    size = cum_ref.shape[1]
    return jnp.transpose(jnp.broadcast_to(cum_ref[h:h + 1, :], (size, size)))


def gates(gate_ref):
    v = gate_ref[...].astype(F32)
    g = 1.0 / (1.0 + jnp.exp(-v))
    return v * g, g


def pre_kernel(heads, x_hbm, b_hbm, c_hbm, ld_hbm, w_hbm,
               st_ref, dec_ref, cum_ref, mixt_ref, scores_ref, yi_ref, wx_ref, kept_ref,
               x_ref, b_ref, c_ref, ld_ref, sems):
    copies = fetch(
        [(ld_hbm, ld_ref), (b_hbm, b_ref), (c_hbm, c_ref), (x_hbm, x_ref)]
        + strips(w_hbm, kept_ref, 0, KEPT), sems
    )
    size = x_ref.shape[0]
    width = x_ref.shape[1] // heads
    row, col = grid_of(size)
    copies[0].wait()
    ld = jnp.concatenate([ld_ref[...], jnp.zeros((8 - heads, size), F32)], axis=0)
    cum = sum_by(ld, (row <= col).astype(BF))
    cum_ref[...] = cum
    copies[1].wait()
    copies[2].wait()
    scores = mm_nt(c_ref[...], b_ref[...])
    scores_ref[...] = scores
    b_t = flip(b_ref[...])
    copies[3].wait()
    for h in range(heads):
        at = slice(h * width, (h + 1) * width)
        across = jnp.broadcast_to(cum[h:h + 1, :], (size, size))
        down = jnp.transpose(across)
        mask = jnp.where(row >= col, jnp.exp(jnp.minimum(down - across, 0.0)), 0.0)
        mixing = scores * mask
        mixt_ref[h] = jnp.transpose(mixing).astype(BF)
        x = x_ref[:, at]
        yi_ref[:, at] = mm(mixing.astype(BF), x)
        last = cum[h:h + 1, size - 1:size]
        tail = jnp.exp(last - down)
        wx = (x.astype(F32) * tail).astype(BF)
        wx_ref[:, at] = wx
        st_ref[:, at] = mm(b_t, wx)
        dec_ref[h] = jnp.broadcast_to(jnp.exp(last), (8, size))
    for copy in copies[4:]:
        copy.wait()


def mid_kernel(heads, near_ref, far_ref, w_hbm, c_hbm, gate_hbm, kept_ref, cum_ref, st_ref, dec_ref,
               msg_ref, dg_ref, w_ref, cot_ref, c_ref, gate_ref, sems):
    chips, piece = near_ref.shape[:2]
    size, full = st_ref.shape
    width = full // heads
    chunk = w_hbm.shape[1] // CHUNKS
    copies = fetch(
        [(c_hbm, c_ref), (gate_hbm, gate_ref)] + strips(w_hbm, w_ref, KEPT, CHUNKS), sems
    )
    core = lax.axis_index("tp") % 2
    for s in range(chips):
        at = pl.multiple_of(piece * (2 * s + core), piece)
        cot_ref[pl.ds(at, piece), :] = near_ref[s]
        at = pl.multiple_of(piece * (2 * s + 1 - core), piece)
        cot_ref[pl.ds(at, piece), :] = far_ref[s]
    copies[0].wait()
    copies[1].wait()
    c_t = flip(c_ref[...])
    silu, g = gates(gate_ref)
    held = KEPT * chunk
    total = mm_nt(cot_ref[:, 0:held], kept_ref[...])
    for i in range(KEPT, CHUNKS):
        copies[2 + i - KEPT].wait()
        own = slice((i - KEPT) * chunk, (i - KEPT + 1) * chunk)
        total = total + mm_nt(cot_ref[:, i * chunk:(i + 1) * chunk], w_ref[:, own])
    dg_ref[...] = total
    sub = lax.broadcasted_iota(jnp.int32, (2, size), 0)
    for h in range(heads):
        at = slice(h * width, (h + 1) * width)
        gw = (total[:, at] * silu[:, at] * jnp.exp(downward(cum_ref, h))).astype(BF)
        inj = mm(c_t, gw)
        decay = dec_ref[h][0:2, :]
        hi = decay.astype(BF).astype(F32)
        pair = jnp.where(sub == 0, hi, decay - hi).astype(BF)
        for a in range(size // 8):
            j = ROWS * (a * heads + h)
            both = jnp.concatenate([st_ref[8 * a:8 * a + 8, at], inj[8 * a:8 * a + 8, :]], axis=0)
            msg_ref[j:j + 16, :] = both.astype(BF)
            msg_ref[j + 16:j + 18, :] = pair


def scan_kernel(msg_ref, out_ref, dec_ref, state_ref):
    count = out_ref.shape[0]
    lanes = out_ref.shape[2]
    state = jnp.zeros((8, lanes), F32)
    for k in range(count):
        at = ROWS * k
        pair = msg_ref[at + 16:at + 18, :].astype(F32)
        decay = jnp.broadcast_to(jnp.sum(pair, axis=0, keepdims=True), (8, lanes))
        dec_ref[k] = decay
        state_ref[k] = state
        state = decay * state + msg_ref[at:at + 8, :].astype(F32)
    adjoint = jnp.zeros((8, lanes), F32)
    for k in reversed(range(count)):
        at = ROWS * k
        out_ref[k] = jnp.concatenate([state_ref[k], adjoint], axis=0).astype(BF)
        adjoint = dec_ref[k] * adjoint + msg_ref[at + 8:at + 16, :].astype(F32)


def fin_kernel(heads, piece, back_ref, x_hbm, b_hbm, c_hbm, w_hbm, gate_hbm, kept_ref, dg_ref, cum_ref,
               mixt_ref, scores_ref, yi_ref, wx_ref, dec_ref,
               mine_ref, theirs_ref, gi_ref, gg_ref, gd_ref,
               state_ref, adj_ref, gated_ref, terms_ref, x_ref, b_ref, c_ref, gate_ref, w_ref, sems):
    size, full = x_ref.shape
    width = full // heads
    copies = fetch(
        [(b_hbm, b_ref), (c_hbm, c_ref), (gate_hbm, gate_ref), (x_hbm, x_ref)]
        + strips(w_hbm, w_ref, KEPT, CHUNKS), sems
    )
    for a in range(size // 8):
        for h in range(heads):
            both = back_ref[a * heads + h].astype(F32)
            state_ref[8 * a:8 * a + 8, h * width:(h + 1) * width] = both[0:8]
            adj_ref[8 * a:8 * a + 8, h * width:(h + 1) * width] = both[8:16]
    state = state_ref[...]
    adj = adj_ref[...]
    state_b = state.astype(BF)
    adj_b = adj.astype(BF)
    copies[0].wait()
    copies[1].wait()
    b = b_ref[...]
    c = c_ref[...]
    copies[2].wait()
    silu, g = gates(gate_ref)
    dg = dg_ref[...]
    downs = [downward(cum_ref, h) for h in range(heads)]
    ec = jnp.concatenate([jnp.exp(down) for down in downs], axis=1)
    tail = jnp.concatenate(
        [jnp.exp(cum_ref[h:h + 1, size - 1:size] - downs[h]) for h in range(heads)], axis=1
    )
    y_inter = mm(c, state_b) * ec
    y = yi_ref[...] + y_inter
    gated = (y * silu).astype(BF)
    core = lax.axis_index("tp") % 2
    places = []
    for i in range(size // piece // 2):
        for k in range(2):
            away = jnp.where(core == k, 0, 1)
            places.append((slice(piece * (2 * i + k), piece * (2 * i + k + 1)),
                           pl.ds(pl.multiple_of(size // 2 * (1 - away) + piece * i, piece), piece)))
    for src, dst in places:
        gated_ref[dst, :] = gated[src, :]
    gg_ref[...] = (dg * y * (g + silu * (1.0 - g))).astype(BF)
    gy = dg * silu
    gy_b = gy.astype(BF)
    gw = (gy * ec).astype(BF)
    sdx = mm(b, adj_b) * tail
    copies[3].wait()
    x = x_ref[...]
    through = x.astype(F32) * sdx
    entering = gy * y_inter
    scores = scores_ref[...]
    row, col = grid_of(size)
    sub = lax.broadcasted_iota(jnp.int32, (8, size), 0)
    dmix_sum = jnp.zeros((size, size), F32)
    columns = jnp.zeros((size, size), F32)
    lines = jnp.zeros((8, size), F32)
    closing = jnp.zeros((8, size), F32)
    product = adj * state
    for h in range(heads):
        at = slice(h * width, (h + 1) * width)
        gap = downs[h] - jnp.broadcast_to(cum_ref[h:h + 1, :], (size, size))
        mask = jnp.where(row >= col, jnp.exp(jnp.minimum(gap, 0.0)), 0.0)
        dmix = mm_nt(gy_b[:, at], x[:, at]) * mask
        dmix_sum = dmix_sum + dmix
        cross = dmix * scores
        gi_ref[:, at] = (mm(mixt_ref[h], gy_b[:, at]) + sdx[:, at]).astype(BF)
        down = jnp.sum(cross + entering[:, at] - through[:, at], axis=1, keepdims=True)
        columns = jnp.where(col == h, down, columns)
        lines = jnp.where(sub == h, jnp.sum(cross, axis=0, keepdims=True), lines)
        end = jnp.sum(jnp.sum(through[:, at], axis=0, keepdims=True), axis=1, keepdims=True)
        dots = jnp.sum(jnp.sum(product[:, at], axis=0, keepdims=True), axis=1, keepdims=True)
        closing = jnp.where(sub == h, end + dec_ref[h] * dots, closing)
    flow = jnp.transpose(columns)[0:8, :] - lines
    total = sum_by(flow, (row >= col).astype(BF)) + closing
    gd_ref[...] = total[0:heads, :]
    n = b.shape[1]
    grad_b = mm(jnp.transpose(dmix_sum).astype(BF), c) + mm_nt(wx_ref[...], adj_b)
    grad_c = mm(dmix_sum.astype(BF), b) + mm_nt(gw, state_b)
    half = size // 2
    out_width = w_hbm.shape[1]
    for src, dst in places:
        terms_ref[dst, 0:n] = grad_b[src, :]
        terms_ref[dst, n:2 * n] = grad_c[src, :]
    theirs_ref[:, out_width:out_width + 2 * n] = terms_ref[0:half, :].astype(BF)
    mine_ref[:, out_width:out_width + 2 * n] = terms_ref[half:size, :].astype(BF)
    step = out_width // CHUNKS
    gated = gated_ref[...]
    for i in range(CHUNKS):
        if i == KEPT or i == (KEPT + CHUNKS) // 2:
            for k in range(i, (KEPT + CHUNKS) // 2 if i == KEPT else CHUNKS):
                copies[4 + k - KEPT].wait()
        own = kept_ref if i < KEPT else w_ref
        at = (i if i < KEPT else i - KEPT) * step
        part = mm(gated, own[:, at:at + step]).astype(BF)
        theirs_ref[:, i * step:(i + 1) * step] = part[0:half, :]
        mine_ref[:, i * step:(i + 1) * step] = part[half:size, :]


def end_kernel(part_ref, out_ref, gb_ref, gc_ref):
    out_width = out_ref.shape[1]
    n = gb_ref.shape[1]
    total = part_ref[0].astype(F32)
    for i in range(1, part_ref.shape[0]):
        total = total + part_ref[i].astype(F32)
    out_ref[...] = total[:, 0:out_width].astype(BF)
    gb_ref[...] = total[:, out_width:out_width + n]
    gc_ref[...] = total[:, out_width + n:out_width + 2 * n]


def call(kernel, outs, count, remote=(), scratch=()):
    return pl.pallas_call(
        kernel,
        out_shape=tuple(jax.ShapeDtypeStruct(s, d) for s, d in outs),
        in_specs=[
            pl.BlockSpec(memory_space=pltpu.HBM if i in remote else pltpu.VMEM)
            for i in range(count)
        ],
        scratch_shapes=list(scratch),
        compiler_params=pltpu.CompilerParams(vmem_limit_bytes=VMEM_LIMIT),
    )


def local(inputs, gate_in, b_proj, c_proj, log_decay, w_out, cotangent):
    size, full = inputs.shape
    heads = log_decay.shape[0]
    n = b_proj.shape[1]
    tp = lax.axis_size("tp")
    chips = tp // 2
    workers = lax.axis_size("ctx")
    piece, out_width = cotangent.shape
    wide = ((size, full), F32)
    wide_b = ((size, full), BF)
    square = (heads, size, size)
    small = pltpu.VMEM((size, n), BF)
    kept_width = out_width // CHUNKS * KEPT
    weights = pltpu.VMEM((full, out_width - kept_width), BF)
    lanes = pltpu.VMEM((size, full), F32)
    rows = pltpu.VMEM((size, full), BF)
    across = [[2 * i + k for i in range(chips)] for k in range(2)]
    swap = [(i, i ^ 1) for i in range(tp)]

    near = lax.all_to_all(
        jnp.broadcast_to(cotangent[None], (chips, piece, out_width)),
        "tp", 0, 0, tiled=True, axis_index_groups=across,
    )
    far = lax.ppermute(near, "tp", swap)
    st, dec, cum, mixt, scores, yi, wx, kept = call(
        functools.partial(pre_kernel, heads),
        [((n, full), F32), ((heads, 8, size), F32), ((8, size), F32), (square, BF), ((size, size), F32),
         wide, wide_b, ((full, kept_width), BF)],
        5, range(5),
        [rows, small, small, pltpu.VMEM((heads, size), F32), pltpu.SemaphoreType.DMA((4 + KEPT,))],
    )(inputs, b_proj, c_proj, log_decay, w_out)
    msg, dg = call(
        functools.partial(mid_kernel, heads),
        [((workers * ROWS, size), BF), wide],
        9, (2, 3, 4),
        [weights, pltpu.VMEM((size, out_width), BF), small, rows,
         pltpu.SemaphoreType.DMA((2 + CHUNKS - KEPT,))],
    )(near, far, w_out, c_proj, gate_in, kept, cum, st, dec)
    msg = lax.all_to_all(msg.reshape(workers, ROWS // 2, 2, size), "ctx", 0, 0, tiled=True)
    msg = msg.reshape(workers * ROWS, size)
    (back,) = call(
        scan_kernel, [((workers, 16, size), BF)], 1, (),
        [pltpu.VMEM((workers, 8, size), F32), pltpu.VMEM((workers, 8, size), F32)],
    )(msg)
    back = lax.all_to_all(back, "ctx", 0, 0, tiled=True)
    half = ((size // 2, out_width + 2 * n), BF)
    mine, theirs, grad_inputs, grad_gate, grad_decay = call(
        functools.partial(fin_kernel, heads, piece),
        [half, half, wide_b, wide_b, ((heads, size), F32)],
        14, range(1, 6),
        [lanes, lanes, rows, pltpu.VMEM((size, 2 * n), F32), rows, small, small, rows, weights,
         pltpu.SemaphoreType.DMA((4 + CHUNKS - KEPT,))],
    )(back, inputs, b_proj, c_proj, w_out, gate_in, kept, dg, cum, mixt, scores, yi, wx, dec)
    part = (mine.astype(F32) + lax.ppermute(theirs, "tp", swap).astype(F32)).astype(BF)
    part = lax.all_to_all(
        part.reshape(chips, piece, out_width + 2 * n),
        "tp", 0, 0, tiled=True, axis_index_groups=across,
    )
    layer_out, grad_b, grad_c = call(
        end_kernel, [((piece, out_width), BF), ((piece, n), F32), ((piece, n), F32)], 1
    )(part)
    return (layer_out, grad_inputs, grad_gate, grad_b, grad_c, grad_decay)


def solution(mesh):
    in_specs = (
        P("ctx", "tp"),
        P("ctx", "tp"),
        P("ctx", None),
        P("ctx", None),
        P("tp", "ctx"),
        P("tp", None),
        P(("ctx", "tp"), None),
    )
    out_specs = (
        P(("ctx", "tp"), None),
        P("ctx", "tp"),
        P("ctx", "tp"),
        P(("ctx", "tp"), None),
        P(("ctx", "tp"), None),
        P("tp", "ctx"),
    )
    return jax.shard_map(local, mesh=mesh, in_specs=in_specs, out_specs=out_specs, check_vma=False)
```

```python
import functools

import jax
import jax.numpy as jnp
from jax import lax
from jax.experimental import pallas as pl
from jax.experimental.pallas import tpu as pltpu
from jax.sharding import PartitionSpec as P

BF = jnp.bfloat16
F32 = jnp.float32
NT = (((1,), (1,)), ((), ()))
VMEM_LIMIT = 48 * 1024 * 1024
ROWS = 18
CHUNKS = 8
KEPT = 4


def mm(a, b):
    return jnp.dot(a, b, preferred_element_type=F32)


def mm_nt(a, b):
    return lax.dot_general(a, b, NT, preferred_element_type=F32)


def flip(a):
    return jnp.transpose(a.astype(F32)).astype(BF)


def split(a):
    hi = a.astype(BF)
    rest = a - hi.astype(F32)
    mid = rest.astype(BF)
    return hi, mid, (rest - mid.astype(F32)).astype(BF)


def sum_by(a, ones):
    hi, mid, lo = split(a)
    return mm(hi, ones) + (mm(mid, ones) + mm(lo, ones))


def grid_of(size):
    return (
        lax.broadcasted_iota(jnp.int32, (size, size), 0),
        lax.broadcasted_iota(jnp.int32, (size, size), 1),
    )


def fetch(pairs, sems):
    copies = [pltpu.make_async_copy(src, dst, sems.at[i]) for i, (src, dst) in enumerate(pairs)]
    for copy in copies:
        copy.start()
    return copies


def strips(src, dst, first, last):
    step = src.shape[1] // CHUNKS
    return [
        (src.at[:, pl.ds(i * step, step)], dst.at[:, pl.ds((i - first) * step, step)])
        for i in range(first, last)
    ]


def downward(cum_ref, h):
    size = cum_ref.shape[1]
    return jnp.transpose(jnp.broadcast_to(cum_ref[h:h + 1, :], (size, size)))


def gates(gate_ref):
    v = gate_ref[...].astype(F32)
    g = 1.0 / (1.0 + jnp.exp(-v))
    return v * g, g


def pre_kernel(heads, x_hbm, b_hbm, c_hbm, ld_hbm, w_hbm,
               st_ref, dec_ref, cum_ref, mixt_ref, scores_ref, yi_ref, wx_ref, kept_ref,
               x_ref, b_ref, c_ref, ld_ref, sems):
    copies = fetch(
        [(ld_hbm, ld_ref), (b_hbm, b_ref), (c_hbm, c_ref), (x_hbm, x_ref)]
        + strips(w_hbm, kept_ref, 0, KEPT), sems
    )
    size = x_ref.shape[0]
    width = x_ref.shape[1] // heads
    row, col = grid_of(size)
    copies[0].wait()
    ld = jnp.concatenate([ld_ref[...], jnp.zeros((8 - heads, size), F32)], axis=0)
    cum = sum_by(ld, (row <= col).astype(BF))
    cum_ref[...] = cum
    copies[1].wait()
    copies[2].wait()
    scores = mm_nt(c_ref[...], b_ref[...])
    scores_ref[...] = scores
    b_t = flip(b_ref[...])
    copies[3].wait()
    for h in range(heads):
        at = slice(h * width, (h + 1) * width)
        across = jnp.broadcast_to(cum[h:h + 1, :], (size, size))
        down = jnp.transpose(across)
        mask = jnp.where(row >= col, jnp.exp(jnp.minimum(down - across, 0.0)), 0.0)
        mixing = scores * mask
        mixt_ref[h] = jnp.transpose(mixing).astype(BF)
        x = x_ref[:, at]
        yi_ref[:, at] = mm(mixing.astype(BF), x)
        last = cum[h:h + 1, size - 1:size]
        tail = jnp.exp(last - down)
        wx = (x.astype(F32) * tail).astype(BF)
        wx_ref[:, at] = wx
        st_ref[:, at] = mm(b_t, wx)
        dec_ref[h] = jnp.broadcast_to(jnp.exp(last), (8, size))
    for copy in copies[4:]:
        copy.wait()


def mid_kernel(heads, near_ref, far_ref, w_hbm, c_hbm, gate_hbm, kept_ref, cum_ref, st_ref, dec_ref,
               msg_ref, dg_ref, w_ref, cot_ref, c_ref, gate_ref, sems):
    chips, piece = near_ref.shape[:2]
    size, full = st_ref.shape
    width = full // heads
    chunk = w_hbm.shape[1] // CHUNKS
    copies = fetch(
        [(c_hbm, c_ref), (gate_hbm, gate_ref)] + strips(w_hbm, w_ref, KEPT, CHUNKS), sems
    )
    core = lax.axis_index("tp") % 2
    for s in range(chips):
        at = pl.multiple_of(piece * (2 * s + core), piece)
        cot_ref[pl.ds(at, piece), :] = near_ref[s]
        at = pl.multiple_of(piece * (2 * s + 1 - core), piece)
        cot_ref[pl.ds(at, piece), :] = far_ref[s]
    copies[0].wait()
    copies[1].wait()
    c_t = flip(c_ref[...])
    silu, g = gates(gate_ref)
    total = None
    for i in range(KEPT):
        own = slice(i * chunk, (i + 1) * chunk)
        term = mm_nt(cot_ref[:, own], kept_ref[:, own])
        total = term if total is None else total + term
    for i in range(KEPT, CHUNKS):
        copies[2 + i - KEPT].wait()
        own = slice((i - KEPT) * chunk, (i - KEPT + 1) * chunk)
        total = total + mm_nt(cot_ref[:, i * chunk:(i + 1) * chunk], w_ref[:, own])
    dg_ref[...] = total
    sub = lax.broadcasted_iota(jnp.int32, (2, size), 0)
    for h in range(heads):
        at = slice(h * width, (h + 1) * width)
        gw = (total[:, at] * silu[:, at] * jnp.exp(downward(cum_ref, h))).astype(BF)
        inj = mm(c_t, gw)
        decay = dec_ref[h][0:2, :]
        hi = decay.astype(BF).astype(F32)
        pair = jnp.where(sub == 0, hi, decay - hi).astype(BF)
        for a in range(size // 8):
            j = ROWS * (a * heads + h)
            both = jnp.concatenate([st_ref[8 * a:8 * a + 8, at], inj[8 * a:8 * a + 8, :]], axis=0)
            msg_ref[j:j + 16, :] = both.astype(BF)
            msg_ref[j + 16:j + 18, :] = pair


def scan_kernel(msg_ref, out_ref, dec_ref, state_ref):
    count = out_ref.shape[0]
    lanes = out_ref.shape[2]
    state = jnp.zeros((8, lanes), F32)
    for k in range(count):
        at = ROWS * k
        pair = msg_ref[at + 16:at + 18, :].astype(F32)
        decay = jnp.broadcast_to(jnp.sum(pair, axis=0, keepdims=True), (8, lanes))
        dec_ref[k] = decay
        state_ref[k] = state
        state = decay * state + msg_ref[at:at + 8, :].astype(F32)
    adjoint = jnp.zeros((8, lanes), F32)
    for k in reversed(range(count)):
        at = ROWS * k
        out_ref[k] = jnp.concatenate([state_ref[k], adjoint], axis=0).astype(BF)
        adjoint = dec_ref[k] * adjoint + msg_ref[at + 8:at + 16, :].astype(F32)


def fin_kernel(heads, piece, back_ref, x_hbm, b_hbm, c_hbm, w_hbm, gate_hbm, kept_ref, dg_ref, cum_ref,
               mixt_ref, scores_ref, yi_ref, wx_ref, dec_ref,
               mine_ref, theirs_ref, gi_ref, gg_ref, gd_ref,
               state_ref, adj_ref, gated_ref, terms_ref, x_ref, b_ref, c_ref, gate_ref, w_ref, sems):
    size, full = x_ref.shape
    width = full // heads
    copies = fetch(
        [(b_hbm, b_ref), (c_hbm, c_ref), (gate_hbm, gate_ref), (x_hbm, x_ref)]
        + strips(w_hbm, w_ref, KEPT, CHUNKS), sems
    )
    for a in range(size // 8):
        for h in range(heads):
            both = back_ref[a * heads + h].astype(F32)
            state_ref[8 * a:8 * a + 8, h * width:(h + 1) * width] = both[0:8]
            adj_ref[8 * a:8 * a + 8, h * width:(h + 1) * width] = both[8:16]
    state = state_ref[...]
    adj = adj_ref[...]
    state_b = state.astype(BF)
    adj_b = adj.astype(BF)
    copies[0].wait()
    copies[1].wait()
    b = b_ref[...]
    c = c_ref[...]
    copies[2].wait()
    silu, g = gates(gate_ref)
    dg = dg_ref[...]
    downs = [downward(cum_ref, h) for h in range(heads)]
    ec = jnp.concatenate([jnp.exp(down) for down in downs], axis=1)
    tail = jnp.concatenate(
        [jnp.exp(cum_ref[h:h + 1, size - 1:size] - downs[h]) for h in range(heads)], axis=1
    )
    y_inter = mm(c, state_b) * ec
    y = yi_ref[...] + y_inter
    gated = (y * silu).astype(BF)
    core = lax.axis_index("tp") % 2
    places = []
    for i in range(size // piece // 2):
        for k in range(2):
            away = jnp.where(core == k, 0, 1)
            places.append((slice(piece * (2 * i + k), piece * (2 * i + k + 1)),
                           pl.ds(pl.multiple_of(size // 2 * (1 - away) + piece * i, piece), piece)))
    for src, dst in places:
        gated_ref[dst, :] = gated[src, :]
    gg_ref[...] = (dg * y * (g + silu * (1.0 - g))).astype(BF)
    gy = dg * silu
    gy_b = gy.astype(BF)
    gw = (gy * ec).astype(BF)
    sdx = mm(b, adj_b) * tail
    copies[3].wait()
    x = x_ref[...]
    through = x.astype(F32) * sdx
    entering = gy * y_inter
    scores = scores_ref[...]
    row, col = grid_of(size)
    sub = lax.broadcasted_iota(jnp.int32, (8, size), 0)
    dmix_sum = jnp.zeros((size, size), F32)
    columns = jnp.zeros((size, size), F32)
    lines = jnp.zeros((8, size), F32)
    closing = jnp.zeros((8, size), F32)
    product = adj * state
    for h in range(heads):
        at = slice(h * width, (h + 1) * width)
        gap = downs[h] - jnp.broadcast_to(cum_ref[h:h + 1, :], (size, size))
        mask = jnp.where(row >= col, jnp.exp(jnp.minimum(gap, 0.0)), 0.0)
        dmix = mm_nt(gy_b[:, at], x[:, at]) * mask
        dmix_sum = dmix_sum + dmix
        cross = dmix * scores
        gi_ref[:, at] = (mm(mixt_ref[h], gy_b[:, at]) + sdx[:, at]).astype(BF)
        down = jnp.sum(cross + entering[:, at] - through[:, at], axis=1, keepdims=True)
        columns = jnp.where(col == h, down, columns)
        lines = jnp.where(sub == h, jnp.sum(cross, axis=0, keepdims=True), lines)
        end = jnp.sum(jnp.sum(through[:, at], axis=0, keepdims=True), axis=1, keepdims=True)
        dots = jnp.sum(jnp.sum(product[:, at], axis=0, keepdims=True), axis=1, keepdims=True)
        closing = jnp.where(sub == h, end + dec_ref[h] * dots, closing)
    flow = jnp.transpose(columns)[0:8, :] - lines
    total = sum_by(flow, (row >= col).astype(BF)) + closing
    gd_ref[...] = total[0:heads, :]
    n = b.shape[1]
    grad_b = mm(jnp.transpose(dmix_sum).astype(BF), c) + mm_nt(wx_ref[...], adj_b)
    grad_c = mm(dmix_sum.astype(BF), b) + mm_nt(gw, state_b)
    half = size // 2
    out_width = w_hbm.shape[1]
    for src, dst in places:
        terms_ref[dst, 0:n] = grad_b[src, :]
        terms_ref[dst, n:2 * n] = grad_c[src, :]
    theirs_ref[:, out_width:out_width + 2 * n] = terms_ref[0:half, :].astype(BF)
    mine_ref[:, out_width:out_width + 2 * n] = terms_ref[half:size, :].astype(BF)
    step = out_width // CHUNKS
    gated = gated_ref[...]
    for i in range(CHUNKS):
        if i == KEPT or i == (KEPT + CHUNKS) // 2:
            for k in range(i, (KEPT + CHUNKS) // 2 if i == KEPT else CHUNKS):
                copies[4 + k - KEPT].wait()
        own = kept_ref if i < KEPT else w_ref
        at = (i if i < KEPT else i - KEPT) * step
        part = mm(gated, own[:, at:at + step]).astype(BF)
        theirs_ref[:, i * step:(i + 1) * step] = part[0:half, :]
        mine_ref[:, i * step:(i + 1) * step] = part[half:size, :]


def end_kernel(part_ref, out_ref, gb_ref, gc_ref):
    out_width = out_ref.shape[1]
    n = gb_ref.shape[1]
    total = part_ref[0].astype(F32)
    for i in range(1, part_ref.shape[0]):
        total = total + part_ref[i].astype(F32)
    out_ref[...] = total[:, 0:out_width].astype(BF)
    gb_ref[...] = total[:, out_width:out_width + n]
    gc_ref[...] = total[:, out_width + n:out_width + 2 * n]


def call(kernel, outs, count, remote=(), scratch=()):
    return pl.pallas_call(
        kernel,
        out_shape=tuple(jax.ShapeDtypeStruct(s, d) for s, d in outs),
        in_specs=[
            pl.BlockSpec(memory_space=pltpu.HBM if i in remote else pltpu.VMEM)
            for i in range(count)
        ],
        scratch_shapes=list(scratch),
        compiler_params=pltpu.CompilerParams(vmem_limit_bytes=VMEM_LIMIT),
    )


def local(inputs, gate_in, b_proj, c_proj, log_decay, w_out, cotangent):
    size, full = inputs.shape
    heads = log_decay.shape[0]
    n = b_proj.shape[1]
    tp = lax.axis_size("tp")
    chips = tp // 2
    workers = lax.axis_size("ctx")
    piece, out_width = cotangent.shape
    wide = ((size, full), F32)
    wide_b = ((size, full), BF)
    square = (heads, size, size)
    small = pltpu.VMEM((size, n), BF)
    kept_width = out_width // CHUNKS * KEPT
    weights = pltpu.VMEM((full, out_width - kept_width), BF)
    lanes = pltpu.VMEM((size, full), F32)
    rows = pltpu.VMEM((size, full), BF)
    across = [[2 * i + k for i in range(chips)] for k in range(2)]
    swap = [(i, i ^ 1) for i in range(tp)]

    near = lax.all_to_all(
        jnp.broadcast_to(cotangent[None], (chips, piece, out_width)),
        "tp", 0, 0, tiled=True, axis_index_groups=across,
    )
    far = lax.ppermute(near, "tp", swap)
    st, dec, cum, mixt, scores, yi, wx, kept = call(
        functools.partial(pre_kernel, heads),
        [((n, full), F32), ((heads, 8, size), F32), ((8, size), F32), (square, BF), ((size, size), F32),
         wide, wide_b, ((full, kept_width), BF)],
        5, range(5),
        [rows, small, small, pltpu.VMEM((heads, size), F32), pltpu.SemaphoreType.DMA((4 + KEPT,))],
    )(inputs, b_proj, c_proj, log_decay, w_out)
    msg, dg = call(
        functools.partial(mid_kernel, heads),
        [((workers * ROWS, size), BF), wide],
        9, (2, 3, 4),
        [weights, pltpu.VMEM((size, out_width), BF), small, rows,
         pltpu.SemaphoreType.DMA((2 + CHUNKS - KEPT,))],
    )(near, far, w_out, c_proj, gate_in, kept, cum, st, dec)
    msg = lax.all_to_all(msg.reshape(workers, ROWS // 2, 2, size), "ctx", 0, 0, tiled=True)
    msg = msg.reshape(workers * ROWS, size)
    (back,) = call(
        scan_kernel, [((workers, 16, size), BF)], 1, (),
        [pltpu.VMEM((workers, 8, size), F32), pltpu.VMEM((workers, 8, size), F32)],
    )(msg)
    back = lax.all_to_all(back, "ctx", 0, 0, tiled=True)
    half = ((size // 2, out_width + 2 * n), BF)
    mine, theirs, grad_inputs, grad_gate, grad_decay = call(
        functools.partial(fin_kernel, heads, piece),
        [half, half, wide_b, wide_b, ((heads, size), F32)],
        14, range(1, 6),
        [lanes, lanes, rows, pltpu.VMEM((size, 2 * n), F32), rows, small, small, rows, weights,
         pltpu.SemaphoreType.DMA((4 + CHUNKS - KEPT,))],
    )(back, inputs, b_proj, c_proj, w_out, gate_in, kept, dg, cum, mixt, scores, yi, wx, dec)
    part = (mine.astype(F32) + lax.ppermute(theirs, "tp", swap).astype(F32)).astype(BF)
    part = lax.all_to_all(
        part.reshape(chips, piece, out_width + 2 * n),
        "tp", 0, 0, tiled=True, axis_index_groups=across,
    )
    layer_out, grad_b, grad_c = call(
        end_kernel, [((piece, out_width), BF), ((piece, n), F32), ((piece, n), F32)], 1
    )(part)
    return (layer_out, grad_inputs, grad_gate, grad_b, grad_c, grad_decay)


def solution(mesh):
    in_specs = (
        P("ctx", "tp"),
        P("ctx", "tp"),
        P("ctx", None),
        P("ctx", None),
        P("tp", "ctx"),
        P("tp", None),
        P(("ctx", "tp"), None),
    )
    out_specs = (
        P(("ctx", "tp"), None),
        P("ctx", "tp"),
        P("ctx", "tp"),
        P(("ctx", "tp"), None),
        P(("ctx", "tp"), None),
        P("tp", "ctx"),
    )
    return jax.shard_map(local, mesh=mesh, in_specs=in_specs, out_specs=out_specs, check_vma=False)
```

```python
import functools

import jax
import jax.numpy as jnp
from jax import lax
from jax.experimental import pallas as pl
from jax.experimental.pallas import tpu as pltpu
from jax.sharding import PartitionSpec as P

BF = jnp.bfloat16
F32 = jnp.float32
NT = (((1,), (1,)), ((), ()))
VMEM_LIMIT = 48 * 1024 * 1024
ROWS = 18
CHUNKS = 8
KEPT = 4


def mm(a, b):
    return jnp.dot(a, b, preferred_element_type=F32)


def mm_nt(a, b):
    return lax.dot_general(a, b, NT, preferred_element_type=F32)


def flip(a):
    return jnp.transpose(a.astype(F32)).astype(BF)


def split(a):
    hi = a.astype(BF)
    rest = a - hi.astype(F32)
    mid = rest.astype(BF)
    return hi, mid, (rest - mid.astype(F32)).astype(BF)


def sum_by(a, ones):
    hi, mid, lo = split(a)
    return mm(hi, ones) + (mm(mid, ones) + mm(lo, ones))


def grid_of(size):
    return (
        lax.broadcasted_iota(jnp.int32, (size, size), 0),
        lax.broadcasted_iota(jnp.int32, (size, size), 1),
    )


def fetch(pairs, sems):
    copies = [pltpu.make_async_copy(src, dst, sems.at[i]) for i, (src, dst) in enumerate(pairs)]
    for copy in copies:
        copy.start()
    return copies


def strips(src, dst, first, last):
    step = src.shape[1] // CHUNKS
    return [
        (src.at[:, pl.ds(i * step, step)], dst.at[:, pl.ds((i - first) * step, step)])
        for i in range(first, last)
    ]


def downward(cum_ref, h):
    size = cum_ref.shape[1]
    return jnp.transpose(jnp.broadcast_to(cum_ref[h:h + 1, :], (size, size)))


def gates(gate_ref):
    v = gate_ref[...].astype(F32)
    g = 1.0 / (1.0 + jnp.exp(-v))
    return v * g, g


def pre_kernel(heads, x_hbm, b_hbm, c_hbm, ld_hbm, w_hbm,
               st_ref, dec_ref, cum_ref, mixt_ref, scores_ref, yi_ref, wx_ref, kept_ref,
               x_ref, b_ref, c_ref, ld_ref, sems):
    copies = fetch(
        [(ld_hbm, ld_ref), (b_hbm, b_ref), (c_hbm, c_ref), (x_hbm, x_ref)]
        + strips(w_hbm, kept_ref, 0, KEPT), sems
    )
    size = x_ref.shape[0]
    width = x_ref.shape[1] // heads
    row, col = grid_of(size)
    copies[0].wait()
    ld = jnp.concatenate([ld_ref[...], jnp.zeros((8 - heads, size), F32)], axis=0)
    cum = sum_by(ld, (row <= col).astype(BF))
    cum_ref[...] = cum
    copies[1].wait()
    copies[2].wait()
    scores = mm_nt(c_ref[...], b_ref[...])
    scores_ref[...] = scores
    b_t = flip(b_ref[...])
    copies[3].wait()
    for h in range(heads):
        at = slice(h * width, (h + 1) * width)
        across = jnp.broadcast_to(cum[h:h + 1, :], (size, size))
        down = jnp.transpose(across)
        mask = jnp.where(row >= col, jnp.exp(jnp.minimum(down - across, 0.0)), 0.0)
        mixing = scores * mask
        mixt_ref[h] = jnp.transpose(mixing).astype(BF)
        x = x_ref[:, at]
        yi_ref[:, at] = mm(mixing.astype(BF), x)
        last = cum[h:h + 1, size - 1:size]
        tail = jnp.exp(last - down)
        wx = (x.astype(F32) * tail).astype(BF)
        wx_ref[:, at] = wx
        st_ref[:, at] = mm(b_t, wx)
        dec_ref[h] = jnp.broadcast_to(jnp.exp(last), (8, size))
    for copy in copies[4:]:
        copy.wait()


def mid_kernel(heads, near_ref, far_ref, w_hbm, c_hbm, gate_hbm, kept_ref, cum_ref, st_ref, dec_ref,
               msg_ref, dg_ref, w_ref, cot_ref, c_ref, gate_ref, sems):
    chips, piece = near_ref.shape[:2]
    size, full = st_ref.shape
    width = full // heads
    chunk = w_hbm.shape[1] // CHUNKS
    copies = fetch(
        [(c_hbm, c_ref), (gate_hbm, gate_ref)] + strips(w_hbm, w_ref, KEPT, CHUNKS), sems
    )
    core = lax.axis_index("tp") % 2
    for s in range(chips):
        at = pl.multiple_of(piece * (2 * s + core), piece)
        cot_ref[pl.ds(at, piece), :] = near_ref[s]
        at = pl.multiple_of(piece * (2 * s + 1 - core), piece)
        cot_ref[pl.ds(at, piece), :] = far_ref[s]
    copies[0].wait()
    copies[1].wait()
    c_t = flip(c_ref[...])
    silu, g = gates(gate_ref)
    total = None
    for i in range(KEPT):
        own = slice(i * chunk, (i + 1) * chunk)
        term = mm_nt(cot_ref[:, own], kept_ref[:, own])
        total = term if total is None else total + term
    for i in range(KEPT, CHUNKS):
        copies[2 + i - KEPT].wait()
        own = slice((i - KEPT) * chunk, (i - KEPT + 1) * chunk)
        total = total + mm_nt(cot_ref[:, i * chunk:(i + 1) * chunk], w_ref[:, own])
    dg_ref[...] = total
    sub = lax.broadcasted_iota(jnp.int32, (2, size), 0)
    for h in range(heads):
        at = slice(h * width, (h + 1) * width)
        gw = (total[:, at] * silu[:, at] * jnp.exp(downward(cum_ref, h))).astype(BF)
        inj = mm(c_t, gw)
        decay = dec_ref[h][0:2, :]
        hi = decay.astype(BF).astype(F32)
        pair = jnp.where(sub == 0, hi, decay - hi).astype(BF)
        for a in range(size // 8):
            j = ROWS * (a * heads + h)
            both = jnp.concatenate([st_ref[8 * a:8 * a + 8, at], inj[8 * a:8 * a + 8, :]], axis=0)
            msg_ref[j:j + 16, :] = both.astype(BF)
            msg_ref[j + 16:j + 18, :] = pair


def scan_kernel(msg_ref, out_ref, dec_ref, state_ref):
    count = out_ref.shape[0]
    lanes = out_ref.shape[2]
    state = jnp.zeros((8, lanes), F32)
    for k in range(count):
        at = ROWS * k
        pair = msg_ref[at + 16:at + 18, :].astype(F32)
        decay = jnp.broadcast_to(jnp.sum(pair, axis=0, keepdims=True), (8, lanes))
        dec_ref[k] = decay
        state_ref[k] = state
        state = decay * state + msg_ref[at:at + 8, :].astype(F32)
    adjoint = jnp.zeros((8, lanes), F32)
    for k in reversed(range(count)):
        at = ROWS * k
        out_ref[k] = jnp.concatenate([state_ref[k], adjoint], axis=0).astype(BF)
        adjoint = dec_ref[k] * adjoint + msg_ref[at + 8:at + 16, :].astype(F32)


def unpack(heads, back_ref, state_ref, adj_ref):
    width = state_ref.shape[1] // heads
    for a in range(state_ref.shape[0] // 8):
        for h in range(heads):
            both = back_ref[a * heads + h].astype(F32)
            state_ref[8 * a:8 * a + 8, h * width:(h + 1) * width] = both[0:8]
            adj_ref[8 * a:8 * a + 8, h * width:(h + 1) * width] = both[8:16]


def mask_of(cum_ref, down, h, row, col):
    gap = down - jnp.broadcast_to(cum_ref[h:h + 1, :], down.shape)
    return jnp.where(row >= col, jnp.exp(jnp.minimum(gap, 0.0)), 0.0)


def fin_kernel(heads, piece, back_ref, x_hbm, b_hbm, c_hbm, w_hbm, gate_hbm, kept_ref, dg_ref, cum_ref,
               yi_ref, wx_ref, mine_ref, theirs_ref, state_ref, adj_ref,
               gated_ref, terms_ref, x_ref, b_ref, c_ref, gate_ref, w_ref, sems):
    size, full = x_ref.shape
    width = full // heads
    copies = fetch(
        [(b_hbm, b_ref), (c_hbm, c_ref), (gate_hbm, gate_ref), (x_hbm, x_ref)]
        + strips(w_hbm, w_ref, KEPT, CHUNKS), sems
    )
    unpack(heads, back_ref, state_ref, adj_ref)
    state_b = state_ref[...].astype(BF)
    adj_b = adj_ref[...].astype(BF)
    for copy in copies[0:4]:
        copy.wait()
    x = x_ref[...]
    b = b_ref[...]
    c = c_ref[...]
    silu, g = gates(gate_ref)
    downs = [downward(cum_ref, h) for h in range(heads)]
    ec = jnp.concatenate([jnp.exp(down) for down in downs], axis=1)
    gated = ((yi_ref[...] + mm(c, state_b) * ec) * silu).astype(BF)
    core = lax.axis_index("tp") % 2
    places = []
    for i in range(size // piece // 2):
        for k in range(2):
            away = jnp.where(core == k, 0, 1)
            places.append((slice(piece * (2 * i + k), piece * (2 * i + k + 1)),
                           pl.ds(pl.multiple_of(size // 2 * (1 - away) + piece * i, piece), piece)))
    for src, dst in places:
        gated_ref[dst, :] = gated[src, :]
    gy = dg_ref[...] * silu
    gy_b = gy.astype(BF)
    gw = (gy * ec).astype(BF)
    row, col = grid_of(size)
    dmix_sum = jnp.zeros((size, size), F32)
    for h in range(heads):
        at = slice(h * width, (h + 1) * width)
        mask = mask_of(cum_ref, downs[h], h, row, col)
        dmix_sum = dmix_sum + mm_nt(gy_b[:, at], x[:, at]) * mask
    n = b.shape[1]
    grad_b = mm(jnp.transpose(dmix_sum).astype(BF), c) + mm_nt(wx_ref[...], adj_b)
    grad_c = mm(dmix_sum.astype(BF), b) + mm_nt(gw, state_b)
    half = size // 2
    out_width = w_hbm.shape[1]
    for src, dst in places:
        terms_ref[dst, 0:n] = grad_b[src, :]
        terms_ref[dst, n:2 * n] = grad_c[src, :]
    theirs_ref[:, out_width:out_width + 2 * n] = terms_ref[0:half, :].astype(BF)
    mine_ref[:, out_width:out_width + 2 * n] = terms_ref[half:size, :].astype(BF)
    step = out_width // CHUNKS
    gated = gated_ref[...]
    for i in range(CHUNKS):
        if i == KEPT or i == (KEPT + CHUNKS) // 2:
            for k in range(i, (KEPT + CHUNKS) // 2 if i == KEPT else CHUNKS):
                copies[4 + k - KEPT].wait()
        own = kept_ref if i < KEPT else w_ref
        at = (i if i < KEPT else i - KEPT) * step
        part = mm(gated, own[:, at:at + step]).astype(BF)
        theirs_ref[:, i * step:(i + 1) * step] = part[0:half, :]
        mine_ref[:, i * step:(i + 1) * step] = part[half:size, :]


def rest_kernel(heads, back_ref, x_hbm, b_hbm, c_hbm, gate_hbm, dg_ref, cum_ref,
                mixt_ref, scores_ref, yi_ref, dec_ref,
                gi_ref, gg_ref, gd_ref, state_ref, adj_ref, x_ref, b_ref, c_ref, gate_ref, sems):
    size, full = x_ref.shape
    width = full // heads
    copies = fetch([(b_hbm, b_ref), (c_hbm, c_ref), (gate_hbm, gate_ref), (x_hbm, x_ref)], sems)
    unpack(heads, back_ref, state_ref, adj_ref)
    state = state_ref[...]
    adj = adj_ref[...]
    for copy in copies:
        copy.wait()
    x = x_ref[...]
    silu, g = gates(gate_ref)
    dg = dg_ref[...]
    downs = [downward(cum_ref, h) for h in range(heads)]
    ec = jnp.concatenate([jnp.exp(down) for down in downs], axis=1)
    tail = jnp.concatenate(
        [jnp.exp(cum_ref[h:h + 1, size - 1:size] - downs[h]) for h in range(heads)], axis=1
    )
    y_inter = mm(c_ref[...], state.astype(BF)) * ec
    gg_ref[...] = (dg * (yi_ref[...] + y_inter) * (g + silu * (1.0 - g))).astype(BF)
    gy = dg * silu
    gy_b = gy.astype(BF)
    sdx = mm(b_ref[...], adj.astype(BF)) * tail
    through = x.astype(F32) * sdx
    entering = gy * y_inter
    scores = scores_ref[...]
    row, col = grid_of(size)
    sub = lax.broadcasted_iota(jnp.int32, (8, size), 0)
    columns = jnp.zeros((size, size), F32)
    lines = jnp.zeros((8, size), F32)
    closing = jnp.zeros((8, size), F32)
    product = adj * state
    for h in range(heads):
        at = slice(h * width, (h + 1) * width)
        mask = mask_of(cum_ref, downs[h], h, row, col)
        cross = mm_nt(gy_b[:, at], x[:, at]) * mask * scores
        gi_ref[:, at] = (mm(mixt_ref[h], gy_b[:, at]) + sdx[:, at]).astype(BF)
        down = jnp.sum(cross + entering[:, at] - through[:, at], axis=1, keepdims=True)
        columns = jnp.where(col == h, down, columns)
        lines = jnp.where(sub == h, jnp.sum(cross, axis=0, keepdims=True), lines)
        end = jnp.sum(jnp.sum(through[:, at], axis=0, keepdims=True), axis=1, keepdims=True)
        dots = jnp.sum(jnp.sum(product[:, at], axis=0, keepdims=True), axis=1, keepdims=True)
        closing = jnp.where(sub == h, end + dec_ref[h] * dots, closing)
    flow = jnp.transpose(columns)[0:8, :] - lines
    total = sum_by(flow, (row >= col).astype(BF)) + closing
    gd_ref[...] = total[0:heads, :]


def end_kernel(part_ref, out_ref, gb_ref, gc_ref):
    out_width = out_ref.shape[1]
    n = gb_ref.shape[1]
    total = part_ref[0].astype(F32)
    for i in range(1, part_ref.shape[0]):
        total = total + part_ref[i].astype(F32)
    out_ref[...] = total[:, 0:out_width].astype(BF)
    gb_ref[...] = total[:, out_width:out_width + n]
    gc_ref[...] = total[:, out_width + n:out_width + 2 * n]


def call(kernel, outs, count, remote=(), scratch=()):
    return pl.pallas_call(
        kernel,
        out_shape=tuple(jax.ShapeDtypeStruct(s, d) for s, d in outs),
        in_specs=[
            pl.BlockSpec(memory_space=pltpu.HBM if i in remote else pltpu.VMEM)
            for i in range(count)
        ],
        scratch_shapes=list(scratch),
        compiler_params=pltpu.CompilerParams(vmem_limit_bytes=VMEM_LIMIT),
    )


def local(inputs, gate_in, b_proj, c_proj, log_decay, w_out, cotangent):
    size, full = inputs.shape
    heads = log_decay.shape[0]
    n = b_proj.shape[1]
    tp = lax.axis_size("tp")
    chips = tp // 2
    workers = lax.axis_size("ctx")
    piece, out_width = cotangent.shape
    wide = ((size, full), F32)
    wide_b = ((size, full), BF)
    square = (heads, size, size)
    small = pltpu.VMEM((size, n), BF)
    kept_width = out_width // CHUNKS * KEPT
    weights = pltpu.VMEM((full, out_width - kept_width), BF)
    lanes = pltpu.VMEM((size, full), F32)
    rows = pltpu.VMEM((size, full), BF)
    across = [[2 * i + k for i in range(chips)] for k in range(2)]
    swap = [(i, i ^ 1) for i in range(tp)]

    near = lax.all_to_all(
        jnp.broadcast_to(cotangent[None], (chips, piece, out_width)),
        "tp", 0, 0, tiled=True, axis_index_groups=across,
    )
    far = lax.ppermute(near, "tp", swap)
    st, dec, cum, mixt, scores, yi, wx, kept = call(
        functools.partial(pre_kernel, heads),
        [((n, full), F32), ((heads, 8, size), F32), ((8, size), F32), (square, BF), ((size, size), F32),
         wide, wide_b, ((full, kept_width), BF)],
        5, range(5),
        [rows, small, small, pltpu.VMEM((heads, size), F32), pltpu.SemaphoreType.DMA((4 + KEPT,))],
    )(inputs, b_proj, c_proj, log_decay, w_out)
    msg, dg = call(
        functools.partial(mid_kernel, heads),
        [((workers * ROWS, size), BF), wide],
        9, (2, 3, 4),
        [weights, pltpu.VMEM((size, out_width), BF), small, rows,
         pltpu.SemaphoreType.DMA((2 + CHUNKS - KEPT,))],
    )(near, far, w_out, c_proj, gate_in, kept, cum, st, dec)
    msg = lax.all_to_all(msg.reshape(workers, ROWS // 2, 2, size), "ctx", 0, 0, tiled=True)
    msg = msg.reshape(workers * ROWS, size)
    (back,) = call(
        scan_kernel, [((workers, 16, size), BF)], 1, (),
        [pltpu.VMEM((workers, 8, size), F32), pltpu.VMEM((workers, 8, size), F32)],
    )(msg)
    back = lax.all_to_all(back, "ctx", 0, 0, tiled=True)
    half = ((size // 2, out_width + 2 * n), BF)
    mine, theirs = call(
        functools.partial(fin_kernel, heads, piece),
        [half, half],
        11, range(1, 6),
        [lanes, lanes, rows, pltpu.VMEM((size, 2 * n), F32), rows, small, small, rows, weights,
         pltpu.SemaphoreType.DMA((4 + CHUNKS - KEPT,))],
    )(back, inputs, b_proj, c_proj, w_out, gate_in, kept, dg, cum, yi, wx)
    grad_inputs, grad_gate, grad_decay = call(
        functools.partial(rest_kernel, heads),
        [wide_b, wide_b, ((heads, size), F32)],
        11, range(1, 5),
        [lanes, lanes, rows, small, small, rows, pltpu.SemaphoreType.DMA((4,))],
    )(back, inputs, b_proj, c_proj, gate_in, dg, cum, mixt, scores, yi, dec)
    other, grad_inputs = lax.optimization_barrier((lax.ppermute(theirs, "tp", swap), grad_inputs))
    part = (mine.astype(F32) + other.astype(F32)).astype(BF)
    part = lax.all_to_all(
        part.reshape(chips, piece, out_width + 2 * n),
        "tp", 0, 0, tiled=True, axis_index_groups=across,
    )
    layer_out, grad_b, grad_c = call(
        end_kernel, [((piece, out_width), BF), ((piece, n), F32), ((piece, n), F32)], 1
    )(part)
    return (layer_out, grad_inputs, grad_gate, grad_b, grad_c, grad_decay)


def solution(mesh):
    in_specs = (
        P("ctx", "tp"),
        P("ctx", "tp"),
        P("ctx", None),
        P("ctx", None),
        P("tp", "ctx"),
        P("tp", None),
        P(("ctx", "tp"), None),
    )
    out_specs = (
        P(("ctx", "tp"), None),
        P("ctx", "tp"),
        P("ctx", "tp"),
        P(("ctx", "tp"), None),
        P(("ctx", "tp"), None),
        P("tp", "ctx"),
    )
    return jax.shard_map(local, mesh=mesh, in_specs=in_specs, out_specs=out_specs, check_vma=False)
```

```python
import functools

import jax
import jax.numpy as jnp
from jax import lax
from jax.experimental import pallas as pl
from jax.experimental.pallas import tpu as pltpu
from jax.sharding import PartitionSpec as P

BF = jnp.bfloat16
F32 = jnp.float32
NT = (((1,), (1,)), ((), ()))
VMEM_LIMIT = 48 * 1024 * 1024
ROWS = 10
CHUNKS = 8
KEPT = 4


def mm(a, b):
    return jnp.dot(a, b, preferred_element_type=F32)


def mm_nt(a, b):
    return lax.dot_general(a, b, NT, preferred_element_type=F32)


def flip(a):
    return jnp.transpose(a.astype(F32)).astype(BF)


def split(a):
    hi = a.astype(BF)
    rest = a - hi.astype(F32)
    mid = rest.astype(BF)
    return hi, mid, (rest - mid.astype(F32)).astype(BF)


def sum_by(a, ones):
    hi, mid, lo = split(a)
    return mm(hi, ones) + (mm(mid, ones) + mm(lo, ones))


def grid_of(size):
    return (
        lax.broadcasted_iota(jnp.int32, (size, size), 0),
        lax.broadcasted_iota(jnp.int32, (size, size), 1),
    )


def fetch(pairs, sems):
    copies = [pltpu.make_async_copy(src, dst, sems.at[i]) for i, (src, dst) in enumerate(pairs)]
    for copy in copies:
        copy.start()
    return copies


def strips(src, dst, first, last):
    step = src.shape[1] // CHUNKS
    return [
        (src.at[:, pl.ds(i * step, step)], dst.at[:, pl.ds((i - first) * step, step)])
        for i in range(first, last)
    ]


def downward(cum_ref, h):
    size = cum_ref.shape[1]
    return jnp.transpose(jnp.broadcast_to(cum_ref[h:h + 1, :], (size, size)))


def gates(gate_ref):
    v = gate_ref[...].astype(F32)
    g = 1.0 / (1.0 + jnp.exp(-v))
    return v * g, g


def send_kernel(heads, x_hbm, b_hbm, ld_hbm, msg_ref, cum_ref, wx_ref, dec_ref, x_ref, b_ref, ld_ref, sems):
    copies = fetch([(ld_hbm, ld_ref), (b_hbm, b_ref), (x_hbm, x_ref)], sems)
    size = x_ref.shape[0]
    width = x_ref.shape[1] // heads
    row, col = grid_of(size)
    copies[0].wait()
    ld = jnp.concatenate([ld_ref[...], jnp.zeros((8 - heads, size), F32)], axis=0)
    cum_ref[...] = sum_by(ld, (row <= col).astype(BF))
    copies[1].wait()
    b_t = flip(b_ref[...])
    copies[2].wait()
    sub = lax.broadcasted_iota(jnp.int32, (2, size), 0)
    for h in range(heads):
        at = slice(h * width, (h + 1) * width)
        last = cum_ref[h:h + 1, size - 1:size]
        wx = (x_ref[:, at].astype(F32) * jnp.exp(last - downward(cum_ref, h))).astype(BF)
        wx_ref[:, at] = wx
        state = mm(b_t, wx).astype(BF)
        decay = jnp.broadcast_to(jnp.exp(last), (8, size))
        dec_ref[h] = decay
        hi = decay[0:2, :].astype(BF).astype(F32)
        pair = jnp.where(sub == 0, hi, decay[0:2, :] - hi).astype(BF)
        for a in range(size // 8):
            j = ROWS * (a * heads + h)
            msg_ref[j:j + 8, :] = state[8 * a:8 * a + 8, :]
            msg_ref[j + 8:j + 10, :] = pair


def join_kernel(a_ref, b_ref, c_ref, d_ref, out_ref):
    piece = a_ref.shape[0]
    for i, ref in enumerate((a_ref, b_ref, c_ref, d_ref)):
        out_ref[i * piece:(i + 1) * piece, :] = ref[...]


def pre_kernel(heads, x_hbm, b_hbm, c_hbm, w_hbm, cum_ref,
               mixt_ref, scores_ref, yi_ref, kept_ref, x_ref, b_ref, c_ref, sems):
    copies = fetch(
        [(b_hbm, b_ref), (c_hbm, c_ref), (x_hbm, x_ref)] + strips(w_hbm, kept_ref, 0, KEPT), sems
    )
    size = x_ref.shape[0]
    width = x_ref.shape[1] // heads
    row, col = grid_of(size)
    for copy in copies[0:3]:
        copy.wait()
    scores = mm_nt(c_ref[...], b_ref[...])
    scores_ref[...] = scores
    for h in range(heads):
        at = slice(h * width, (h + 1) * width)
        mixing = scores * mask_of(cum_ref, downward(cum_ref, h), h, row, col)
        mixt_ref[h] = jnp.transpose(mixing).astype(BF)
        yi_ref[:, at] = mm(mixing.astype(BF), x_ref[:, at])
    for copy in copies[3:]:
        copy.wait()


def mid_kernel(heads, piece, near_ref, far_ref, w_hbm, c_hbm, gate_hbm, kept_ref, cum_ref,
               inj_ref, dg_ref, w_ref, cot_ref, c_ref, gate_ref, sems):
    chips = near_ref.shape[0] // piece
    size, full = gate_ref.shape
    width = full // heads
    chunk = w_hbm.shape[1] // CHUNKS
    copies = fetch(
        [(c_hbm, c_ref), (gate_hbm, gate_ref)] + strips(w_hbm, w_ref, KEPT, CHUNKS), sems
    )
    me = lax.axis_index("tp")
    core = me % 2
    for s in range(chips):
        src = 2 * ((me // 2 + chips - s) % chips)
        rows = slice(s * piece, (s + 1) * piece)
        cot_ref[pl.ds(pl.multiple_of(piece * (src + core), piece), piece), :] = near_ref[rows, :]
        cot_ref[pl.ds(pl.multiple_of(piece * (src + 1 - core), piece), piece), :] = far_ref[rows, :]
    copies[0].wait()
    copies[1].wait()
    c_t = flip(c_ref[...])
    silu, g = gates(gate_ref)
    total = None
    for i in range(KEPT):
        own = slice(i * chunk, (i + 1) * chunk)
        term = mm_nt(cot_ref[:, own], kept_ref[:, own])
        total = term if total is None else total + term
    for i in range(KEPT, CHUNKS):
        copies[2 + i - KEPT].wait()
        own = slice((i - KEPT) * chunk, (i - KEPT + 1) * chunk)
        total = total + mm_nt(cot_ref[:, i * chunk:(i + 1) * chunk], w_ref[:, own])
    dg_ref[...] = total
    for h in range(heads):
        at = slice(h * width, (h + 1) * width)
        gw = (total[:, at] * silu[:, at] * jnp.exp(downward(cum_ref, h))).astype(BF)
        inj_ref[:, at] = mm(c_t, gw)


def ahead_kernel(heads, msg_ref, inj_ref, out_ref, dec_ref):
    count = out_ref.shape[0]
    lanes = out_ref.shape[2]
    width = inj_ref.shape[1] // heads
    state = jnp.zeros((8, lanes), F32)
    for k in range(count):
        at = ROWS * k
        pair = msg_ref[at + 8:at + 10, :].astype(F32)
        decay = jnp.broadcast_to(jnp.sum(pair, axis=0, keepdims=True), (8, lanes))
        dec_ref[k] = decay
        a, h = k // heads, k % heads
        inj = inj_ref[8 * a:8 * a + 8, h * width:(h + 1) * width]
        out_ref[k] = jnp.concatenate([state, inj], axis=0).astype(BF)
        state = decay * state + msg_ref[at:at + 8, :].astype(F32)


def turn_kernel(heads, piece, both_ref, decays_ref, c_hbm, w_hbm, gate_hbm, kept_ref, cum_ref, yi_ref,
                mine_ref, theirs_ref, back_ref, state_ref,
                gated_ref, c_ref, gate_ref, w_ref, sems):
    size, full = yi_ref.shape
    width = full // heads
    copies = fetch([(c_hbm, c_ref), (gate_hbm, gate_ref)] + strips(w_hbm, w_ref, KEPT, CHUNKS), sems)
    adjoint = jnp.zeros((8, both_ref.shape[2]), F32)
    for k in reversed(range(both_ref.shape[0])):
        both = both_ref[k].astype(F32)
        a, h = k // heads, k % heads
        state_ref[8 * a:8 * a + 8, h * width:(h + 1) * width] = both[0:8]
        back_ref[k] = adjoint.astype(BF)
        adjoint = decays_ref[k] * adjoint + both[8:16]
    copies[0].wait()
    copies[1].wait()
    silu, g = gates(gate_ref)
    ec = jnp.concatenate([jnp.exp(downward(cum_ref, h)) for h in range(heads)], axis=1)
    state_b = state_ref[...].astype(BF)
    gated = ((yi_ref[...] + mm(c_ref[...], state_b) * ec) * silu).astype(BF)
    core = lax.axis_index("tp") % 2
    half = size // 2
    for i in range(half // piece):
        for k in range(2):
            away = jnp.where(core == k, 0, 1)
            dst = pl.ds(pl.multiple_of(half * (1 - away) + piece * i, piece), piece)
            gated_ref[dst, :] = gated[piece * (2 * i + k):piece * (2 * i + k + 1), :]
    step = w_hbm.shape[1] // CHUNKS
    gated = gated_ref[...]
    for i in range(CHUNKS):
        if i == KEPT:
            for copy in copies[2:]:
                copy.wait()
        own = kept_ref if i < KEPT else w_ref
        at = (i if i < KEPT else i - KEPT) * step
        part = mm(gated, own[:, at:at + step]).astype(BF)
        theirs_ref[:, i * step:(i + 1) * step] = part[0:half, :]
        mine_ref[:, i * step:(i + 1) * step] = part[half:size, :]


def pair_kernel(piece, mine_ref, other_ref, own_ref, one_ref, two_ref, three_ref):
    chips = mine_ref.shape[0] // piece
    chip = lax.axis_index("tp") // 2
    for s, ref in enumerate((own_ref, one_ref, two_ref, three_ref)):
        at = pl.ds(pl.multiple_of(piece * ((chip + s) % chips), piece), piece)
        ref[...] = (mine_ref[at, :].astype(F32) + other_ref[at, :].astype(F32)).astype(BF)


def total_kernel(a_ref, b_ref, c_ref, d_ref, out_ref):
    total = a_ref[...].astype(F32) + b_ref[...].astype(F32)
    out_ref[...] = (total + (c_ref[...].astype(F32) + d_ref[...].astype(F32))).astype(BF)


def unpack(heads, back_ref, adj_ref):
    width = adj_ref.shape[1] // heads
    for a in range(adj_ref.shape[0] // 8):
        for h in range(heads):
            tile = back_ref[a * heads + h].astype(F32)
            adj_ref[8 * a:8 * a + 8, h * width:(h + 1) * width] = tile


def mask_of(cum_ref, down, h, row, col):
    gap = down - jnp.broadcast_to(cum_ref[h:h + 1, :], down.shape)
    return jnp.where(row >= col, jnp.exp(jnp.minimum(gap, 0.0)), 0.0)


def fin_kernel(heads, back_ref, x_hbm, b_hbm, c_hbm, gate_hbm, dg_ref, cum_ref, wx_ref, state_ref,
               terms_ref, adj_ref, x_ref, b_ref, c_ref, gate_ref, sems):
    size, full = x_ref.shape
    width = full // heads
    copies = fetch([(b_hbm, b_ref), (c_hbm, c_ref), (gate_hbm, gate_ref), (x_hbm, x_ref)], sems)
    unpack(heads, back_ref, adj_ref)
    state_b = state_ref[...].astype(BF)
    adj_b = adj_ref[...].astype(BF)
    for copy in copies:
        copy.wait()
    x = x_ref[...]
    silu, g = gates(gate_ref)
    gy = dg_ref[...] * silu
    gy_b = gy.astype(BF)
    row, col = grid_of(size)
    dmix_sum = jnp.zeros((size, size), F32)
    ecs = []
    for h in range(heads):
        at = slice(h * width, (h + 1) * width)
        down = downward(cum_ref, h)
        ecs.append(jnp.exp(down))
        dmix_sum = dmix_sum + mm_nt(gy_b[:, at], x[:, at]) * mask_of(cum_ref, down, h, row, col)
    gw = (gy * jnp.concatenate(ecs, axis=1)).astype(BF)
    n = b_ref.shape[1]
    grad_b = mm(jnp.transpose(dmix_sum).astype(BF), c_ref[...]) + mm_nt(wx_ref[...], adj_b)
    grad_c = mm(dmix_sum.astype(BF), b_ref[...]) + mm_nt(gw, state_b)
    terms_ref[:, 0:n] = grad_b.astype(BF)
    terms_ref[:, n:2 * n] = grad_c.astype(BF)


def rest_kernel(heads, back_ref, x_hbm, b_hbm, c_hbm, gate_hbm, dg_ref, cum_ref,
                mixt_ref, scores_ref, yi_ref, dec_ref, state_ref,
                gi_ref, gg_ref, gd_ref, adj_ref, x_ref, b_ref, c_ref, gate_ref, sems):
    size, full = x_ref.shape
    width = full // heads
    copies = fetch([(b_hbm, b_ref), (c_hbm, c_ref), (gate_hbm, gate_ref), (x_hbm, x_ref)], sems)
    unpack(heads, back_ref, adj_ref)
    state = state_ref[...]
    adj = adj_ref[...]
    for copy in copies:
        copy.wait()
    x = x_ref[...]
    silu, g = gates(gate_ref)
    dg = dg_ref[...]
    downs = [downward(cum_ref, h) for h in range(heads)]
    ec = jnp.concatenate([jnp.exp(down) for down in downs], axis=1)
    tail = jnp.concatenate(
        [jnp.exp(cum_ref[h:h + 1, size - 1:size] - downs[h]) for h in range(heads)], axis=1
    )
    y_inter = mm(c_ref[...], state.astype(BF)) * ec
    gg_ref[...] = (dg * (yi_ref[...] + y_inter) * (g + silu * (1.0 - g))).astype(BF)
    gy = dg * silu
    gy_b = gy.astype(BF)
    sdx = mm(b_ref[...], adj.astype(BF)) * tail
    through = x.astype(F32) * sdx
    entering = gy * y_inter
    scores = scores_ref[...]
    row, col = grid_of(size)
    sub = lax.broadcasted_iota(jnp.int32, (8, size), 0)
    columns = jnp.zeros((size, size), F32)
    lines = jnp.zeros((8, size), F32)
    closing = jnp.zeros((8, size), F32)
    product = adj * state
    for h in range(heads):
        at = slice(h * width, (h + 1) * width)
        mask = mask_of(cum_ref, downs[h], h, row, col)
        cross = mm_nt(gy_b[:, at], x[:, at]) * mask * scores
        gi_ref[:, at] = (mm(mixt_ref[h], gy_b[:, at]) + sdx[:, at]).astype(BF)
        down = jnp.sum(cross + entering[:, at] - through[:, at], axis=1, keepdims=True)
        columns = jnp.where(col == h, down, columns)
        lines = jnp.where(sub == h, jnp.sum(cross, axis=0, keepdims=True), lines)
        end = jnp.sum(jnp.sum(through[:, at], axis=0, keepdims=True), axis=1, keepdims=True)
        dots = jnp.sum(jnp.sum(product[:, at], axis=0, keepdims=True), axis=1, keepdims=True)
        closing = jnp.where(sub == h, end + dec_ref[h] * dots, closing)
    flow = jnp.transpose(columns)[0:8, :] - lines
    total = sum_by(flow, (row >= col).astype(BF)) + closing
    gd_ref[...] = total[0:heads, :]


def end_kernel(part_ref, gb_ref, gc_ref):
    n = gb_ref.shape[1]
    total = part_ref[0].astype(F32)
    for i in range(1, part_ref.shape[0]):
        total = total + part_ref[i].astype(F32)
    gb_ref[...] = total[:, 0:n]
    gc_ref[...] = total[:, n:2 * n]


def call(kernel, outs, count, remote=(), scratch=()):
    return pl.pallas_call(
        kernel,
        out_shape=tuple(jax.ShapeDtypeStruct(s, d) for s, d in outs),
        in_specs=[
            pl.BlockSpec(memory_space=pltpu.HBM if i in remote else pltpu.VMEM)
            for i in range(count)
        ],
        scratch_shapes=list(scratch),
        compiler_params=pltpu.CompilerParams(vmem_limit_bytes=VMEM_LIMIT),
    )


def local(inputs, gate_in, b_proj, c_proj, log_decay, w_out, cotangent):
    size, full = inputs.shape
    heads = log_decay.shape[0]
    n = b_proj.shape[1]
    tp = lax.axis_size("tp")
    chips = tp // 2
    workers = lax.axis_size("ctx")
    piece, out_width = cotangent.shape
    wide = ((size, full), F32)
    wide_b = ((size, full), BF)
    square = (heads, size, size)
    small = pltpu.VMEM((size, n), BF)
    kept_width = out_width // CHUNKS * KEPT
    weights = pltpu.VMEM((full, out_width - kept_width), BF)
    lanes = pltpu.VMEM((size, full), F32)
    rows = pltpu.VMEM((size, full), BF)
    swap = [(i, i ^ 1) for i in range(tp)]
    strip_sems = pltpu.SemaphoreType.DMA((4 + CHUNKS - KEPT,))
    slab = ((piece, out_width), BF)

    def turn(s):
        return [(2 * i + k, 2 * ((i + s) % chips) + k) for i in range(chips) for k in range(2)]

    def spread(a):
        return lax.all_to_all(a, "ctx", 0, 0, tiled=True)

    pieces = [cotangent] + [lax.ppermute(cotangent, "tp", turn(s)) for s in range(1, chips)]
    msg, cum, wx, dec = call(
        functools.partial(send_kernel, heads),
        [((workers * ROWS, size), BF), ((8, size), F32), wide_b, ((heads, 8, size), F32)],
        3, range(3), [rows, small, pltpu.VMEM((heads, size), F32), strip_sems],
    )(inputs, b_proj, log_decay)
    pieces, msg = lax.optimization_barrier((pieces, msg))
    msg = spread(msg.reshape(workers, ROWS // 2, 2, size)).reshape(workers * ROWS, size)
    (near,) = call(join_kernel, [((size // 2, out_width), BF)], 4)(*pieces)
    far = lax.ppermute(near, "tp", swap)
    mixt, scores, yi, kept = call(
        functools.partial(pre_kernel, heads),
        [(square, BF), ((size, size), F32), wide, ((full, kept_width), BF)],
        5, range(4), [rows, small, small, pltpu.SemaphoreType.DMA((3 + KEPT,))],
    )(inputs, b_proj, c_proj, w_out, cum)
    inj, dg = call(
        functools.partial(mid_kernel, heads, piece),
        [((n, full), F32), wide],
        7, (2, 3, 4), [weights, pltpu.VMEM((size, out_width), BF), small, rows, strip_sems],
    )(near, far, w_out, c_proj, gate_in, kept, cum)
    both, decays = call(
        functools.partial(ahead_kernel, heads),
        [((workers, 16, size), BF), ((workers, 8, size), F32)], 2,
    )(msg, inj)
    both = spread(both)
    half = ((size // 2, out_width), BF)
    mine, theirs, back, state = call(
        functools.partial(turn_kernel, heads, piece),
        [half, half, ((workers, 8, size), BF), wide],
        8, (2, 3, 4), [rows, small, rows, weights, strip_sems],
    )(both, decays, c_proj, w_out, gate_in, kept, cum, yi)
    other = lax.ppermute(theirs, "tp", swap)
    back = spread(back)
    sums = call(functools.partial(pair_kernel, piece), [slab] * chips, 2)(mine, other)
    sums = [sums[0]] + [lax.ppermute(sums[s], "tp", turn(s)) for s in range(1, chips)]
    (layer_out,) = call(total_kernel, [slab], 4)(*sums)
    (terms,) = call(
        functools.partial(fin_kernel, heads), [((size, 2 * n), BF)],
        9, range(1, 5), [lanes, rows, small, small, rows, strip_sems],
    )(back, inputs, b_proj, c_proj, gate_in, dg, cum, wx, state)
    terms = lax.all_to_all(terms.reshape(tp, piece, 2 * n), "tp", 0, 0, tiled=True)
    grad_inputs, grad_gate, grad_decay = call(
        functools.partial(rest_kernel, heads),
        [wide_b, wide_b, ((heads, size), F32)],
        12, range(1, 5), [lanes, rows, small, small, rows, strip_sems],
    )(back, inputs, b_proj, c_proj, gate_in, dg, cum, mixt, scores, yi, dec, state)
    grad_b, grad_c = call(end_kernel, [((piece, n), F32), ((piece, n), F32)], 1)(terms)
    return (layer_out, grad_inputs, grad_gate, grad_b, grad_c, grad_decay)


def solution(mesh):
    in_specs = (
        P("ctx", "tp"),
        P("ctx", "tp"),
        P("ctx", None),
        P("ctx", None),
        P("tp", "ctx"),
        P("tp", None),
        P(("ctx", "tp"), None),
    )
    out_specs = (
        P(("ctx", "tp"), None),
        P("ctx", "tp"),
        P("ctx", "tp"),
        P(("ctx", "tp"), None),
        P(("ctx", "tp"), None),
        P("tp", "ctx"),
    )
    return jax.shard_map(local, mesh=mesh, in_specs=in_specs, out_specs=out_specs, check_vma=False)
```

```python
import functools

import jax
import jax.numpy as jnp
from jax import lax
from jax.experimental import pallas as pl
from jax.experimental.pallas import tpu as pltpu
from jax.sharding import PartitionSpec as P

BF = jnp.bfloat16
F32 = jnp.float32
NT = (((1,), (1,)), ((), ()))
VMEM_LIMIT = 48 * 1024 * 1024
ROWS = 18
CHUNKS = 8
KEPT = 5


def mm(a, b):
    return jnp.dot(a, b, preferred_element_type=F32)


def mm_nt(a, b):
    return lax.dot_general(a, b, NT, preferred_element_type=F32)


def flip(a):
    return jnp.transpose(a.astype(F32)).astype(BF)


def split(a):
    hi = a.astype(BF)
    rest = a - hi.astype(F32)
    mid = rest.astype(BF)
    return hi, mid, (rest - mid.astype(F32)).astype(BF)


def sum_by(a, ones):
    hi, mid, lo = split(a)
    return mm(hi, ones) + (mm(mid, ones) + mm(lo, ones))


def grid_of(size):
    return (
        lax.broadcasted_iota(jnp.int32, (size, size), 0),
        lax.broadcasted_iota(jnp.int32, (size, size), 1),
    )


def fetch(pairs, sems):
    copies = [pltpu.make_async_copy(src, dst, sems.at[i]) for i, (src, dst) in enumerate(pairs)]
    for copy in copies:
        copy.start()
    return copies


def strips(src, dst, first, last):
    step = src.shape[1] // CHUNKS
    return [
        (src.at[:, pl.ds(i * step, step)], dst.at[:, pl.ds((i - first) * step, step)])
        for i in range(first, last)
    ]


def downward(cum_ref, h):
    size = cum_ref.shape[1]
    return jnp.transpose(jnp.broadcast_to(cum_ref[h:h + 1, :], (size, size)))


def gates(gate_ref):
    v = gate_ref[...].astype(F32)
    g = 1.0 / (1.0 + jnp.exp(-v))
    return v * g, g


def pre_kernel(heads, x_hbm, b_hbm, c_hbm, ld_hbm, w_hbm,
               st_ref, dec_ref, cum_ref, mixt_ref, scores_ref, yi_ref, wx_ref, kept_ref,
               x_ref, b_ref, c_ref, ld_ref, sems):
    copies = fetch(
        [(ld_hbm, ld_ref), (b_hbm, b_ref), (c_hbm, c_ref), (x_hbm, x_ref)]
        + strips(w_hbm, kept_ref, 0, KEPT), sems
    )
    size = x_ref.shape[0]
    width = x_ref.shape[1] // heads
    row, col = grid_of(size)
    copies[0].wait()
    ld = jnp.concatenate([ld_ref[...], jnp.zeros((8 - heads, size), F32)], axis=0)
    cum = sum_by(ld, (row <= col).astype(BF))
    cum_ref[...] = cum
    copies[1].wait()
    copies[2].wait()
    scores = mm_nt(c_ref[...], b_ref[...])
    scores_ref[...] = scores
    b_t = flip(b_ref[...])
    copies[3].wait()
    for h in range(heads):
        at = slice(h * width, (h + 1) * width)
        across = jnp.broadcast_to(cum[h:h + 1, :], (size, size))
        down = jnp.transpose(across)
        mask = jnp.where(row >= col, jnp.exp(jnp.minimum(down - across, 0.0)), 0.0)
        mixing = scores * mask
        mixt_ref[h] = jnp.transpose(mixing).astype(BF)
        x = x_ref[:, at]
        yi_ref[:, at] = mm(mixing.astype(BF), x)
        last = cum[h:h + 1, size - 1:size]
        tail = jnp.exp(last - down)
        wx = (x.astype(F32) * tail).astype(BF)
        wx_ref[:, at] = wx
        st_ref[:, at] = mm(b_t, wx)
        dec_ref[h] = jnp.broadcast_to(jnp.exp(last), (8, size))
    for copy in copies[4:]:
        copy.wait()


def mid_kernel(heads, near_ref, far_ref, w_hbm, c_hbm, gate_hbm, kept_ref, cum_ref, st_ref, dec_ref,
               msg_ref, dg_ref, w_ref, cot_ref, c_ref, gate_ref, sems):
    chips, piece = near_ref.shape[:2]
    size, full = st_ref.shape
    width = full // heads
    chunk = w_hbm.shape[1] // CHUNKS
    copies = fetch(
        [(c_hbm, c_ref), (gate_hbm, gate_ref)] + strips(w_hbm, w_ref, KEPT, CHUNKS), sems
    )
    core = lax.axis_index("tp") % 2
    for s in range(chips):
        at = pl.multiple_of(piece * (2 * s + core), piece)
        cot_ref[pl.ds(at, piece), :] = near_ref[s]
        at = pl.multiple_of(piece * (2 * s + 1 - core), piece)
        cot_ref[pl.ds(at, piece), :] = far_ref[s]
    copies[0].wait()
    copies[1].wait()
    c_t = flip(c_ref[...])
    silu, g = gates(gate_ref)
    total = None
    for i in range(KEPT):
        own = slice(i * chunk, (i + 1) * chunk)
        term = mm_nt(cot_ref[:, own], kept_ref[:, own])
        total = term if total is None else total + term
    for i in range(KEPT, CHUNKS):
        copies[2 + i - KEPT].wait()
        own = slice((i - KEPT) * chunk, (i - KEPT + 1) * chunk)
        total = total + mm_nt(cot_ref[:, i * chunk:(i + 1) * chunk], w_ref[:, own])
    dg_ref[...] = total
    sub = lax.broadcasted_iota(jnp.int32, (2, size), 0)
    for h in range(heads):
        at = slice(h * width, (h + 1) * width)
        gw = (total[:, at] * silu[:, at] * jnp.exp(downward(cum_ref, h))).astype(BF)
        inj = mm(c_t, gw)
        decay = dec_ref[h][0:2, :]
        hi = decay.astype(BF).astype(F32)
        pair = jnp.where(sub == 0, hi, decay - hi).astype(BF)
        for a in range(size // 8):
            j = ROWS * (a * heads + h)
            both = jnp.concatenate([st_ref[8 * a:8 * a + 8, at], inj[8 * a:8 * a + 8, :]], axis=0)
            msg_ref[j:j + 16, :] = both.astype(BF)
            msg_ref[j + 16:j + 18, :] = pair


def scan_kernel(msg_ref, out_ref, dec_ref, state_ref):
    count = out_ref.shape[0]
    lanes = out_ref.shape[2]
    state = jnp.zeros((8, lanes), F32)
    for k in range(count):
        at = ROWS * k
        pair = msg_ref[at + 16:at + 18, :].astype(F32)
        decay = jnp.broadcast_to(jnp.sum(pair, axis=0, keepdims=True), (8, lanes))
        dec_ref[k] = decay
        state_ref[k] = state
        state = decay * state + msg_ref[at:at + 8, :].astype(F32)
    adjoint = jnp.zeros((8, lanes), F32)
    for k in reversed(range(count)):
        at = ROWS * k
        out_ref[k] = jnp.concatenate([state_ref[k], adjoint], axis=0).astype(BF)
        adjoint = dec_ref[k] * adjoint + msg_ref[at + 8:at + 16, :].astype(F32)


def unpack(heads, back_ref, state_ref, adj_ref):
    width = state_ref.shape[1] // heads
    for a in range(state_ref.shape[0] // 8):
        for h in range(heads):
            both = back_ref[a * heads + h].astype(F32)
            state_ref[8 * a:8 * a + 8, h * width:(h + 1) * width] = both[0:8]
            adj_ref[8 * a:8 * a + 8, h * width:(h + 1) * width] = both[8:16]


def mask_of(cum_ref, down, h, row, col):
    gap = down - jnp.broadcast_to(cum_ref[h:h + 1, :], down.shape)
    return jnp.where(row >= col, jnp.exp(jnp.minimum(gap, 0.0)), 0.0)


def fin_kernel(heads, piece, back_ref, x_hbm, b_hbm, c_hbm, w_hbm, gate_hbm, kept_ref, dg_ref, cum_ref,
               yi_ref, wx_ref, mine_ref, theirs_ref, state_ref, adj_ref,
               gated_ref, terms_ref, x_ref, b_ref, c_ref, gate_ref, w_ref, sems):
    size, full = x_ref.shape
    width = full // heads
    copies = fetch(
        [(b_hbm, b_ref), (c_hbm, c_ref), (gate_hbm, gate_ref), (x_hbm, x_ref)]
        + strips(w_hbm, w_ref, KEPT, CHUNKS), sems
    )
    unpack(heads, back_ref, state_ref, adj_ref)
    state_b = state_ref[...].astype(BF)
    adj_b = adj_ref[...].astype(BF)
    for copy in copies[0:4]:
        copy.wait()
    x = x_ref[...]
    b = b_ref[...]
    c = c_ref[...]
    silu, g = gates(gate_ref)
    downs = [downward(cum_ref, h) for h in range(heads)]
    ec = jnp.concatenate([jnp.exp(down) for down in downs], axis=1)
    gated = ((yi_ref[...] + mm(c, state_b) * ec) * silu).astype(BF)
    core = lax.axis_index("tp") % 2
    places = []
    for i in range(size // piece // 2):
        for k in range(2):
            away = jnp.where(core == k, 0, 1)
            places.append((slice(piece * (2 * i + k), piece * (2 * i + k + 1)),
                           pl.ds(pl.multiple_of(size // 2 * (1 - away) + piece * i, piece), piece)))
    for src, dst in places:
        gated_ref[dst, :] = gated[src, :]
    gy = dg_ref[...] * silu
    gy_b = gy.astype(BF)
    gw = (gy * ec).astype(BF)
    row, col = grid_of(size)
    dmix_sum = jnp.zeros((size, size), F32)
    for h in range(heads):
        at = slice(h * width, (h + 1) * width)
        mask = mask_of(cum_ref, downs[h], h, row, col)
        dmix_sum = dmix_sum + mm_nt(gy_b[:, at], x[:, at]) * mask
    n = b.shape[1]
    grad_b = mm(jnp.transpose(dmix_sum).astype(BF), c) + mm_nt(wx_ref[...], adj_b)
    grad_c = mm(dmix_sum.astype(BF), b) + mm_nt(gw, state_b)
    half = size // 2
    out_width = w_hbm.shape[1]
    for src, dst in places:
        terms_ref[dst, 0:n] = grad_b[src, :]
        terms_ref[dst, n:2 * n] = grad_c[src, :]
    theirs_ref[:, out_width:out_width + 2 * n] = terms_ref[0:half, :].astype(BF)
    mine_ref[:, out_width:out_width + 2 * n] = terms_ref[half:size, :].astype(BF)
    step = out_width // CHUNKS
    gated = gated_ref[...]
    for i in range(CHUNKS):
        if i == KEPT or i == (KEPT + CHUNKS) // 2:
            for k in range(i, (KEPT + CHUNKS) // 2 if i == KEPT else CHUNKS):
                copies[4 + k - KEPT].wait()
        own = kept_ref if i < KEPT else w_ref
        at = (i if i < KEPT else i - KEPT) * step
        part = mm(gated, own[:, at:at + step]).astype(BF)
        theirs_ref[:, i * step:(i + 1) * step] = part[0:half, :]
        mine_ref[:, i * step:(i + 1) * step] = part[half:size, :]


def rest_kernel(heads, back_ref, x_hbm, b_hbm, c_hbm, gate_hbm, dg_ref, cum_ref,
                mixt_ref, scores_ref, yi_ref, dec_ref,
                gi_ref, gg_ref, gd_ref, state_ref, adj_ref, x_ref, b_ref, c_ref, gate_ref, sems):
    size, full = x_ref.shape
    width = full // heads
    copies = fetch([(b_hbm, b_ref), (c_hbm, c_ref), (gate_hbm, gate_ref), (x_hbm, x_ref)], sems)
    unpack(heads, back_ref, state_ref, adj_ref)
    state = state_ref[...]
    adj = adj_ref[...]
    for copy in copies:
        copy.wait()
    x = x_ref[...]
    silu, g = gates(gate_ref)
    dg = dg_ref[...]
    downs = [downward(cum_ref, h) for h in range(heads)]
    ec = jnp.concatenate([jnp.exp(down) for down in downs], axis=1)
    tail = jnp.concatenate(
        [jnp.exp(cum_ref[h:h + 1, size - 1:size] - downs[h]) for h in range(heads)], axis=1
    )
    y_inter = mm(c_ref[...], state.astype(BF)) * ec
    gg_ref[...] = (dg * (yi_ref[...] + y_inter) * (g + silu * (1.0 - g))).astype(BF)
    gy = dg * silu
    gy_b = gy.astype(BF)
    sdx = mm(b_ref[...], adj.astype(BF)) * tail
    through = x.astype(F32) * sdx
    entering = gy * y_inter
    scores = scores_ref[...]
    row, col = grid_of(size)
    sub = lax.broadcasted_iota(jnp.int32, (8, size), 0)
    columns = jnp.zeros((size, size), F32)
    lines = jnp.zeros((8, size), F32)
    closing = jnp.zeros((8, size), F32)
    product = adj * state
    for h in range(heads):
        at = slice(h * width, (h + 1) * width)
        mask = mask_of(cum_ref, downs[h], h, row, col)
        cross = mm_nt(gy_b[:, at], x[:, at]) * mask * scores
        gi_ref[:, at] = (mm(mixt_ref[h], gy_b[:, at]) + sdx[:, at]).astype(BF)
        down = jnp.sum(cross + entering[:, at] - through[:, at], axis=1, keepdims=True)
        columns = jnp.where(col == h, down, columns)
        lines = jnp.where(sub == h, jnp.sum(cross, axis=0, keepdims=True), lines)
        end = jnp.sum(jnp.sum(through[:, at], axis=0, keepdims=True), axis=1, keepdims=True)
        dots = jnp.sum(jnp.sum(product[:, at], axis=0, keepdims=True), axis=1, keepdims=True)
        closing = jnp.where(sub == h, end + dec_ref[h] * dots, closing)
    flow = jnp.transpose(columns)[0:8, :] - lines
    total = sum_by(flow, (row >= col).astype(BF)) + closing
    gd_ref[...] = total[0:heads, :]


def end_kernel(part_ref, out_ref, gb_ref, gc_ref):
    out_width = out_ref.shape[1]
    n = gb_ref.shape[1]
    total = part_ref[0].astype(F32)
    for i in range(1, part_ref.shape[0]):
        total = total + part_ref[i].astype(F32)
    out_ref[...] = total[:, 0:out_width].astype(BF)
    gb_ref[...] = total[:, out_width:out_width + n]
    gc_ref[...] = total[:, out_width + n:out_width + 2 * n]


def call(kernel, outs, count, remote=(), scratch=()):
    return pl.pallas_call(
        kernel,
        out_shape=tuple(jax.ShapeDtypeStruct(s, d) for s, d in outs),
        in_specs=[
            pl.BlockSpec(memory_space=pltpu.HBM if i in remote else pltpu.VMEM)
            for i in range(count)
        ],
        scratch_shapes=list(scratch),
        compiler_params=pltpu.CompilerParams(vmem_limit_bytes=VMEM_LIMIT),
    )


def local(inputs, gate_in, b_proj, c_proj, log_decay, w_out, cotangent):
    size, full = inputs.shape
    heads = log_decay.shape[0]
    n = b_proj.shape[1]
    tp = lax.axis_size("tp")
    chips = tp // 2
    workers = lax.axis_size("ctx")
    piece, out_width = cotangent.shape
    wide = ((size, full), F32)
    wide_b = ((size, full), BF)
    square = (heads, size, size)
    small = pltpu.VMEM((size, n), BF)
    kept_width = out_width // CHUNKS * KEPT
    weights = pltpu.VMEM((full, out_width - kept_width), BF)
    lanes = pltpu.VMEM((size, full), F32)
    rows = pltpu.VMEM((size, full), BF)
    across = [[2 * i + k for i in range(chips)] for k in range(2)]
    swap = [(i, i ^ 1) for i in range(tp)]

    near = lax.all_to_all(
        jnp.broadcast_to(cotangent[None], (chips, piece, out_width)),
        "tp", 0, 0, tiled=True, axis_index_groups=across,
    )
    far = lax.ppermute(near, "tp", swap)
    st, dec, cum, mixt, scores, yi, wx, kept = call(
        functools.partial(pre_kernel, heads),
        [((n, full), F32), ((heads, 8, size), F32), ((8, size), F32), (square, BF), ((size, size), F32),
         wide, wide_b, ((full, kept_width), BF)],
        5, range(5),
        [rows, small, small, pltpu.VMEM((heads, size), F32), pltpu.SemaphoreType.DMA((4 + KEPT,))],
    )(inputs, b_proj, c_proj, log_decay, w_out)
    msg, dg = call(
        functools.partial(mid_kernel, heads),
        [((workers * ROWS, size), BF), wide],
        9, (2, 3, 4),
        [weights, pltpu.VMEM((size, out_width), BF), small, rows,
         pltpu.SemaphoreType.DMA((2 + CHUNKS - KEPT,))],
    )(near, far, w_out, c_proj, gate_in, kept, cum, st, dec)
    msg = lax.all_to_all(msg.reshape(workers, ROWS // 2, 2, size), "ctx", 0, 0, tiled=True)
    msg = msg.reshape(workers * ROWS, size)
    (back,) = call(
        scan_kernel, [((workers, 16, size), BF)], 1, (),
        [pltpu.VMEM((workers, 8, size), F32), pltpu.VMEM((workers, 8, size), F32)],
    )(msg)
    back = lax.all_to_all(back, "ctx", 0, 0, tiled=True)
    half = ((size // 2, out_width + 2 * n), BF)
    mine, theirs = call(
        functools.partial(fin_kernel, heads, piece),
        [half, half],
        11, range(1, 6),
        [lanes, lanes, rows, pltpu.VMEM((size, 2 * n), F32), rows, small, small, rows, weights,
         pltpu.SemaphoreType.DMA((4 + CHUNKS - KEPT,))],
    )(back, inputs, b_proj, c_proj, w_out, gate_in, kept, dg, cum, yi, wx)
    grad_inputs, grad_gate, grad_decay = call(
        functools.partial(rest_kernel, heads),
        [wide_b, wide_b, ((heads, size), F32)],
        11, range(1, 5),
        [lanes, lanes, rows, small, small, rows, pltpu.SemaphoreType.DMA((4,))],
    )(back, inputs, b_proj, c_proj, gate_in, dg, cum, mixt, scores, yi, dec)
    other, grad_inputs = lax.optimization_barrier((lax.ppermute(theirs, "tp", swap), grad_inputs))
    part = (mine.astype(F32) + other.astype(F32)).astype(BF)
    part = lax.all_to_all(
        part.reshape(chips, piece, out_width + 2 * n),
        "tp", 0, 0, tiled=True, axis_index_groups=across,
    )
    layer_out, grad_b, grad_c = call(
        end_kernel, [((piece, out_width), BF), ((piece, n), F32), ((piece, n), F32)], 1
    )(part)
    return (layer_out, grad_inputs, grad_gate, grad_b, grad_c, grad_decay)


def solution(mesh):
    in_specs = (
        P("ctx", "tp"),
        P("ctx", "tp"),
        P("ctx", None),
        P("ctx", None),
        P("tp", "ctx"),
        P("tp", None),
        P(("ctx", "tp"), None),
    )
    out_specs = (
        P(("ctx", "tp"), None),
        P("ctx", "tp"),
        P("ctx", "tp"),
        P(("ctx", "tp"), None),
        P(("ctx", "tp"), None),
        P("tp", "ctx"),
    )
    return jax.shard_map(local, mesh=mesh, in_specs=in_specs, out_specs=out_specs, check_vma=False)
```

```python
import functools

import jax
import jax.numpy as jnp
from jax import lax
from jax.experimental import pallas as pl
from jax.experimental.pallas import tpu as pltpu
from jax.sharding import PartitionSpec as P

BF = jnp.bfloat16
F32 = jnp.float32
NT = (((1,), (1,)), ((), ()))
VMEM_LIMIT = 48 * 1024 * 1024
ROWS = 18
CHUNKS = 8
KEPT = 6


def mm(a, b):
    return jnp.dot(a, b, preferred_element_type=F32)


def mm_nt(a, b):
    return lax.dot_general(a, b, NT, preferred_element_type=F32)


def flip(a):
    return jnp.transpose(a.astype(F32)).astype(BF)


def split(a):
    hi = a.astype(BF)
    rest = a - hi.astype(F32)
    mid = rest.astype(BF)
    return hi, mid, (rest - mid.astype(F32)).astype(BF)


def sum_by(a, ones):
    hi, mid, lo = split(a)
    return mm(hi, ones) + (mm(mid, ones) + mm(lo, ones))


def grid_of(size):
    return (
        lax.broadcasted_iota(jnp.int32, (size, size), 0),
        lax.broadcasted_iota(jnp.int32, (size, size), 1),
    )


def fetch(pairs, sems):
    copies = [pltpu.make_async_copy(src, dst, sems.at[i]) for i, (src, dst) in enumerate(pairs)]
    for copy in copies:
        copy.start()
    return copies


def strips(src, dst, first, last):
    step = src.shape[1] // CHUNKS
    return [
        (src.at[:, pl.ds(i * step, step)], dst.at[:, pl.ds((i - first) * step, step)])
        for i in range(first, last)
    ]


def downward(cum_ref, h):
    size = cum_ref.shape[1]
    return jnp.transpose(jnp.broadcast_to(cum_ref[h:h + 1, :], (size, size)))


def gates(gate_ref):
    v = gate_ref[...].astype(F32)
    g = 1.0 / (1.0 + jnp.exp(-v))
    return v * g, g


def pre_kernel(heads, x_hbm, b_hbm, c_hbm, ld_hbm, w_hbm,
               st_ref, dec_ref, cum_ref, mixt_ref, scores_ref, yi_ref, wx_ref, kept_ref,
               x_ref, b_ref, c_ref, ld_ref, sems):
    copies = fetch(
        [(ld_hbm, ld_ref), (b_hbm, b_ref), (c_hbm, c_ref), (x_hbm, x_ref)]
        + strips(w_hbm, kept_ref, 0, KEPT), sems
    )
    size = x_ref.shape[0]
    width = x_ref.shape[1] // heads
    row, col = grid_of(size)
    copies[0].wait()
    ld = jnp.concatenate([ld_ref[...], jnp.zeros((8 - heads, size), F32)], axis=0)
    cum = sum_by(ld, (row <= col).astype(BF))
    cum_ref[...] = cum
    copies[1].wait()
    copies[2].wait()
    scores = mm_nt(c_ref[...], b_ref[...])
    scores_ref[...] = scores
    b_t = flip(b_ref[...])
    copies[3].wait()
    for h in range(heads):
        at = slice(h * width, (h + 1) * width)
        across = jnp.broadcast_to(cum[h:h + 1, :], (size, size))
        down = jnp.transpose(across)
        mask = jnp.where(row >= col, jnp.exp(jnp.minimum(down - across, 0.0)), 0.0)
        mixing = scores * mask
        mixt_ref[h] = jnp.transpose(mixing).astype(BF)
        x = x_ref[:, at]
        yi_ref[:, at] = mm(mixing.astype(BF), x)
        last = cum[h:h + 1, size - 1:size]
        tail = jnp.exp(last - down)
        wx = (x.astype(F32) * tail).astype(BF)
        wx_ref[:, at] = wx
        st_ref[:, at] = mm(b_t, wx)
        dec_ref[h] = jnp.broadcast_to(jnp.exp(last), (8, size))
    for copy in copies[4:]:
        copy.wait()


def mid_kernel(heads, near_ref, far_ref, w_hbm, c_hbm, gate_hbm, kept_ref, cum_ref, st_ref, dec_ref,
               msg_ref, dg_ref, w_ref, cot_ref, c_ref, gate_ref, sems):
    chips, piece = near_ref.shape[:2]
    size, full = st_ref.shape
    width = full // heads
    chunk = w_hbm.shape[1] // CHUNKS
    copies = fetch(
        [(c_hbm, c_ref), (gate_hbm, gate_ref)] + strips(w_hbm, w_ref, KEPT, CHUNKS), sems
    )
    core = lax.axis_index("tp") % 2
    for s in range(chips):
        at = pl.multiple_of(piece * (2 * s + core), piece)
        cot_ref[pl.ds(at, piece), :] = near_ref[s]
        at = pl.multiple_of(piece * (2 * s + 1 - core), piece)
        cot_ref[pl.ds(at, piece), :] = far_ref[s]
    copies[0].wait()
    copies[1].wait()
    c_t = flip(c_ref[...])
    silu, g = gates(gate_ref)
    total = None
    for i in range(KEPT):
        own = slice(i * chunk, (i + 1) * chunk)
        term = mm_nt(cot_ref[:, own], kept_ref[:, own])
        total = term if total is None else total + term
    for i in range(KEPT, CHUNKS):
        copies[2 + i - KEPT].wait()
        own = slice((i - KEPT) * chunk, (i - KEPT + 1) * chunk)
        total = total + mm_nt(cot_ref[:, i * chunk:(i + 1) * chunk], w_ref[:, own])
    dg_ref[...] = total
    sub = lax.broadcasted_iota(jnp.int32, (2, size), 0)
    for h in range(heads):
        at = slice(h * width, (h + 1) * width)
        gw = (total[:, at] * silu[:, at] * jnp.exp(downward(cum_ref, h))).astype(BF)
        inj = mm(c_t, gw)
        decay = dec_ref[h][0:2, :]
        hi = decay.astype(BF).astype(F32)
        pair = jnp.where(sub == 0, hi, decay - hi).astype(BF)
        for a in range(size // 8):
            j = ROWS * (a * heads + h)
            both = jnp.concatenate([st_ref[8 * a:8 * a + 8, at], inj[8 * a:8 * a + 8, :]], axis=0)
            msg_ref[j:j + 16, :] = both.astype(BF)
            msg_ref[j + 16:j + 18, :] = pair


def scan_kernel(msg_ref, out_ref, dec_ref, state_ref):
    count = out_ref.shape[0]
    lanes = out_ref.shape[2]
    state = jnp.zeros((8, lanes), F32)
    for k in range(count):
        at = ROWS * k
        pair = msg_ref[at + 16:at + 18, :].astype(F32)
        decay = jnp.broadcast_to(jnp.sum(pair, axis=0, keepdims=True), (8, lanes))
        dec_ref[k] = decay
        state_ref[k] = state
        state = decay * state + msg_ref[at:at + 8, :].astype(F32)
    adjoint = jnp.zeros((8, lanes), F32)
    for k in reversed(range(count)):
        at = ROWS * k
        out_ref[k] = jnp.concatenate([state_ref[k], adjoint], axis=0).astype(BF)
        adjoint = dec_ref[k] * adjoint + msg_ref[at + 8:at + 16, :].astype(F32)


def unpack(heads, back_ref, state_ref, adj_ref):
    width = state_ref.shape[1] // heads
    for a in range(state_ref.shape[0] // 8):
        for h in range(heads):
            both = back_ref[a * heads + h].astype(F32)
            state_ref[8 * a:8 * a + 8, h * width:(h + 1) * width] = both[0:8]
            adj_ref[8 * a:8 * a + 8, h * width:(h + 1) * width] = both[8:16]


def mask_of(cum_ref, down, h, row, col):
    gap = down - jnp.broadcast_to(cum_ref[h:h + 1, :], down.shape)
    return jnp.where(row >= col, jnp.exp(jnp.minimum(gap, 0.0)), 0.0)


def fin_kernel(heads, piece, back_ref, x_hbm, b_hbm, c_hbm, w_hbm, gate_hbm, kept_ref, dg_ref, cum_ref,
               yi_ref, wx_ref, mine_ref, theirs_ref, state_ref, adj_ref,
               gated_ref, terms_ref, x_ref, b_ref, c_ref, gate_ref, w_ref, sems):
    size, full = x_ref.shape
    width = full // heads
    copies = fetch(
        [(b_hbm, b_ref), (c_hbm, c_ref), (gate_hbm, gate_ref), (x_hbm, x_ref)]
        + strips(w_hbm, w_ref, KEPT, CHUNKS), sems
    )
    unpack(heads, back_ref, state_ref, adj_ref)
    state_b = state_ref[...].astype(BF)
    adj_b = adj_ref[...].astype(BF)
    for copy in copies[0:4]:
        copy.wait()
    x = x_ref[...]
    b = b_ref[...]
    c = c_ref[...]
    silu, g = gates(gate_ref)
    downs = [downward(cum_ref, h) for h in range(heads)]
    ec = jnp.concatenate([jnp.exp(down) for down in downs], axis=1)
    gated = ((yi_ref[...] + mm(c, state_b) * ec) * silu).astype(BF)
    core = lax.axis_index("tp") % 2
    places = []
    for i in range(size // piece // 2):
        for k in range(2):
            away = jnp.where(core == k, 0, 1)
            places.append((slice(piece * (2 * i + k), piece * (2 * i + k + 1)),
                           pl.ds(pl.multiple_of(size // 2 * (1 - away) + piece * i, piece), piece)))
    for src, dst in places:
        gated_ref[dst, :] = gated[src, :]
    gy = dg_ref[...] * silu
    gy_b = gy.astype(BF)
    gw = (gy * ec).astype(BF)
    row, col = grid_of(size)
    dmix_sum = jnp.zeros((size, size), F32)
    for h in range(heads):
        at = slice(h * width, (h + 1) * width)
        mask = mask_of(cum_ref, downs[h], h, row, col)
        dmix_sum = dmix_sum + mm_nt(gy_b[:, at], x[:, at]) * mask
    n = b.shape[1]
    grad_b = mm(jnp.transpose(dmix_sum).astype(BF), c) + mm_nt(wx_ref[...], adj_b)
    grad_c = mm(dmix_sum.astype(BF), b) + mm_nt(gw, state_b)
    half = size // 2
    out_width = w_hbm.shape[1]
    for src, dst in places:
        terms_ref[dst, 0:n] = grad_b[src, :]
        terms_ref[dst, n:2 * n] = grad_c[src, :]
    theirs_ref[:, out_width:out_width + 2 * n] = terms_ref[0:half, :].astype(BF)
    mine_ref[:, out_width:out_width + 2 * n] = terms_ref[half:size, :].astype(BF)
    step = out_width // CHUNKS
    gated = gated_ref[...]
    for i in range(CHUNKS):
        if i == KEPT or i == (KEPT + CHUNKS) // 2:
            for k in range(i, (KEPT + CHUNKS) // 2 if i == KEPT else CHUNKS):
                copies[4 + k - KEPT].wait()
        own = kept_ref if i < KEPT else w_ref
        at = (i if i < KEPT else i - KEPT) * step
        part = mm(gated, own[:, at:at + step]).astype(BF)
        theirs_ref[:, i * step:(i + 1) * step] = part[0:half, :]
        mine_ref[:, i * step:(i + 1) * step] = part[half:size, :]


def rest_kernel(heads, back_ref, x_hbm, b_hbm, c_hbm, gate_hbm, dg_ref, cum_ref,
                mixt_ref, scores_ref, yi_ref, dec_ref,
                gi_ref, gg_ref, gd_ref, state_ref, adj_ref, x_ref, b_ref, c_ref, gate_ref, sems):
    size, full = x_ref.shape
    width = full // heads
    copies = fetch([(b_hbm, b_ref), (c_hbm, c_ref), (gate_hbm, gate_ref), (x_hbm, x_ref)], sems)
    unpack(heads, back_ref, state_ref, adj_ref)
    state = state_ref[...]
    adj = adj_ref[...]
    for copy in copies:
        copy.wait()
    x = x_ref[...]
    silu, g = gates(gate_ref)
    dg = dg_ref[...]
    downs = [downward(cum_ref, h) for h in range(heads)]
    ec = jnp.concatenate([jnp.exp(down) for down in downs], axis=1)
    tail = jnp.concatenate(
        [jnp.exp(cum_ref[h:h + 1, size - 1:size] - downs[h]) for h in range(heads)], axis=1
    )
    y_inter = mm(c_ref[...], state.astype(BF)) * ec
    gg_ref[...] = (dg * (yi_ref[...] + y_inter) * (g + silu * (1.0 - g))).astype(BF)
    gy = dg * silu
    gy_b = gy.astype(BF)
    sdx = mm(b_ref[...], adj.astype(BF)) * tail
    through = x.astype(F32) * sdx
    entering = gy * y_inter
    scores = scores_ref[...]
    row, col = grid_of(size)
    sub = lax.broadcasted_iota(jnp.int32, (8, size), 0)
    columns = jnp.zeros((size, size), F32)
    lines = jnp.zeros((8, size), F32)
    closing = jnp.zeros((8, size), F32)
    product = adj * state
    for h in range(heads):
        at = slice(h * width, (h + 1) * width)
        mask = mask_of(cum_ref, downs[h], h, row, col)
        cross = mm_nt(gy_b[:, at], x[:, at]) * mask * scores
        gi_ref[:, at] = (mm(mixt_ref[h], gy_b[:, at]) + sdx[:, at]).astype(BF)
        down = jnp.sum(cross + entering[:, at] - through[:, at], axis=1, keepdims=True)
        columns = jnp.where(col == h, down, columns)
        lines = jnp.where(sub == h, jnp.sum(cross, axis=0, keepdims=True), lines)
        end = jnp.sum(jnp.sum(through[:, at], axis=0, keepdims=True), axis=1, keepdims=True)
        dots = jnp.sum(jnp.sum(product[:, at], axis=0, keepdims=True), axis=1, keepdims=True)
        closing = jnp.where(sub == h, end + dec_ref[h] * dots, closing)
    flow = jnp.transpose(columns)[0:8, :] - lines
    total = sum_by(flow, (row >= col).astype(BF)) + closing
    gd_ref[...] = total[0:heads, :]


def end_kernel(part_ref, out_ref, gb_ref, gc_ref):
    out_width = out_ref.shape[1]
    n = gb_ref.shape[1]
    total = part_ref[0].astype(F32)
    for i in range(1, part_ref.shape[0]):
        total = total + part_ref[i].astype(F32)
    out_ref[...] = total[:, 0:out_width].astype(BF)
    gb_ref[...] = total[:, out_width:out_width + n]
    gc_ref[...] = total[:, out_width + n:out_width + 2 * n]


def call(kernel, outs, count, remote=(), scratch=()):
    return pl.pallas_call(
        kernel,
        out_shape=tuple(jax.ShapeDtypeStruct(s, d) for s, d in outs),
        in_specs=[
            pl.BlockSpec(memory_space=pltpu.HBM if i in remote else pltpu.VMEM)
            for i in range(count)
        ],
        scratch_shapes=list(scratch),
        compiler_params=pltpu.CompilerParams(vmem_limit_bytes=VMEM_LIMIT),
    )


def local(inputs, gate_in, b_proj, c_proj, log_decay, w_out, cotangent):
    size, full = inputs.shape
    heads = log_decay.shape[0]
    n = b_proj.shape[1]
    tp = lax.axis_size("tp")
    chips = tp // 2
    workers = lax.axis_size("ctx")
    piece, out_width = cotangent.shape
    wide = ((size, full), F32)
    wide_b = ((size, full), BF)
    square = (heads, size, size)
    small = pltpu.VMEM((size, n), BF)
    kept_width = out_width // CHUNKS * KEPT
    weights = pltpu.VMEM((full, out_width - kept_width), BF)
    lanes = pltpu.VMEM((size, full), F32)
    rows = pltpu.VMEM((size, full), BF)
    across = [[2 * i + k for i in range(chips)] for k in range(2)]
    swap = [(i, i ^ 1) for i in range(tp)]

    near = lax.all_to_all(
        jnp.broadcast_to(cotangent[None], (chips, piece, out_width)),
        "tp", 0, 0, tiled=True, axis_index_groups=across,
    )
    far = lax.ppermute(near, "tp", swap)
    st, dec, cum, mixt, scores, yi, wx, kept = call(
        functools.partial(pre_kernel, heads),
        [((n, full), F32), ((heads, 8, size), F32), ((8, size), F32), (square, BF), ((size, size), F32),
         wide, wide_b, ((full, kept_width), BF)],
        5, range(5),
        [rows, small, small, pltpu.VMEM((heads, size), F32), pltpu.SemaphoreType.DMA((4 + KEPT,))],
    )(inputs, b_proj, c_proj, log_decay, w_out)
    msg, dg = call(
        functools.partial(mid_kernel, heads),
        [((workers * ROWS, size), BF), wide],
        9, (2, 3, 4),
        [weights, pltpu.VMEM((size, out_width), BF), small, rows,
         pltpu.SemaphoreType.DMA((2 + CHUNKS - KEPT,))],
    )(near, far, w_out, c_proj, gate_in, kept, cum, st, dec)
    msg = lax.all_to_all(msg.reshape(workers, ROWS // 2, 2, size), "ctx", 0, 0, tiled=True)
    msg = msg.reshape(workers * ROWS, size)
    (back,) = call(
        scan_kernel, [((workers, 16, size), BF)], 1, (),
        [pltpu.VMEM((workers, 8, size), F32), pltpu.VMEM((workers, 8, size), F32)],
    )(msg)
    back = lax.all_to_all(back, "ctx", 0, 0, tiled=True)
    half = ((size // 2, out_width + 2 * n), BF)
    mine, theirs = call(
        functools.partial(fin_kernel, heads, piece),
        [half, half],
        11, range(1, 6),
        [lanes, lanes, rows, pltpu.VMEM((size, 2 * n), F32), rows, small, small, rows, weights,
         pltpu.SemaphoreType.DMA((4 + CHUNKS - KEPT,))],
    )(back, inputs, b_proj, c_proj, w_out, gate_in, kept, dg, cum, yi, wx)
    grad_inputs, grad_gate, grad_decay = call(
        functools.partial(rest_kernel, heads),
        [wide_b, wide_b, ((heads, size), F32)],
        11, range(1, 5),
        [lanes, lanes, rows, small, small, rows, pltpu.SemaphoreType.DMA((4,))],
    )(back, inputs, b_proj, c_proj, gate_in, dg, cum, mixt, scores, yi, dec)
    other, grad_inputs = lax.optimization_barrier((lax.ppermute(theirs, "tp", swap), grad_inputs))
    part = (mine.astype(F32) + other.astype(F32)).astype(BF)
    part = lax.all_to_all(
        part.reshape(chips, piece, out_width + 2 * n),
        "tp", 0, 0, tiled=True, axis_index_groups=across,
    )
    layer_out, grad_b, grad_c = call(
        end_kernel, [((piece, out_width), BF), ((piece, n), F32), ((piece, n), F32)], 1
    )(part)
    return (layer_out, grad_inputs, grad_gate, grad_b, grad_c, grad_decay)


def solution(mesh):
    in_specs = (
        P("ctx", "tp"),
        P("ctx", "tp"),
        P("ctx", None),
        P("ctx", None),
        P("tp", "ctx"),
        P("tp", None),
        P(("ctx", "tp"), None),
    )
    out_specs = (
        P(("ctx", "tp"), None),
        P("ctx", "tp"),
        P("ctx", "tp"),
        P(("ctx", "tp"), None),
        P(("ctx", "tp"), None),
        P("tp", "ctx"),
    )
    return jax.shard_map(local, mesh=mesh, in_specs=in_specs, out_specs=out_specs, check_vma=False)
```

```python
import functools

import jax
import jax.numpy as jnp
from jax import lax
from jax.experimental import pallas as pl
from jax.experimental.pallas import tpu as pltpu
from jax.sharding import PartitionSpec as P

BF = jnp.bfloat16
F32 = jnp.float32
NT = (((1,), (1,)), ((), ()))
VMEM_LIMIT = 48 * 1024 * 1024
ROWS = 18
CHUNKS = 8
KEPT = 5


def mm(a, b):
    return jnp.dot(a, b, preferred_element_type=F32)


def mm_nt(a, b):
    return lax.dot_general(a, b, NT, preferred_element_type=F32)


def flip(a):
    return jnp.transpose(a.astype(F32)).astype(BF)


def split(a):
    hi = a.astype(BF)
    rest = a - hi.astype(F32)
    mid = rest.astype(BF)
    return hi, mid, (rest - mid.astype(F32)).astype(BF)


def sum_by(a, ones):
    hi, mid, lo = split(a)
    return mm(hi, ones) + (mm(mid, ones) + mm(lo, ones))


def grid_of(size):
    return (
        lax.broadcasted_iota(jnp.int32, (size, size), 0),
        lax.broadcasted_iota(jnp.int32, (size, size), 1),
    )


def fetch(pairs, sems):
    copies = [pltpu.make_async_copy(src, dst, sems.at[i]) for i, (src, dst) in enumerate(pairs)]
    for copy in copies:
        copy.start()
    return copies


def strips(src, dst, first, last):
    step = src.shape[1] // CHUNKS
    return [
        (src.at[:, pl.ds(i * step, step)], dst.at[:, pl.ds((i - first) * step, step)])
        for i in range(first, last)
    ]


def downward(cum_ref, h):
    size = cum_ref.shape[1]
    return jnp.transpose(jnp.broadcast_to(cum_ref[h:h + 1, :], (size, size)))


def gates(gate_ref):
    v = gate_ref[...].astype(F32)
    g = 1.0 / (1.0 + jnp.exp(-v))
    return v * g, g


def pre_kernel(heads, x_hbm, b_hbm, c_hbm, ld_hbm, w_hbm,
               st_ref, dec_ref, cum_ref, mixt_ref, scores_ref, yi_ref, wx_ref, kept_ref,
               x_ref, b_ref, c_ref, ld_ref, sems):
    copies = fetch(
        [(ld_hbm, ld_ref), (b_hbm, b_ref), (c_hbm, c_ref), (x_hbm, x_ref)]
        + strips(w_hbm, kept_ref, 0, KEPT), sems
    )
    size = x_ref.shape[0]
    width = x_ref.shape[1] // heads
    row, col = grid_of(size)
    copies[0].wait()
    ld = jnp.concatenate([ld_ref[...], jnp.zeros((8 - heads, size), F32)], axis=0)
    cum = sum_by(ld, (row <= col).astype(BF))
    cum_ref[...] = cum
    copies[1].wait()
    copies[2].wait()
    scores = mm_nt(c_ref[...], b_ref[...])
    scores_ref[...] = scores
    b_t = flip(b_ref[...])
    copies[3].wait()
    for h in range(heads):
        at = slice(h * width, (h + 1) * width)
        across = jnp.broadcast_to(cum[h:h + 1, :], (size, size))
        down = jnp.transpose(across)
        mask = jnp.where(row >= col, jnp.exp(jnp.minimum(down - across, 0.0)), 0.0)
        mixing = scores * mask
        mixt_ref[h] = jnp.transpose(mixing).astype(BF)
        x = x_ref[:, at]
        yi_ref[:, at] = mm(mixing.astype(BF), x)
        last = cum[h:h + 1, size - 1:size]
        tail = jnp.exp(last - down)
        wx = (x.astype(F32) * tail).astype(BF)
        wx_ref[:, at] = wx
        st_ref[:, at] = mm(b_t, wx)
        dec_ref[h] = jnp.broadcast_to(jnp.exp(last), (8, size))
    for copy in copies[4:]:
        copy.wait()


def mid_kernel(heads, near_ref, far_ref, w_hbm, c_hbm, gate_hbm, kept_ref, cum_ref, st_ref, dec_ref,
               msg_ref, dg_ref, w_ref, cot_ref, c_ref, gate_ref, sems):
    chips, piece = near_ref.shape[:2]
    size, full = st_ref.shape
    width = full // heads
    chunk = w_hbm.shape[1] // CHUNKS
    copies = fetch(
        [(c_hbm, c_ref), (gate_hbm, gate_ref)] + strips(w_hbm, w_ref, KEPT, CHUNKS), sems
    )
    core = lax.axis_index("tp") % 2
    for s in range(chips):
        at = pl.multiple_of(piece * (2 * s + core), piece)
        cot_ref[pl.ds(at, piece), :] = near_ref[s]
        at = pl.multiple_of(piece * (2 * s + 1 - core), piece)
        cot_ref[pl.ds(at, piece), :] = far_ref[s]
    copies[0].wait()
    copies[1].wait()
    c_t = flip(c_ref[...])
    silu, g = gates(gate_ref)
    total = None
    for i in range(KEPT):
        own = slice(i * chunk, (i + 1) * chunk)
        term = mm_nt(cot_ref[:, own], kept_ref[:, own])
        total = term if total is None else total + term
    for i in range(KEPT, CHUNKS):
        copies[2 + i - KEPT].wait()
        own = slice((i - KEPT) * chunk, (i - KEPT + 1) * chunk)
        total = total + mm_nt(cot_ref[:, i * chunk:(i + 1) * chunk], w_ref[:, own])
    dg_ref[...] = total
    sub = lax.broadcasted_iota(jnp.int32, (2, size), 0)
    for h in range(heads):
        at = slice(h * width, (h + 1) * width)
        gw = (total[:, at] * silu[:, at] * jnp.exp(downward(cum_ref, h))).astype(BF)
        inj = mm(c_t, gw)
        decay = dec_ref[h][0:2, :]
        hi = decay.astype(BF).astype(F32)
        pair = jnp.where(sub == 0, hi, decay - hi).astype(BF)
        for a in range(size // 8):
            j = ROWS * (a * heads + h)
            both = jnp.concatenate([st_ref[8 * a:8 * a + 8, at], inj[8 * a:8 * a + 8, :]], axis=0)
            msg_ref[j:j + 16, :] = both.astype(BF)
            msg_ref[j + 16:j + 18, :] = pair


def scan_kernel(msg_ref, out_ref, dec_ref, state_ref):
    count = out_ref.shape[0]
    lanes = out_ref.shape[2]
    state = jnp.zeros((8, lanes), F32)
    for k in range(count):
        at = ROWS * k
        pair = msg_ref[at + 16:at + 18, :].astype(F32)
        decay = jnp.broadcast_to(jnp.sum(pair, axis=0, keepdims=True), (8, lanes))
        dec_ref[k] = decay
        state_ref[k] = state
        state = decay * state + msg_ref[at:at + 8, :].astype(F32)
    adjoint = jnp.zeros((8, lanes), F32)
    for k in reversed(range(count)):
        at = ROWS * k
        out_ref[k] = jnp.concatenate([state_ref[k], adjoint], axis=0).astype(BF)
        adjoint = dec_ref[k] * adjoint + msg_ref[at + 8:at + 16, :].astype(F32)


def unpack(heads, back_ref, state_ref, adj_ref):
    width = state_ref.shape[1] // heads
    for a in range(state_ref.shape[0] // 8):
        for h in range(heads):
            both = back_ref[a * heads + h].astype(F32)
            state_ref[8 * a:8 * a + 8, h * width:(h + 1) * width] = both[0:8]
            adj_ref[8 * a:8 * a + 8, h * width:(h + 1) * width] = both[8:16]


def mask_of(cum_ref, down, h, row, col):
    gap = down - jnp.broadcast_to(cum_ref[h:h + 1, :], down.shape)
    return jnp.where(row >= col, jnp.exp(jnp.minimum(gap, 0.0)), 0.0)


def fin_kernel(heads, piece, back_ref, x_hbm, b_hbm, c_hbm, w_hbm, gate_hbm, kept_ref, dg_ref, cum_ref,
               yi_ref, wx_ref, mine_ref, theirs_ref, state_ref, adj_ref,
               gated_ref, terms_ref, x_ref, b_ref, c_ref, gate_ref, w_ref, sems):
    size, full = x_ref.shape
    width = full // heads
    copies = fetch(
        [(b_hbm, b_ref), (c_hbm, c_ref), (gate_hbm, gate_ref), (x_hbm, x_ref)]
        + strips(w_hbm, w_ref, KEPT, CHUNKS), sems
    )
    unpack(heads, back_ref, state_ref, adj_ref)
    state_b = state_ref[...].astype(BF)
    adj_b = adj_ref[...].astype(BF)
    for copy in copies[0:4]:
        copy.wait()
    x = x_ref[...]
    b = b_ref[...]
    c = c_ref[...]
    silu, g = gates(gate_ref)
    downs = [downward(cum_ref, h) for h in range(heads)]
    ec = jnp.concatenate([jnp.exp(down) for down in downs], axis=1)
    gated = ((yi_ref[...] + mm(c, state_b) * ec) * silu).astype(BF)
    core = lax.axis_index("tp") % 2
    places = []
    for i in range(size // piece // 2):
        for k in range(2):
            away = jnp.where(core == k, 0, 1)
            places.append((slice(piece * (2 * i + k), piece * (2 * i + k + 1)),
                           pl.ds(pl.multiple_of(size // 2 * (1 - away) + piece * i, piece), piece)))
    for src, dst in places:
        gated_ref[dst, :] = gated[src, :]
    gy = dg_ref[...] * silu
    gy_b = gy.astype(BF)
    gw = (gy * ec).astype(BF)
    row, col = grid_of(size)
    dmix_sum = jnp.zeros((size, size), F32)
    for h in range(heads):
        at = slice(h * width, (h + 1) * width)
        mask = mask_of(cum_ref, downs[h], h, row, col)
        dmix_sum = dmix_sum + mm_nt(gy_b[:, at], x[:, at]) * mask
    n = b.shape[1]
    grad_b = mm(jnp.transpose(dmix_sum).astype(BF), c) + mm_nt(wx_ref[...], adj_b)
    grad_c = mm(dmix_sum.astype(BF), b) + mm_nt(gw, state_b)
    half = size // 2
    out_width = w_hbm.shape[1]
    for src, dst in places:
        terms_ref[dst, 0:n] = grad_b[src, :]
        terms_ref[dst, n:2 * n] = grad_c[src, :]
    theirs_ref[:, out_width:out_width + 2 * n] = terms_ref[0:half, :].astype(BF)
    mine_ref[:, out_width:out_width + 2 * n] = terms_ref[half:size, :].astype(BF)
    step = out_width // CHUNKS
    gated = gated_ref[...]
    for i in range(CHUNKS):
        if i == KEPT or i == (KEPT + CHUNKS) // 2:
            for k in range(i, (KEPT + CHUNKS) // 2 if i == KEPT else CHUNKS):
                copies[4 + k - KEPT].wait()
        own = kept_ref if i < KEPT else w_ref
        at = (i if i < KEPT else i - KEPT) * step
        part = mm(gated, own[:, at:at + step]).astype(BF)
        theirs_ref[:, i * step:(i + 1) * step] = part[0:half, :]
        mine_ref[:, i * step:(i + 1) * step] = part[half:size, :]


def rest_kernel(heads, back_ref, x_hbm, b_hbm, c_hbm, gate_hbm, dg_ref, cum_ref,
                mixt_ref, scores_ref, yi_ref, dec_ref,
                gi_ref, gg_ref, gd_ref, state_ref, adj_ref, x_ref, b_ref, c_ref, gate_ref, sems):
    size, full = x_ref.shape
    width = full // heads
    copies = fetch([(b_hbm, b_ref), (c_hbm, c_ref), (gate_hbm, gate_ref), (x_hbm, x_ref)], sems)
    unpack(heads, back_ref, state_ref, adj_ref)
    state = state_ref[...]
    adj = adj_ref[...]
    for copy in copies:
        copy.wait()
    x = x_ref[...]
    silu, g = gates(gate_ref)
    dg = dg_ref[...]
    downs = [downward(cum_ref, h) for h in range(heads)]
    ec = jnp.concatenate([jnp.exp(down) for down in downs], axis=1)
    tail = jnp.concatenate(
        [jnp.exp(cum_ref[h:h + 1, size - 1:size] - downs[h]) for h in range(heads)], axis=1
    )
    y_inter = mm(c_ref[...], state.astype(BF)) * ec
    gg_ref[...] = (dg * (yi_ref[...] + y_inter) * (g + silu * (1.0 - g))).astype(BF)
    gy = dg * silu
    gy_b = gy.astype(BF)
    sdx = mm(b_ref[...], adj.astype(BF)) * tail
    through = x.astype(F32) * sdx
    entering = gy * y_inter
    scores = scores_ref[...]
    row, col = grid_of(size)
    sub = lax.broadcasted_iota(jnp.int32, (8, size), 0)
    columns = jnp.zeros((size, size), F32)
    lines = jnp.zeros((8, size), F32)
    closing = jnp.zeros((8, size), F32)
    product = adj * state
    for h in range(heads):
        at = slice(h * width, (h + 1) * width)
        mask = mask_of(cum_ref, downs[h], h, row, col)
        cross = mm_nt(gy_b[:, at], x[:, at]) * mask * scores
        gi_ref[:, at] = (mm(mixt_ref[h], gy_b[:, at]) + sdx[:, at]).astype(BF)
        down = jnp.sum(cross + entering[:, at] - through[:, at], axis=1, keepdims=True)
        columns = jnp.where(col == h, down, columns)
        lines = jnp.where(sub == h, jnp.sum(cross, axis=0, keepdims=True), lines)
        end = jnp.sum(jnp.sum(through[:, at], axis=0, keepdims=True), axis=1, keepdims=True)
        dots = jnp.sum(jnp.sum(product[:, at], axis=0, keepdims=True), axis=1, keepdims=True)
        closing = jnp.where(sub == h, end + dec_ref[h] * dots, closing)
    flow = jnp.transpose(columns)[0:8, :] - lines
    total = sum_by(flow, (row >= col).astype(BF)) + closing
    gd_ref[...] = total[0:heads, :]


def end_kernel(part_ref, out_ref, gb_ref, gc_ref):
    out_width = out_ref.shape[1]
    n = gb_ref.shape[1]
    total = part_ref[0].astype(F32)
    for i in range(1, part_ref.shape[0]):
        total = total + part_ref[i].astype(F32)
    out_ref[...] = total[:, 0:out_width].astype(BF)
    gb_ref[...] = total[:, out_width:out_width + n]
    gc_ref[...] = total[:, out_width + n:out_width + 2 * n]


def call(kernel, outs, count, remote=(), scratch=()):
    return pl.pallas_call(
        kernel,
        out_shape=tuple(jax.ShapeDtypeStruct(s, d) for s, d in outs),
        in_specs=[
            pl.BlockSpec(memory_space=pltpu.HBM if i in remote else pltpu.VMEM)
            for i in range(count)
        ],
        scratch_shapes=list(scratch),
        compiler_params=pltpu.CompilerParams(vmem_limit_bytes=VMEM_LIMIT),
    )


def local(inputs, gate_in, b_proj, c_proj, log_decay, w_out, cotangent):
    size, full = inputs.shape
    heads = log_decay.shape[0]
    n = b_proj.shape[1]
    tp = lax.axis_size("tp")
    chips = tp // 2
    workers = lax.axis_size("ctx")
    piece, out_width = cotangent.shape
    wide = ((size, full), F32)
    wide_b = ((size, full), BF)
    square = (heads, size, size)
    small = pltpu.VMEM((size, n), BF)
    kept_width = out_width // CHUNKS * KEPT
    weights = pltpu.VMEM((full, out_width - kept_width), BF)
    lanes = pltpu.VMEM((size, full), F32)
    rows = pltpu.VMEM((size, full), BF)
    across = [[2 * i + k for i in range(chips)] for k in range(2)]
    swap = [(i, i ^ 1) for i in range(tp)]

    near = lax.all_to_all(
        jnp.broadcast_to(cotangent[None], (chips, piece, out_width)),
        "tp", 0, 0, tiled=True, axis_index_groups=across,
    )
    far = lax.ppermute(near, "tp", swap)
    st, dec, cum, mixt, scores, yi, wx, kept = call(
        functools.partial(pre_kernel, heads),
        [((n, full), F32), ((heads, 8, size), F32), ((8, size), F32), (square, BF), ((size, size), F32),
         wide, wide_b, ((full, kept_width), BF)],
        5, range(5),
        [rows, small, small, pltpu.VMEM((heads, size), F32), pltpu.SemaphoreType.DMA((4 + KEPT,))],
    )(inputs, b_proj, c_proj, log_decay, w_out)
    msg, dg = call(
        functools.partial(mid_kernel, heads),
        [((workers * ROWS, size), BF), wide],
        9, (2, 3, 4),
        [weights, pltpu.VMEM((size, out_width), BF), small, rows,
         pltpu.SemaphoreType.DMA((2 + CHUNKS - KEPT,))],
    )(near, far, w_out, c_proj, gate_in, kept, cum, st, dec)
    msg = lax.all_to_all(msg.reshape(workers, ROWS // 2, 2, size), "ctx", 0, 0, tiled=True)
    msg = msg.reshape(workers * ROWS, size)
    (back,) = call(
        scan_kernel, [((workers, 16, size), BF)], 1, (),
        [pltpu.VMEM((workers, 8, size), F32), pltpu.VMEM((workers, 8, size), F32)],
    )(msg)
    back = lax.all_to_all(back, "ctx", 0, 0, tiled=True)
    half = ((size // 2, out_width + 2 * n), BF)
    mine, theirs = call(
        functools.partial(fin_kernel, heads, piece),
        [half, half],
        11, range(1, 6),
        [lanes, lanes, rows, pltpu.VMEM((size, 2 * n), F32), rows, small, small, rows, weights,
         pltpu.SemaphoreType.DMA((4 + CHUNKS - KEPT,))],
    )(back, inputs, b_proj, c_proj, w_out, gate_in, kept, dg, cum, yi, wx)
    grad_inputs, grad_gate, grad_decay = call(
        functools.partial(rest_kernel, heads),
        [wide_b, wide_b, ((heads, size), F32)],
        11, range(1, 5),
        [lanes, lanes, rows, small, small, rows, pltpu.SemaphoreType.DMA((4,))],
    )(back, inputs, b_proj, c_proj, gate_in, dg, cum, mixt, scores, yi, dec)
    part = (mine.astype(F32) + lax.ppermute(theirs, "tp", swap).astype(F32)).astype(BF)
    part = lax.all_to_all(
        part.reshape(chips, piece, out_width + 2 * n),
        "tp", 0, 0, tiled=True, axis_index_groups=across,
    )
    layer_out, grad_b, grad_c = call(
        end_kernel, [((piece, out_width), BF), ((piece, n), F32), ((piece, n), F32)], 1
    )(part)
    return (layer_out, grad_inputs, grad_gate, grad_b, grad_c, grad_decay)


def solution(mesh):
    in_specs = (
        P("ctx", "tp"),
        P("ctx", "tp"),
        P("ctx", None),
        P("ctx", None),
        P("tp", "ctx"),
        P("tp", None),
        P(("ctx", "tp"), None),
    )
    out_specs = (
        P(("ctx", "tp"), None),
        P("ctx", "tp"),
        P("ctx", "tp"),
        P(("ctx", "tp"), None),
        P(("ctx", "tp"), None),
        P("tp", "ctx"),
    )
    return jax.shard_map(local, mesh=mesh, in_specs=in_specs, out_specs=out_specs, check_vma=False)
```
